128 devices in a mesh: section: 8 (over y, core), row: 16 (over x, z).
Axes of the slice: x: 4, y: 4, z: 4, core: 2. Of those that a mesh axis runs over, the one named last changes fastest.
Arguments:
- coupling: bfloat16 [2048, 128, 128], P(('section', 'row')), may hold values from -4 to 4
- diag_inverse: float32 [2048, 128, 128], P(('section', 'row')), may hold values from -0.046875 to 0.046875
- pivot_inverse: bfloat16 [512, 128, 128], P(('section', 'row')), may hold values from -0.5 to 0.5
- cross_left: bfloat16 [16384, 128, 128], P(('section', 'row')), may hold values from -0.5 to 0.5
- cross_right: bfloat16 [16384, 128, 128], P(('section', 'row')), may hold values from -4 to 4
- cross_pivot: int32 [16384], P(('section', 'row')), may hold values from 0 to 3
- cross_owner: int32 [16384, 1], P(('section', 'row')), may hold values from 0 to 15; in each aligned block of 128 rows (0 to 127, 128 to 255, ...) at most 16 rows name the same one
- foreign_target_row: int32 [16384], P(('section', 'row')), may hold values from 0 to 15
- cross_count: int32 [128], P(('section', 'row')), may hold values from 1 to 128, 12288 in all
- local_left: bfloat16 [16384, 128, 128], P(('section', 'row')), may hold values from -0.5 to 0.5
- local_right: bfloat16 [16384, 128, 128], P(('section', 'row')), may hold values from -4 to 4
- local_pivot: int32 [16384], P(('section', 'row')), may hold values from 0 to 3
- local_target: int32 [16384], P(('section', 'row')), may hold values from 0 to 15
- adjoint_seed: float32 [2048, 128, 128], P(('section', 'row')), may hold values from -48 to 48
Outputs:
- coupling_new: float32 [2048, 128, 128], P(('section', 'row'))
- adjoint: float32 [2048, 128, 128], P(('section', 'row'))
The draws below stay inside these ranges and needn't reach their ends.
Inputs may be any that keep to these rules, and one draw needn't show every extreme that they name: `cross_owner`: among the 128 cross slots of one device, live or not, at most 16 name the same owner, a bound that some block reaches of them. `cross_count`: some device has all its cross slots live.
All inputs are finite; a program needn't handle non-finite values.
Results may differ from the reference program's by a relative error of at most 0.0089.
Values may be sent and summed in bfloat16 or wider, within the bound.
No kernel may reach another device: no remote copies, remote signals or barrier semaphores. Data moves between devices by JAX's collectives and lax.ppermute only.
A program may use at most 192 MiB of HBM per device.

```python
import math
import jax
import jax.numpy as jnp
import numpy as np
from jax import lax

B = 128
ROWS_DEV = 16
UPD_DEV = 128
LOC_DEV = 128
PIV_DEV = 4
NRHS = 128
NBLK = 2048
SLOTS = 16384
LSLOTS = 16384
PIVOTS = 512
N_SECTION = 8
N_ROW = 16


def with_ends(result, key, low, top_value):
    spot = [jax.random.randint(jax.random.fold_in(key, axis), (), 0, length) for axis, length in enumerate(result.shape)]
    widest = result.shape.index(max(result.shape))
    beside = spot[:widest] + [(spot[widest] + 1) % result.shape[widest]] + spot[widest + 1:]
    return result.at[tuple(spot)].set(low).at[tuple(beside)].set(top_value)


def steps_of(key, dims, split, low, high):
    def one(position, shards_of):
        draws = jax.random.uniform(jax.random.fold_in(jax.random.fold_in(key, 6), position), (shards_of,), jnp.float32, low / len(split), high / len(split))
        return jnp.repeat(jnp.exp(draws), dims[position] // shards_of).reshape((-1,) + (1,) * (len(dims) - position - 1))

    gain = one(*split[0])
    for cut in split[1:]:
        gain = gain * one(*cut)
    return gain


def length_profile(number_of, total, limit, slope):
    portions = [(1 << 20) // math.isqrt(standing ** slope) + 1 for standing in range(2, number_of + 1)]
    spare, given = total - limit - (number_of - 1), [1] * (number_of - 1)
    while spare > 0:
        free = [i for i in range(number_of - 1) if given[i] < limit]
        pool, left = sum([portions[i] for i in free]), spare
        for i in free:
            extra = min(limit - given[i], max(1, left * portions[i] // pool), spare)
            given[i] = given[i] + extra
            spare = spare - extra
    return np.array([limit] + given)


def ragged_sizes(stream_key, count, total, bound, slope):
    if count == 2:
        one = jax.random.randint(stream_key, (), max(1, total - bound), min(bound, total - 1) + 1)
        return jnp.stack([one, total - one])
    lengths = jnp.asarray(length_profile(count, total, bound, slope), jnp.int32)
    pairs = (count - 1) // 2
    donor, receiver = lengths[1:1 + 2 * pairs:2], lengths[2:2 + 2 * pairs:2]
    room = jnp.minimum(donor - 1, bound - receiver)
    moved = jax.random.randint(jax.random.fold_in(stream_key, 1), (pairs,), 0, 1 << 20) % (room + 1)
    lengths = lengths.at[1:1 + 2 * pairs:2].set(donor - moved).at[2:2 + 2 * pairs:2].set(receiver + moved)
    return lengths[jax.random.permutation(jax.random.fold_in(stream_key, 2), count)]


def deal_out(rng, own, number, rows, count, top, reach, slope):
    order = jax.random.permutation(rng, count)
    crowded, ordinary = load_shares(count, rows * top, reach, slope, True), load_shares(count, rows * top, reach, slope, False)
    places = jnp.arange(count)

    def named(tallies, offset_by):
        used = int((tallies > 0).sum())
        fixed = max(1, used // 4)
        moved = fixed + (places - fixed + offset_by * (used - fixed)) % max(1, count - fixed)
        return jnp.zeros((count,), jnp.int32).at[order[jnp.where(places < fixed, places, moved)]].set(jnp.asarray(tallies, jnp.int32))

    tallies = jnp.where(number % 4 == 0, named(crowded, number // 4), named(ordinary, number - number // 4 - 1))
    mixed = jax.random.permutation(jax.random.fold_in(own, 3), count)
    giver, taker = mixed[0:count // 2 * 2:2], mixed[1:count // 2 * 2:2]
    margin = jnp.minimum(tallies[giver] - 1, reach - tallies[taker]) // 2
    margin = jnp.where((giver == order[0]) | (taker == order[0]) | (tallies[taker] == 0), 0, jnp.maximum(margin, 0))
    moved = jax.random.randint(jax.random.fold_in(own, 4), (count // 2,), 0, 1 << 20) % (margin + 1)
    tallies = tallies.at[giver].add(-moved).at[taker].add(moved)
    members = jnp.searchsorted(jnp.cumsum(tallies), jnp.arange(rows * top), side="right").astype(jnp.int32)
    grid = members.reshape(top, rows).T
    grid = grid[jax.random.permutation(jax.random.fold_in(own, 1), rows)]
    offset_by = jax.random.randint(jax.random.fold_in(own, 2), (rows, 1), 0, top)
    return jnp.take_along_axis(grid, (jnp.arange(top)[None, :] + offset_by) % top, axis=1)


def load_shares(count, total, limit, slope, full):
    loads = [(1 << 20) // math.isqrt(grade ** slope) + 1 for grade in range(1, count + 1)]
    largest = limit if full else min(limit, max(-(-total // count), total * loads[0] // sum(loads)))
    least = 1 if total - largest >= count - 1 else 0
    counts, rest = [largest] + [least] * (count - 1), total - largest - least * (count - 1)
    while rest > 0:
        free = [i for i in range(1, count) if counts[i] < largest] or [i for i in range(1, count) if counts[i] < limit]
        mass, left = sum([loads[i] for i in free]), rest
        for i in free:
            extra = min(limit - counts[i], max(1, left * loads[i] // mass), rest)
            counts[i] = counts[i] + extra
            rest = rest - extra
    return np.array(counts)


def gaussian(key, extent, spread, reach, shards=(), held_as=jnp.bfloat16):
    array = jax.random.normal(key, extent, jnp.float32) * spread
    if len(shards) > 0:
        array = steps_of(key, extent, shards, -0.22, 0.18) * array
    return jnp.clip(array, min=-reach, max=reach).astype(held_as)


def setup_inputs(seed: int = 0) -> dict:
    seeds = jax.random.split(jax.random.key(seed), 15)
    coupling = gaussian(seeds[0], (NBLK, B, B), 0.3, 4.0, ((0, 128),))
    diag_inverse = gaussian(seeds[1], (NBLK, B, B), (B * B) ** -0.5, 0.046875, ((0, 128),), jnp.float32)
    pivot_inverse = gaussian(seeds[2], (PIVOTS, B, B), B ** -0.5, 0.5, ((0, 128),))
    cross_left = gaussian(seeds[3], (SLOTS, B, B), B ** -0.5, 0.5, ((0, 128),))
    cross_right = gaussian(seeds[4], (SLOTS, B, B), 0.25, 4.0, ((0, 128),))
    cross_pivot = with_ends(jax.random.randint(seeds[5], (SLOTS,), 0, PIV_DEV), jax.random.fold_in(seeds[5], 1), 0, PIV_DEV - 1).astype(jnp.int32)
    cross_owner_keys = jax.random.split(jax.random.fold_in(seeds[6], 1), SLOTS // UPD_DEV)
    cross_owner_turns = jax.random.permutation(jax.random.fold_in(seeds[6], 3), SLOTS // UPD_DEV)
    cross_owner = jax.vmap(lambda own, number: deal_out(jax.random.fold_in(seeds[6], 2), own, number, UPD_DEV, N_ROW, 1, UPD_DEV // 8, 2))(cross_owner_keys, cross_owner_turns).reshape((SLOTS, 1))
    foreign_target_row = with_ends(jax.random.randint(seeds[7], (SLOTS,), 0, ROWS_DEV), jax.random.fold_in(seeds[7], 1), 0, ROWS_DEV - 1).astype(jnp.int32)
    cross_count = ragged_sizes(seeds[8], N_SECTION * N_ROW, N_SECTION * N_ROW * UPD_DEV * 3 // 4, UPD_DEV, 2).astype(jnp.int32)
    local_left = gaussian(seeds[9], (LSLOTS, B, B), B ** -0.5, 0.5, ((0, 128),))
    local_right = gaussian(seeds[10], (LSLOTS, B, B), 0.25, 4.0, ((0, 128),))
    local_pivot = with_ends(jax.random.randint(seeds[11], (LSLOTS,), 0, PIV_DEV), jax.random.fold_in(seeds[11], 1), 0, PIV_DEV - 1).astype(jnp.int32)
    local_target = with_ends(jax.random.randint(seeds[12], (LSLOTS,), 0, ROWS_DEV), jax.random.fold_in(seeds[12], 1), 0, ROWS_DEV - 1).astype(jnp.int32)
    adjoint_seed = gaussian(seeds[13], (NBLK, NRHS, B), (B // 16), 48.0, ((0, 128),), jnp.float32)
    return dict(coupling=coupling, diag_inverse=diag_inverse, pivot_inverse=pivot_inverse, cross_left=cross_left, cross_right=cross_right, cross_pivot=cross_pivot, cross_owner=cross_owner, foreign_target_row=foreign_target_row, cross_count=cross_count, local_left=local_left, local_right=local_right, local_pivot=local_pivot, local_target=local_target, adjoint_seed=adjoint_seed)


precise = lax.Precision.HIGHEST


def scaled_products(lower_factor_blocks, upper_factor_blocks, selected_entry):
    rescaled_blocks = jnp.einsum("zmq,zqy->zmy", lower_factor_blocks.astype(jnp.float32), selected_entry.astype(jnp.float32)).astype(jnp.bfloat16)
    return jnp.einsum("zmq,zqy->zmy", rescaled_blocks.astype(jnp.float32), upper_factor_blocks.astype(jnp.float32)).astype(jnp.bfloat16)


def reference(coupling, diag_inverse, pivot_inverse, cross_left, cross_right, cross_pivot, cross_owner, foreign_target_row, cross_count, local_left, local_right, local_pivot, local_target, adjoint_seed):
    devices = N_SECTION * N_ROW
    total_rows = ROWS_DEV * devices
    width = coupling.shape[1]
    pivot_table = pivot_inverse.reshape(devices, PIV_DEV, width, width)
    inputs = (
        jnp.arange(devices, dtype=jnp.int32),
        cross_left.reshape(devices, UPD_DEV, width, width),
        cross_right.reshape(devices, UPD_DEV, width, width),
        cross_pivot.reshape(devices, UPD_DEV),
        cross_owner.reshape(devices, UPD_DEV),
        foreign_target_row.reshape(devices, UPD_DEV),
        cross_count,
        local_left.reshape(devices, LOC_DEV, width, width),
        local_right.reshape(devices, LOC_DEV, width, width),
        local_pivot.reshape(devices, LOC_DEV),
        local_target.reshape(devices, LOC_DEV),
        pivot_table,
    )

    def per_device(updated, pieces):
        (device, portion_lower_factor, piece_right, piece_pivot, piece_owner, piece_target, piece_count,
         own_left, own_right, own_pivot, own_target, piece_table) = pieces
        cross_blocks = scaled_products(portion_lower_factor, piece_right, piece_table[piece_pivot])
        local_blocks = scaled_products(own_left, own_right, piece_table[own_pivot])
        section_first = (device // N_ROW) * N_ROW
        live = jnp.arange(UPD_DEV, dtype=jnp.int32) < piece_count
        cross_rows = jnp.where(live, (section_first + piece_owner) * ROWS_DEV + piece_target, total_rows).astype(jnp.int32)
        local_rows = (device * ROWS_DEV + own_target).astype(jnp.int32)
        updated = updated.at[cross_rows].add(-cross_blocks.astype(jnp.float32), mode="drop")
        updated = updated.at[local_rows].add(-local_blocks.astype(jnp.float32))
        return updated, None

    updated, unused = lax.scan(per_device, coupling.astype(jnp.float32), inputs)
    step_matrix = -jnp.einsum("kab,kbc->kac", diag_inverse, updated, precision=precise)
    step_offset = jnp.einsum("kab,knb->kna", diag_inverse, adjoint_seed, precision=precise)
    per_section = N_ROW * ROWS_DEV
    section_matrix = step_matrix.reshape(N_SECTION, per_section, width, width)
    section_offset = step_offset.reshape(N_SECTION, per_section, NRHS, width)

    def backward(later, pieces):
        matrix, vector = pieces
        current = vector + jnp.einsum("kab,knb->kna", matrix, later, precision=precise)
        return current, current

    closing_state, adjoint = lax.scan(backward, jnp.zeros((per_section, NRHS, width), jnp.float32), (section_matrix, section_offset), reverse=True)
    return updated, adjoint.reshape(total_rows, NRHS, width)
```

```python
import functools

import jax
import jax.numpy as jnp
from jax import lax
from jax.experimental import pallas as pl
from jax.experimental.pallas import tpu as pltpu
from jax.sharding import PartitionSpec as P

B = 128
SIDE = 4
UNROLL = 4
MIB = 1 << 20

HBM = pl.BlockSpec(memory_space=pl.ANY)
VMEM = pl.BlockSpec(memory_space=pltpu.VMEM)
SMEM = pl.BlockSpec(memory_space=pltpu.SMEM)

bf16 = jnp.bfloat16
f32 = jnp.float32
precise = lax.Precision.HIGHEST


def mm(a, b):
    return jnp.dot(a, b, preferred_element_type=f32)


def mm_nt(a, b):
    return lax.dot_general(a, b, (((1,), (1,)), ((), ())), preferred_element_type=f32)


def split(x):
    high = x.astype(bf16)
    return high, (x - high.astype(f32)).astype(bf16)


def cross_kernel(first, cells, sizes, cell_ref, pivot_ref, table_ref, left_ref, right_ref, *refs):
    outs = refs[: len(sizes)]
    slot_list, cell_list, left, right, total, lsem, rsem, osem = refs[len(sizes) :]
    slots = left_ref.shape[0]

    def note(i, n):
        c = cell_ref[i] - first
        slot_list[n] = i
        cell_list[n] = c
        return n + jnp.where((c >= 0) & (c < cells), 1, 0)

    count = lax.fori_loop(0, slots, note, 0, unroll=8)
    rounds = (count + UNROLL - 1) // UNROLL

    def pad(j, _):
        slot_list[j] = 0
        cell_list[j] = cells
        return 0

    lax.fori_loop(count, rounds * UNROLL, pad, 0)

    def fetch(j, _):
        s = slot_list[j]
        pltpu.make_async_copy(left_ref.at[s], left.at[j], lsem.at[j]).start()
        pltpu.make_async_copy(right_ref.at[s], right.at[j], rsem.at[j]).start()
        return 0

    lax.fori_loop(0, rounds * UNROLL, fetch, 0)

    def clear(c, _):
        total[c] = jnp.zeros((B, B), bf16)
        return 0

    lax.fori_loop(0, cells + 1, clear, 0, unroll=4)

    def work(r, _):
        js = [r * UNROLL + u for u in range(UNROLL)]
        for j in js:
            pltpu.make_async_copy(left_ref.at[0], left.at[j], lsem.at[j]).wait()
            pltpu.make_async_copy(right_ref.at[0], right.at[j], rsem.at[j]).wait()
        scaled = [mm(left[j], table_ref[pivot_ref[slot_list[j]]]).astype(bf16) for j in js]
        updates = [mm(s, right[j]) for s, j in zip(scaled, js)]
        for j, u in zip(js, updates):
            c = cell_list[j]
            total[c] = (total[c].astype(f32) + u).astype(bf16)
        return 0

    lax.fori_loop(0, rounds, work, 0)

    copies = []
    start = 0
    for k, size in enumerate(sizes):
        copies.append(pltpu.make_async_copy(total.at[pl.ds(start, size)], outs[k], osem.at[k]))
        start += size
    for c in copies:
        c.start()
    for c in copies:
        c.wait()


def cross_sums(first, sizes, cell, pivot, table, left, right, live):
    cells = sum(sizes)
    slots = left.shape[0]
    return pl.pallas_call(
        functools.partial(cross_kernel, first, cells, sizes),
        out_shape=[jax.ShapeDtypeStruct((n, B, B), bf16) for n in sizes],
        in_specs=[SMEM, SMEM, VMEM, HBM, HBM],
        out_specs=[HBM] * len(sizes),
        scratch_shapes=[
            pltpu.SMEM((slots + UNROLL,), jnp.int32),
            pltpu.SMEM((slots + UNROLL,), jnp.int32),
            pltpu.VMEM((slots, B, B), bf16),
            pltpu.VMEM((slots, B, B), bf16),
            pltpu.VMEM((cells + 1, B, B), bf16),
            pltpu.SemaphoreType.DMA((slots,)),
            pltpu.SemaphoreType.DMA((slots,)),
            pltpu.SemaphoreType.DMA((len(sizes),)),
        ],
        compiler_params=pltpu.CompilerParams(vmem_limit_bytes=30 * MIB),
        cost_estimate=pl.CostEstimate(
            flops=live * 4 * B**3, bytes_accessed=live * 4 * B * B + cells * 2 * B * B, transcendentals=0
        ),
        name="cross_sums",
    )(cell, pivot, table, left, right)


def local_kernel(per_step, pivot_ref, target_ref, table_ref, coupling_ref, left_ref, right_ref, order_ref, out_ref):
    step = pl.program_id(0)

    @pl.when(step == 0)
    def _():
        out_ref[...] = coupling_ref[...].astype(f32)

    for base in range(0, per_step, UNROLL):
        js = range(base, base + UNROLL)
        scaled = [mm(left_ref[j], table_ref[pivot_ref[step * per_step + j]]).astype(bf16) for j in js]
        updates = [mm(s, right_ref[j]).astype(bf16).astype(f32) for s, j in zip(scaled, js)]
        for j, u in zip(js, updates):
            t = target_ref[step * per_step + j]
            out_ref[t] = out_ref[t] - u


def local_sums(pivot, target, table, coupling, left, right, order):
    slots = left.shape[0]
    rows = coupling.shape[0]
    per_step = 8
    block = pl.BlockSpec((per_step, B, B), lambda i: (i, 0, 0))
    return pl.pallas_call(
        functools.partial(local_kernel, per_step),
        grid=(slots // per_step,),
        out_shape=jax.ShapeDtypeStruct((rows, B, B), f32),
        in_specs=[SMEM, SMEM, VMEM, VMEM, block, block, HBM],
        out_specs=pl.BlockSpec((rows, B, B), lambda i: (0, 0, 0)),
        compiler_params=pltpu.CompilerParams(vmem_limit_bytes=16 * MIB),
        cost_estimate=pl.CostEstimate(
            flops=slots * 4 * B**3, bytes_accessed=slots * 4 * B * B + rows * 6 * B * B, transcendentals=0
        ),
        name="local_sums",
    )(pivot, target, table, coupling, left, right, order)


def first_totals_kernel(own_x, own_z, *refs):
    arrivals = refs[:8]
    outs = refs[8:16]
    held, sem = refs[16:]
    b = pl.program_id(0)
    for s, own in enumerate((own_x, own_z)):
        for half in range(2):
            t = own[half, 0].astype(f32)
            for a in arrivals[s * 4 + half * 2 : s * 4 + half * 2 + 2]:
                t = t + a[0].astype(f32)
            held[b, s, half] = t.astype(bf16)
    for k in range(SIDE):

        @pl.when(b == k)
        def _():
            for s in range(2):
                pltpu.make_async_copy(held.at[k, s], outs[s * SIDE + k], sem.at[k, s]).start()

    @pl.when(b == SIDE - 1)
    def _():
        for k in range(SIDE):
            for s in range(2):
                pltpu.make_async_copy(held.at[k, s], outs[s * SIDE + k], sem.at[k, s]).wait()


def first_totals(own_x, own_z, arrivals):
    quarter = own_x.shape[0] // (2 * SIDE)
    own_spec = pl.BlockSpec((2, 1, quarter, B, B), lambda b: (0, b, 0, 0, 0))
    spec = pl.BlockSpec((1, quarter, B, B), lambda b: (b, 0, 0, 0))
    outs = pl.pallas_call(
        first_totals_kernel,
        grid=(SIDE,),
        out_shape=[jax.ShapeDtypeStruct((2, quarter, B, B), bf16)] * (2 * SIDE),
        in_specs=[own_spec, own_spec] + [spec] * 8,
        out_specs=[HBM] * (2 * SIDE),
        scratch_shapes=[
            pltpu.VMEM((SIDE, 2, 2, quarter, B, B), bf16),
            pltpu.SemaphoreType.DMA((SIDE, 2)),
        ],
        compiler_params=pltpu.CompilerParams(vmem_limit_bytes=16 * MIB),
        cost_estimate=pl.CostEstimate(flops=0, bytes_accessed=256 * 2 * B * B, transcendentals=0),
        name="first_totals",
    )(
        own_x.reshape(2, SIDE, quarter, B, B),
        own_z.reshape(2, SIDE, quarter, B, B),
        *[a.reshape(SIDE, quarter, B, B) for a in arrivals],
    )
    return outs[:SIDE], outs[SIDE:]


def coupling_kernel(base_ref, diag_ref, *refs):
    parts = refs[:8]
    new_ref, step_ref = refs[8:]
    i = pl.program_id(0)
    per = base_ref.shape[0]
    steps = pl.num_programs(0) // 2

    def finish(mine):
        for r in range(per):
            t = base_ref[r]
            for p in mine:
                t = t - p[r].astype(f32)
            new_ref[r] = t
            th, tl = split(t)
            dh, dl = split(diag_ref[r])
            step_ref[r] = -(mm(dh, th) + (mm(dh, tl) + mm(dl, th))).astype(bf16)

    @pl.when(i < steps)
    def _():
        finish(parts[:4])

    @pl.when(i >= steps)
    def _():
        finish(parts[4:])


def coupling_and_step(base, diag, parts_x, parts_z):
    rows = base.shape[0]
    per = 2
    steps = rows // per // 2
    block = pl.BlockSpec((per, B, B), lambda i: (i, 0, 0))
    x_block = pl.BlockSpec((per, B, B), lambda i: (jnp.minimum(i, steps - 1), 0, 0))
    z_block = pl.BlockSpec((per, B, B), lambda i: (jnp.maximum(i - steps, 0), 0, 0))
    return pl.pallas_call(
        coupling_kernel,
        grid=(rows // per,),
        out_shape=[jax.ShapeDtypeStruct((rows, B, B), f32), jax.ShapeDtypeStruct((rows, B, B), bf16)],
        in_specs=[block, block] + [x_block] * 4 + [z_block] * 4,
        out_specs=[block, block],
        compiler_params=pltpu.CompilerParams(vmem_limit_bytes=16 * MIB),
        cost_estimate=pl.CostEstimate(flops=rows * 6 * B**3, bytes_accessed=rows * 22 * B * B, transcendentals=0),
        name="coupling_and_step",
    )(base, diag, *parts_x, *parts_z)


def chain_kernel(sections, chains, step_ref, offset_ref, out_ref):
    current = []
    for j in range(chains):
        k = (sections - 1) * chains + j
        o = offset_ref[k]
        out_ref[k] = o
        current.append(o.astype(f32))
    for s in range(sections - 2, -1, -1):
        for j in range(chains):
            k = s * chains + j
            high, low = split(current[j])
            m = step_ref[k]
            new = offset_ref[k].astype(f32) + (mm_nt(high, m) + mm_nt(low, m))
            out_ref[k] = new.astype(bf16)
            current[j] = new


def run_chains(sections, steps, offsets):
    rows = steps.shape[0]
    return pl.pallas_call(
        functools.partial(chain_kernel, sections, rows // sections),
        out_shape=jax.ShapeDtypeStruct((rows, B, B), bf16),
        in_specs=[VMEM, VMEM],
        out_specs=VMEM,
        compiler_params=pltpu.CompilerParams(vmem_limit_bytes=16 * MIB),
        cost_estimate=pl.CostEstimate(flops=rows * 4 * B**3, bytes_accessed=rows * 6 * B * B, transcendentals=0),
        name="run_chains",
    )(steps, offsets)


def moved(x, along, by):
    pairs = []
    for a in range(SIDE):
        for c in range(SIDE):
            if along == 0:
                pairs.append((a * SIDE + c, (a + by) % SIDE * SIDE + c))
            else:
                pairs.append((a * SIDE + c, a * SIDE + (c + by) % SIDE))
    return lax.ppermute(x, "row", pairs)


def add(a, b):
    return (a.astype(f32) + b.astype(f32)).astype(bf16)


def per_device(
    coupling,
    diag_inverse,
    pivot_inverse,
    cross_left,
    cross_right,
    cross_pivot,
    cross_owner,
    foreign_target_row,
    cross_count,
    local_left,
    local_right,
    local_pivot,
    local_target,
    adjoint_seed,
):
    sections = lax.axis_size("section")
    rows = coupling.shape[0]
    slots = cross_left.shape[0]
    half = rows // 2
    quarter = rows // 4
    me = lax.axis_index("row")

    owner = cross_owner[:, 0]
    dx = (owner // SIDE - me // SIDE) % SIDE
    dz = (owner % SIDE - me % SIDE) % SIDE
    second = foreign_target_row // half
    row = foreign_target_row % half
    a = jnp.where(second == 0, dx, dz)
    b = jnp.where(second == 0, dz, dx)
    upper = row // quarter
    spot = b * quarter + row % quarter
    n = SIDE * quarter
    group = 4 * n
    minus = (a == 3).astype(jnp.int32)
    cell = jnp.where(
        a == 2,
        second * 2 * n + upper * n + spot,
        jnp.where(
            a == 0,
            3 * group + second * 2 * n + upper * n + spot,
            jnp.where(minus == upper, 2 * group, group) + second * 2 * n + minus * n + spot,
        ),
    )
    live = jnp.arange(slots, dtype=jnp.int32) < cross_count[0]
    cell = jnp.where(live, cell, -1)

    sums = functools.partial(
        cross_sums,
        cell=cell,
        pivot=cross_pivot,
        table=pivot_inverse,
        left=cross_left,
        right=cross_right,
    )
    far = sums(0, [n] * 4, live=slots // 4)
    ways = ((0, 1), (0, -1), (1, 1), (1, -1))
    far_in = [moved(x, *w) for x, w in zip(far, ways)]
    near = sums(group, [n] * 8 + [2 * n] * 2, live=slots * 3 // 4)
    free_in = [moved(x, *w) for x, w in zip(near[:4], ways)]
    joined = [add(x, y) for x, y in zip(near[4:8], far_in)]
    joined_in = [moved(x, *w) for x, w in zip(joined, ways)]

    step_offset = jnp.einsum("kab,knb->kna", diag_inverse, adjoint_seed, precision=precise).astype(bf16)
    offsets = lax.all_to_all(step_offset, "section", split_axis=0, concat_axis=0, tiled=True)
    base = local_sums(local_pivot, local_target, pivot_inverse, coupling, local_left, local_right, joined[0])

    arrivals = []
    for s in range(2):
        fp, fm = free_in[2 * s : 2 * s + 2]
        jp, jm = joined_in[2 * s : 2 * s + 2]
        arrivals += [jp, fm, fp, jm]
    tot_x, tot_z = first_totals(near[8], near[9], arrivals)
    flat = lambda x: x.reshape(half, B, B)
    parts_x = [flat(tot_x[0])] + [moved(flat(tot_x[k]), 1, k) for k in (2, 1, 3)]
    parts_z = [flat(tot_z[0])] + [moved(flat(tot_z[k]), 0, k) for k in (2, 1, 3)]
    updated, step_matrix = coupling_and_step(base, diag_inverse, parts_x, parts_z)
    steps = lax.all_to_all(step_matrix, "section", split_axis=0, concat_axis=0, tiled=True)
    solved = run_chains(sections, steps, offsets)
    adjoint = lax.all_to_all(solved, "section", split_axis=0, concat_axis=0, tiled=True).astype(f32)
    return (updated, adjoint)


def solution(mesh):
    spread = ("section", "row")
    block = P(spread, None, None)
    line = P(spread)
    return jax.shard_map(
        per_device,
        mesh=mesh,
        in_specs=(
            block,
            block,
            block,
            block,
            block,
            line,
            P(spread, None),
            line,
            line,
            block,
            block,
            line,
            line,
            block,
        ),
        out_specs=(block, block),
        check_vma=False,
    )
```

```python
import functools

import jax
import jax.numpy as jnp
from jax import lax
from jax.experimental import pallas as pl
from jax.experimental.pallas import tpu as pltpu
from jax.sharding import PartitionSpec as P

B = 128
SIDE = 4
UNROLL = 16
CHUNKS = 8
CELL_MASK, PIVOT_BIT, FAR_BIT, NEAR_BIT, SLOT_BIT = 511, 9, 16, 17, 20
MIB = 1 << 20

ANY = pl.BlockSpec(memory_space=pl.ANY)
HBM = pl.BlockSpec(memory_space=pltpu.HBM)
VMEM = pl.BlockSpec(memory_space=pltpu.VMEM)
SMEM = pl.BlockSpec(memory_space=pltpu.SMEM)

bf16 = jnp.bfloat16
f32 = jnp.float32


def mm(a, b):
    return jnp.dot(a, b, preferred_element_type=f32)


def mm_nt(a, b):
    return lax.dot_general(a, b, (((1,), (1,)), ((), ())), preferred_element_type=f32)


def split(x):
    high = x.astype(bf16)
    return high, (x - high.astype(f32)).astype(bf16)


def stay(x):
    return pltpu.with_memory_space_constraint(x, pltpu.HBM)


def bulk(left_ref, right_ref, left, right, lsem, rsem):
    per = left.shape[0] // CHUNKS
    pairs = []
    for k in range(CHUNKS):
        part = pl.ds(k * per, per)
        pair = (
            pltpu.make_async_copy(left_ref.at[part], left.at[part], lsem.at[k]),
            pltpu.make_async_copy(right_ref.at[part], right.at[part], rsem.at[k]),
        )
        for c in pair:
            c.start()
        pairs.append(pair)
    return pairs


def cross_kernel(first, sizes, flag, index_ref, table_ref, left_ref, right_ref, *refs):
    outs = refs[-8 - len(sizes) : -8]
    listed, left, right, total, table, lsem, rsem, tsem = refs[-8:]
    cells = sum(sizes)
    slots = left.shape[0]
    table_copy = pltpu.make_async_copy(table_ref, table, tsem)
    table_copy.start()
    pairs = bulk(left_ref, right_ref, left, right, lsem, rsem)

    def note(i, n):
        word = index_ref[i]
        listed[n] = word
        return n + ((word >> flag) & 1)

    count = lax.fori_loop(0, slots, note, 0, unroll=32)
    for u in range(UNROLL):
        listed[count + u] = first + cells

    def clear(c, _):
        total[c] = jnp.zeros((B, B), bf16)
        return 0

    lax.fori_loop(0, cells + 1, clear, 0, unroll=8)
    table_copy.wait()
    for pair in pairs:
        for c in pair:
            c.wait()

    def work(r, _):
        words = [listed[r * UNROLL + u] for u in range(UNROLL)]
        scaled = [mm(left[w >> SLOT_BIT], table[(w >> PIVOT_BIT) & 3]).astype(bf16) for w in words]
        updates = [mm(x, right[w >> SLOT_BIT]) for x, w in zip(scaled, words)]
        for w, u in zip(words, updates):
            c = (w & CELL_MASK) - first
            total[c] = (total[c].astype(f32) + u).astype(bf16)
        return 0

    lax.fori_loop(0, (count + UNROLL - 1) // UNROLL, work, 0)

    start = 0
    for out, size in zip(outs, sizes):

        def give(c, _, out=out, start=start):
            out[c] = total[start + c]
            return 0

        lax.fori_loop(0, size, give, 0, unroll=8)
        start += size


def cross_sums(first, sizes, flag, index, table, left, right, live, order=()):
    cells = sum(sizes)
    slots = left.shape[0]
    return pl.pallas_call(
        functools.partial(cross_kernel, first, sizes, flag),
        out_shape=[jax.ShapeDtypeStruct((n, B, B), bf16) for n in sizes],
        in_specs=[SMEM, HBM, HBM, HBM] + [ANY] * len(order),
        out_specs=[VMEM] * len(sizes),
        scratch_shapes=[
            pltpu.SMEM((slots + UNROLL,), jnp.int32),
            pltpu.VMEM((slots, B, B), bf16),
            pltpu.VMEM((slots, B, B), bf16),
            pltpu.VMEM((cells + 1, B, B), bf16),
            pltpu.VMEM(table.shape, bf16),
            pltpu.SemaphoreType.DMA((CHUNKS,)),
            pltpu.SemaphoreType.DMA((CHUNKS,)),
            pltpu.SemaphoreType.DMA,
        ],
        compiler_params=pltpu.CompilerParams(vmem_limit_bytes=9 * MIB + cells * 4 * B * B),
        cost_estimate=pl.CostEstimate(
            flops=live * 4 * B**3, bytes_accessed=slots * 4 * B * B + cells * 2 * B * B, transcendentals=0
        ),
        name="cross_sums",
    )(index, stay(table), stay(left), stay(right), *order)


def offset_kernel(diag_ref, seed_ref, out_ref, held, sem):
    rows = held.shape[0]
    group = rows // 2
    copies = []
    for g in range(2):

        def one(i, _, g=g):
            r = g * group + i
            dh, dl = split(diag_ref[r])
            sh, sl = split(seed_ref[r])
            held[r] = (mm_nt(sh, dh) + (mm_nt(sh, dl) + mm_nt(sl, dh))).astype(bf16)
            return 0

        lax.fori_loop(0, group, one, 0, unroll=4)
        part = pl.ds(g * group, group)
        copies.append(pltpu.make_async_copy(held.at[part], out_ref.at[part], sem.at[g]))
        copies[-1].start()
    for c in copies:
        c.wait()


def offsets_of(diag, seed):
    rows = diag.shape[0]
    return pl.pallas_call(
        offset_kernel,
        out_shape=jax.ShapeDtypeStruct((rows, B, B), bf16),
        in_specs=[VMEM, VMEM],
        out_specs=HBM,
        scratch_shapes=[pltpu.VMEM((rows, B, B), bf16), pltpu.SemaphoreType.DMA((2,))],
        compiler_params=pltpu.CompilerParams(vmem_limit_bytes=4 * MIB),
        cost_estimate=pl.CostEstimate(flops=rows * 6 * B**3, bytes_accessed=rows * 10 * B * B, transcendentals=0),
        name="offsets",
    )(diag, seed)


def local_kernel(index_ref, table_ref, coupling_ref, left_ref, right_ref, *refs):
    base_ref, left, right, table, lsem, rsem, tsem = refs[-7:]
    slots = left.shape[0]
    rows = coupling_ref.shape[0]
    table_copy = pltpu.make_async_copy(table_ref, table, tsem)
    table_copy.start()
    pairs = bulk(left_ref, right_ref, left, right, lsem, rsem)
    for r in range(rows):
        base_ref[r] = coupling_ref[r].astype(f32)
    table_copy.wait()
    per = slots // CHUNKS
    for k, pair in enumerate(pairs):
        for c in pair:
            c.wait()

        def work(i, _, k=k):
            at = [k * per + i * UNROLL + u for u in range(UNROLL)]
            words = [index_ref[j] for j in at]
            scaled = [mm(left[j], table[(w >> PIVOT_BIT) & 3]).astype(bf16) for j, w in zip(at, words)]
            updates = [mm(x, right[j]).astype(bf16).astype(f32) for x, j in zip(scaled, at)]
            for w, u in zip(words, updates):
                t = w & CELL_MASK
                base_ref[t] = base_ref[t] - u
            return 0

        lax.fori_loop(0, per // UNROLL, work, 0)


def local_sums(index, table, coupling, left, right, order):
    slots = left.shape[0]
    rows = coupling.shape[0]
    return pl.pallas_call(
        local_kernel,
        out_shape=jax.ShapeDtypeStruct((rows, B, B), f32),
        in_specs=[SMEM, HBM, VMEM, HBM, HBM] + [ANY] * len(order),
        out_specs=VMEM,
        scratch_shapes=[
            pltpu.VMEM((slots, B, B), bf16),
            pltpu.VMEM((slots, B, B), bf16),
            pltpu.VMEM(table.shape, bf16),
            pltpu.SemaphoreType.DMA((CHUNKS,)),
            pltpu.SemaphoreType.DMA((CHUNKS,)),
            pltpu.SemaphoreType.DMA,
        ],
        compiler_params=pltpu.CompilerParams(vmem_limit_bytes=12 * MIB),
        cost_estimate=pl.CostEstimate(
            flops=slots * 4 * B**3, bytes_accessed=slots * 4 * B * B + rows * 6 * B * B, transcendentals=0
        ),
        name="local_sums",
    )(index, stay(table), coupling, stay(left), stay(right), *order)


def first_totals_kernel(own_x, own_z, *refs):
    arrivals = refs[:8]
    outs = refs[-2 * SIDE :]
    q = arrivals[0].shape[0] // SIDE
    for s, own in enumerate((own_x, own_z)):
        for half in range(2):
            for b in range(SIDE):
                t = own[pl.ds((half * SIDE + b) * q, q)].astype(f32)
                for a in arrivals[s * 4 + half * 2 : s * 4 + half * 2 + 2]:
                    t = t + a[pl.ds(b * q, q)].astype(f32)
                outs[s * SIDE + b][pl.ds(half * q, q)] = t.astype(bf16)


def first_totals(own_x, own_z, arrivals, order):
    half = own_x.shape[0] // SIDE
    outs = pl.pallas_call(
        first_totals_kernel,
        out_shape=[jax.ShapeDtypeStruct((half, B, B), bf16)] * (2 * SIDE),
        in_specs=[VMEM] * 10 + [ANY] * len(order),
        out_specs=[VMEM] * (2 * SIDE),
        compiler_params=pltpu.CompilerParams(vmem_limit_bytes=9 * MIB),
        cost_estimate=pl.CostEstimate(flops=0, bytes_accessed=256 * 2 * B * B, transcendentals=0),
        name="first_totals",
    )(own_x, own_z, *arrivals, *order)
    return outs[:SIDE], outs[SIDE:]


def coupling_kernel(base_ref, diag_ref, *refs):
    new_ref, step_ref = refs[8:]
    half = base_ref.shape[0] // 2
    for s in range(2):
        parts = refs[s * 4 : s * 4 + 4]

        def finish(i, _, s=s, parts=parts):
            r = s * half + i
            t = base_ref[r]
            for p in parts:
                t = t - p[i].astype(f32)
            new_ref[r] = t
            th, tl = split(t)
            dh, dl = split(diag_ref[r])
            step_ref[r] = -(mm(dh, th) + (mm(dh, tl) + mm(dl, th))).astype(bf16)
            return 0

        lax.fori_loop(0, half, finish, 0, unroll=4)


def coupling_and_step(base, diag, parts_x, parts_z):
    rows = base.shape[0]
    return pl.pallas_call(
        coupling_kernel,
        out_shape=[jax.ShapeDtypeStruct((rows, B, B), f32), jax.ShapeDtypeStruct((rows, B, B), bf16)],
        in_specs=[VMEM] * 10,
        out_specs=[VMEM, VMEM],
        compiler_params=pltpu.CompilerParams(vmem_limit_bytes=7 * MIB),
        cost_estimate=pl.CostEstimate(flops=rows * 6 * B**3, bytes_accessed=rows * 22 * B * B, transcendentals=0),
        name="coupling_and_step",
    )(base, diag, *parts_x, *parts_z)


def chain_kernel(sections, chains, step_ref, offset_ref, out_ref):
    current = []
    for j in range(chains):
        k = (sections - 1) * chains + j
        o = offset_ref[k]
        out_ref[k] = o
        current.append(o.astype(f32))
    for s in range(sections - 2, -1, -1):
        for j in range(chains):
            k = s * chains + j
            high, low = split(current[j])
            m = step_ref[k]
            new = offset_ref[k].astype(f32) + (mm_nt(high, m) + mm_nt(low, m))
            out_ref[k] = new.astype(bf16)
            current[j] = new


def run_chains(sections, steps, offsets):
    rows = steps.shape[0]
    return pl.pallas_call(
        functools.partial(chain_kernel, sections, rows // sections),
        out_shape=jax.ShapeDtypeStruct((rows, B, B), bf16),
        in_specs=[VMEM, VMEM],
        out_specs=VMEM,
        compiler_params=pltpu.CompilerParams(vmem_limit_bytes=4 * MIB),
        cost_estimate=pl.CostEstimate(flops=rows * 4 * B**3, bytes_accessed=rows * 6 * B * B, transcendentals=0),
        name="run_chains",
    )(steps, offsets)


def moved(x, along, by):
    pairs = []
    for a in range(SIDE):
        for c in range(SIDE):
            if along == 0:
                pairs.append((a * SIDE + c, (a + by) % SIDE * SIDE + c))
            else:
                pairs.append((a * SIDE + c, a * SIDE + (c + by) % SIDE))
    return lax.ppermute(x, "row", pairs)


def add(a, b):
    return (a.astype(f32) + b.astype(f32)).astype(bf16)


def per_device(
    coupling,
    diag_inverse,
    pivot_inverse,
    cross_left,
    cross_right,
    cross_pivot,
    cross_owner,
    foreign_target_row,
    cross_count,
    local_left,
    local_right,
    local_pivot,
    local_target,
    adjoint_seed,
):
    sections = lax.axis_size("section")
    rows = coupling.shape[0]
    slots = cross_left.shape[0]
    half = rows // 2
    quarter = rows // 4
    me = lax.axis_index("row")

    owner = cross_owner[:, 0]
    dx = (owner // SIDE - me // SIDE) % SIDE
    dz = (owner % SIDE - me % SIDE) % SIDE
    second = foreign_target_row // half
    row = foreign_target_row % half
    a = jnp.where(second == 0, dx, dz)
    b = jnp.where(second == 0, dz, dx)
    upper = row // quarter
    spot = b * quarter + row % quarter
    n = SIDE * quarter
    group = 4 * n
    minus = (a == 3).astype(jnp.int32)
    cell = jnp.where(
        a == 2,
        second * 2 * n + upper * n + spot,
        jnp.where(
            a == 0,
            3 * group + second * 2 * n + upper * n + spot,
            jnp.where(minus == upper, 2 * group, group) + second * 2 * n + minus * n + spot,
        ),
    )
    slot = jnp.arange(slots, dtype=jnp.int32)
    live = slot < cross_count[0]
    word = cell | (cross_pivot << PIVOT_BIT) | (slot << SLOT_BIT)
    word = word | jnp.where(live, jnp.where(cell < group, 1 << FAR_BIT, 1 << NEAR_BIT), 0)
    local_word = local_target | (local_pivot << PIVOT_BIT)

    step_offset = offsets_of(diag_inverse, adjoint_seed)
    every = lax.all_gather(step_offset, "section", axis=0, tiled=False)
    chains = rows // sections

    sums = functools.partial(cross_sums, index=word, table=pivot_inverse, left=cross_left, right=cross_right)
    far = sums(0, [n] * 4, FAR_BIT, live=slots // 4, order=[step_offset])
    ways = ((0, 1), (0, -1), (1, 1), (1, -1))
    far_in = [moved(x, *w) for x, w in zip(far, ways)]
    near = sums(group, [n] * 8 + [2 * n] * 2, NEAR_BIT, live=slots * 3 // 4)
    free_in = [moved(x, *w) for x, w in zip(near[:4], ways)]
    joined = [add(x, y) for x, y in zip(near[4:8], far_in)]
    joined_in = [moved(x, *w) for x, w in zip(joined, ways)]

    base = local_sums(local_word, pivot_inverse, coupling, local_left, local_right, joined)

    arrivals = []
    for s in range(2):
        fp, fm = free_in[2 * s : 2 * s + 2]
        jp, jm = joined_in[2 * s : 2 * s + 2]
        arrivals += [jp, fm, fp, jm]
    tot_x, tot_z = first_totals(near[8], near[9], arrivals, [base])
    parts_x = [tot_x[0]] + [moved(tot_x[k], 1, k) for k in (2, 1, 3)]
    parts_z = [tot_z[0]] + [moved(tot_z[k], 0, k) for k in (2, 1, 3)]
    updated, step_matrix = coupling_and_step(base, diag_inverse, parts_x, parts_z)
    steps = lax.all_to_all(step_matrix, "section", split_axis=0, concat_axis=0, tiled=True)
    offsets = lax.dynamic_slice_in_dim(every, lax.axis_index("section") * chains, chains, axis=1)
    offsets = offsets.reshape(rows, B, B)
    solved = run_chains(sections, steps, offsets)
    adjoint = lax.all_to_all(solved, "section", split_axis=0, concat_axis=0, tiled=True).astype(f32)
    return (updated, adjoint)


def solution(mesh):
    spread = ("section", "row")
    block = P(spread, None, None)
    line = P(spread)
    return jax.shard_map(
        per_device,
        mesh=mesh,
        in_specs=(
            block,
            block,
            block,
            block,
            block,
            line,
            P(spread, None),
            line,
            line,
            block,
            block,
            line,
            line,
            block,
        ),
        out_specs=(block, block),
        check_vma=False,
    )
```

```python
import functools

import jax
import jax.numpy as jnp
from jax import lax
from jax.experimental import pallas as pl
from jax.experimental.pallas import tpu as pltpu
from jax.sharding import PartitionSpec as P

B = 128
SIDE = 4
UNROLL = 16
CHUNKS = 8
CELL_MASK, PIVOT_BIT, FAR_BIT, NEAR_BIT, SLOT_BIT = 511, 9, 16, 17, 20
MIB = 1 << 20

ANY = pl.BlockSpec(memory_space=pl.ANY)
HBM = pl.BlockSpec(memory_space=pltpu.HBM)
VMEM = pl.BlockSpec(memory_space=pltpu.VMEM)
SMEM = pl.BlockSpec(memory_space=pltpu.SMEM)

bf16 = jnp.bfloat16
f32 = jnp.float32


def mm(a, b):
    return jnp.dot(a, b, preferred_element_type=f32)


def mm_nt(a, b):
    return lax.dot_general(a, b, (((1,), (1,)), ((), ())), preferred_element_type=f32)


def split(x):
    high = x.astype(bf16)
    return high, (x - high.astype(f32)).astype(bf16)


def stay(x):
    return pltpu.with_memory_space_constraint(x, pltpu.HBM)


def bulk(left_ref, right_ref, left, right, lsem, rsem):
    per = left.shape[0] // CHUNKS
    pairs = []
    for k in range(CHUNKS):
        part = pl.ds(k * per, per)
        pair = (
            pltpu.make_async_copy(left_ref.at[part], left.at[part], lsem.at[k]),
            pltpu.make_async_copy(right_ref.at[part], right.at[part], rsem.at[k]),
        )
        for c in pair:
            c.start()
        pairs.append(pair)
    return pairs


def cross_kernel(first, sizes, flag, index_ref, table_ref, left_ref, right_ref, *refs):
    outs = refs[-8 - len(sizes) : -8]
    listed, left, right, total, table, lsem, rsem, tsem = refs[-8:]
    cells = sum(sizes)
    slots = left.shape[0]
    table_copy = pltpu.make_async_copy(table_ref, table, tsem)
    table_copy.start()
    pairs = bulk(left_ref, right_ref, left, right, lsem, rsem)

    def note(i, n):
        word = index_ref[i]
        listed[n] = word
        return n + ((word >> flag) & 1)

    count = lax.fori_loop(0, slots, note, 0, unroll=32)
    for u in range(UNROLL):
        listed[count + u] = first + cells

    def clear(c, _):
        total[c] = jnp.zeros((B, B), bf16)
        return 0

    lax.fori_loop(0, cells + 1, clear, 0, unroll=8)
    table_copy.wait()
    for pair in pairs:
        for c in pair:
            c.wait()

    def work(r, _):
        words = [listed[r * UNROLL + u] for u in range(UNROLL)]
        scaled = [mm(left[w >> SLOT_BIT], table[(w >> PIVOT_BIT) & 3]).astype(bf16) for w in words]
        updates = [mm(x, right[w >> SLOT_BIT]) for x, w in zip(scaled, words)]
        for w, u in zip(words, updates):
            c = (w & CELL_MASK) - first
            total[c] = (total[c].astype(f32) + u).astype(bf16)
        return 0

    lax.fori_loop(0, (count + UNROLL - 1) // UNROLL, work, 0)

    start = 0
    for out, size in zip(outs, sizes):

        def give(c, _, out=out, start=start):
            out[c] = total[start + c]
            return 0

        lax.fori_loop(0, size, give, 0, unroll=8)
        start += size


def cross_sums(first, sizes, flag, index, table, left, right, live, order=()):
    cells = sum(sizes)
    slots = left.shape[0]
    return pl.pallas_call(
        functools.partial(cross_kernel, first, sizes, flag),
        out_shape=[jax.ShapeDtypeStruct((n, B, B), bf16) for n in sizes],
        in_specs=[SMEM, HBM, HBM, HBM] + [ANY] * len(order),
        out_specs=[VMEM] * len(sizes),
        scratch_shapes=[
            pltpu.SMEM((slots + UNROLL,), jnp.int32),
            pltpu.VMEM((slots, B, B), bf16),
            pltpu.VMEM((slots, B, B), bf16),
            pltpu.VMEM((cells + 1, B, B), bf16),
            pltpu.VMEM(table.shape, bf16),
            pltpu.SemaphoreType.DMA((CHUNKS,)),
            pltpu.SemaphoreType.DMA((CHUNKS,)),
            pltpu.SemaphoreType.DMA,
        ],
        compiler_params=pltpu.CompilerParams(vmem_limit_bytes=9 * MIB + cells * 4 * B * B),
        cost_estimate=pl.CostEstimate(
            flops=live * 4 * B**3, bytes_accessed=slots * 4 * B * B + cells * 2 * B * B, transcendentals=0
        ),
        name="cross_sums",
    )(index, stay(table), stay(left), stay(right), *order)


def local_kernel(index_ref, table_ref, coupling_ref, left_ref, right_ref, diag_ref, seed_ref, *refs):
    base_ref, offset_ref, left, right, table, lsem, rsem, tsem = refs[-8:]
    slots = left.shape[0]
    rows = coupling_ref.shape[0]
    half = rows // 2
    core = lax.axis_index("section") % 2
    table_copy = pltpu.make_async_copy(table_ref, table, tsem)
    table_copy.start()
    pairs = bulk(left_ref, right_ref, left, right, lsem, rsem)
    for r in range(rows):
        base_ref[r] = coupling_ref[r].astype(f32)

    def offset(r, _):
        dh, dl = split(diag_ref[r])
        sh, sl = split(seed_ref[r])
        o = mm_nt(sh, dh) + (mm_nt(sh, dl) + mm_nt(sl, dh))
        offset_ref[(r + core * half) % rows] = o.astype(bf16)
        return 0

    lax.fori_loop(0, rows, offset, 0, unroll=4)
    table_copy.wait()
    per = slots // CHUNKS
    for k, pair in enumerate(pairs):
        for c in pair:
            c.wait()

        def work(i, _, k=k):
            at = [k * per + i * UNROLL + u for u in range(UNROLL)]
            words = [index_ref[j] for j in at]
            scaled = [mm(left[j], table[(w >> PIVOT_BIT) & 3]).astype(bf16) for j, w in zip(at, words)]
            updates = [mm(x, right[j]).astype(bf16).astype(f32) for x, j in zip(scaled, at)]
            for w, u in zip(words, updates):
                t = w & CELL_MASK
                base_ref[t] = base_ref[t] - u
            return 0

        lax.fori_loop(0, per // UNROLL, work, 0)


def local_and_offset(index, table, coupling, left, right, diag, seed, order):
    slots = left.shape[0]
    rows = coupling.shape[0]
    return pl.pallas_call(
        local_kernel,
        out_shape=[jax.ShapeDtypeStruct((rows, B, B), f32), jax.ShapeDtypeStruct((rows, B, B), bf16)],
        in_specs=[SMEM, HBM, VMEM, HBM, HBM, VMEM, VMEM] + [ANY] * len(order),
        out_specs=[VMEM, VMEM],
        scratch_shapes=[
            pltpu.VMEM((slots, B, B), bf16),
            pltpu.VMEM((slots, B, B), bf16),
            pltpu.VMEM(table.shape, bf16),
            pltpu.SemaphoreType.DMA((CHUNKS,)),
            pltpu.SemaphoreType.DMA((CHUNKS,)),
            pltpu.SemaphoreType.DMA,
        ],
        compiler_params=pltpu.CompilerParams(vmem_limit_bytes=16 * MIB),
        cost_estimate=pl.CostEstimate(
            flops=slots * 4 * B**3, bytes_accessed=slots * 4 * B * B + rows * 16 * B * B, transcendentals=0
        ),
        name="local_and_offset",
    )(index, stay(table), coupling, stay(left), stay(right), diag, seed, *order)


def first_totals_kernel(own_x, own_z, *refs):
    arrivals = refs[:8]
    outs = refs[-2 * SIDE :]
    q = arrivals[0].shape[0] // SIDE
    for s, own in enumerate((own_x, own_z)):
        for half in range(2):
            for b in range(SIDE):
                t = own[pl.ds((half * SIDE + b) * q, q)].astype(f32)
                for a in arrivals[s * 4 + half * 2 : s * 4 + half * 2 + 2]:
                    t = t + a[pl.ds(b * q, q)].astype(f32)
                outs[s * SIDE + b][pl.ds(half * q, q)] = t.astype(bf16)


def first_totals(own_x, own_z, arrivals, order):
    half = own_x.shape[0] // SIDE
    outs = pl.pallas_call(
        first_totals_kernel,
        out_shape=[jax.ShapeDtypeStruct((half, B, B), bf16)] * (2 * SIDE),
        in_specs=[VMEM] * 10 + [ANY] * len(order),
        out_specs=[VMEM] * (2 * SIDE),
        compiler_params=pltpu.CompilerParams(vmem_limit_bytes=9 * MIB),
        cost_estimate=pl.CostEstimate(flops=0, bytes_accessed=256 * 2 * B * B, transcendentals=0),
        name="first_totals",
    )(own_x, own_z, *arrivals, *order)
    return outs[:SIDE], outs[SIDE:]


def coupling_kernel(base_ref, diag_ref, offset_ref, *refs):
    new_ref, keep_ref, give_ref, held = refs[-4:]
    rows = base_ref.shape[0]
    half = rows // 2
    core = lax.axis_index("section") % 2
    for s in range(2):
        parts = refs[s * 4 : s * 4 + 4]

        def finish(i, _, s=s, parts=parts):
            r = s * half + i
            t = base_ref[r]
            for p in parts:
                t = t - p[i].astype(f32)
            new_ref[r] = t
            th, tl = split(t)
            dh, dl = split(diag_ref[r])
            held[(r + core * half) % rows] = -(mm(dh, th) + (mm(dh, tl) + mm(dl, th))).astype(bf16)
            return 0

        lax.fori_loop(0, half, finish, 0, unroll=4)
    for i in range(half):
        keep_ref[i] = held[i]
        give_ref[i] = held[half + i]
        give_ref[half + i] = offset_ref[half + i]


def coupling_and_step(base, diag, offsets, parts_x, parts_z):
    rows = base.shape[0]
    half = rows // 2
    return pl.pallas_call(
        coupling_kernel,
        out_shape=[
            jax.ShapeDtypeStruct((rows, B, B), f32),
            jax.ShapeDtypeStruct((half, B, B), bf16),
            jax.ShapeDtypeStruct((rows, B, B), bf16),
        ],
        in_specs=[VMEM] * 11,
        out_specs=[VMEM] * 3,
        scratch_shapes=[pltpu.VMEM((rows, B, B), bf16)],
        compiler_params=pltpu.CompilerParams(vmem_limit_bytes=9 * MIB),
        cost_estimate=pl.CostEstimate(flops=rows * 6 * B**3, bytes_accessed=rows * 22 * B * B, transcendentals=0),
        name="coupling_and_step",
    )(base, diag, offsets, *parts_x, *parts_z)


def compose_kernel(chips, keep_ref, offset_ref, got_ref, *outs):
    section = lax.axis_index("section")
    chip = section // 2
    half = keep_ref.shape[0]
    per = half // chips

    def compose(first):
        for k in range(chips):
            for j in range(per):
                i = (chip + k) % chips * per + j
                mine = (keep_ref[i], offset_ref[i])
                other = (got_ref[i], got_ref[half + i])
                (ma, oa), (mb, ob) = (mine, other) if first else (other, mine)
                outs[k][j] = mm(ma, mb).astype(bf16)
                outs[k][per + j] = (oa.astype(f32) + mm_nt(ob, ma)).astype(bf16)

    @pl.when(section % 2 == 0)
    def _():
        compose(True)

    @pl.when(section % 2 == 1)
    def _():
        compose(False)


def compose(chips, keep, offsets, got):
    half = keep.shape[0]
    return pl.pallas_call(
        functools.partial(compose_kernel, chips),
        out_shape=[jax.ShapeDtypeStruct((2 * half // chips, B, B), bf16)] * chips,
        in_specs=[VMEM] * 3,
        out_specs=[VMEM] * chips,
        compiler_params=pltpu.CompilerParams(vmem_limit_bytes=4 * MIB),
        cost_estimate=pl.CostEstimate(flops=half * 4 * B**3, bytes_accessed=half * 12 * B * B, transcendentals=0),
        name="compose",
    )(keep, offsets, got)


def chain_kernel(chips, *refs):
    parts = refs[:chips]
    outs = refs[chips : 2 * chips]
    maps, incoming = refs[2 * chips :]
    chip = lax.axis_index("section") // 2
    per = outs[0].shape[0]
    for k in range(chips):
        for i in range(2 * per):
            maps[(chip - k + chips) % chips, i] = parts[k][i]
    current = [jnp.zeros((B, B), f32)] * per
    for c in range(chips - 1, -1, -1):
        for j in range(per):
            incoming[c, j] = current[j].astype(bf16)
            if c > 0:
                new = maps[c, per + j].astype(f32)
                if c < chips - 1:
                    high, low = split(current[j])
                    new = new + (mm_nt(high, maps[c, j]) + mm_nt(low, maps[c, j]))
                current[j] = new
    for k in range(chips):
        for j in range(per):
            outs[k][j] = incoming[(chip + k) % chips, j]


def run_chains(parts):
    chips = len(parts)
    per = parts[0].shape[0] // 2
    return pl.pallas_call(
        functools.partial(chain_kernel, chips),
        out_shape=[jax.ShapeDtypeStruct((per, B, B), bf16)] * chips,
        in_specs=[VMEM] * chips,
        out_specs=[VMEM] * chips,
        scratch_shapes=[pltpu.VMEM((chips, 2 * per, B, B), bf16), pltpu.VMEM((chips, per, B, B), bf16)],
        compiler_params=pltpu.CompilerParams(vmem_limit_bytes=4 * MIB),
        cost_estimate=pl.CostEstimate(
            flops=chips * per * 4 * B**3, bytes_accessed=chips * per * 6 * B * B, transcendentals=0
        ),
        name="run_chains",
    )(*parts)


def expand_kernel(chips, keep_ref, offset_ref, got_ref, *refs):
    parts = refs[:chips]
    mine_ref, other_ref = refs[chips:]
    section = lax.axis_index("section")
    chip = section // 2
    half = keep_ref.shape[0]
    per = half // chips

    def expand(first):
        for k in range(chips):
            for j in range(per):
                i = (chip - k + chips) % chips * per + j
                mine = (keep_ref[i], offset_ref[i])
                other = (got_ref[i], got_ref[half + i])
                (ma, oa), (mb, ob) = (mine, other) if first else (other, mine)
                b = ob.astype(f32) + mm_nt(parts[k][j], mb)
                high, low = split(b)
                a = oa.astype(f32) + (mm_nt(high, ma) + mm_nt(low, ma))
                mine_ref[i] = a if first else b
                other_ref[i] = (b if first else a).astype(bf16)

    @pl.when(section % 2 == 0)
    def _():
        expand(True)

    @pl.when(section % 2 == 1)
    def _():
        expand(False)


def expand(keep, offsets, got, parts):
    chips = len(parts)
    half = keep.shape[0]
    return pl.pallas_call(
        functools.partial(expand_kernel, chips),
        out_shape=[jax.ShapeDtypeStruct((half, B, B), f32), jax.ShapeDtypeStruct((half, B, B), bf16)],
        in_specs=[VMEM] * (3 + chips),
        out_specs=[VMEM] * 2,
        compiler_params=pltpu.CompilerParams(vmem_limit_bytes=4 * MIB),
        cost_estimate=pl.CostEstimate(flops=half * 6 * B**3, bytes_accessed=half * 16 * B * B, transcendentals=0),
        name="expand",
    )(keep, offsets, got, *parts)


def gather_kernel(mine_ref, got_ref, out_ref, held, sem):
    half = mine_ref.shape[0]
    core = lax.axis_index("section") % 2
    own = pltpu.make_async_copy(mine_ref, out_ref.at[pl.ds(core * half, half)], sem.at[0])
    own.start()
    for i in range(half):
        held[i] = got_ref[i].astype(f32)
    rest = pltpu.make_async_copy(held, out_ref.at[pl.ds((1 - core) * half, half)], sem.at[1])
    rest.start()
    own.wait()
    rest.wait()


def gather_rows(mine, got):
    half = mine.shape[0]
    return pl.pallas_call(
        gather_kernel,
        out_shape=jax.ShapeDtypeStruct((2 * half, B, B), f32),
        in_specs=[VMEM, VMEM],
        out_specs=HBM,
        scratch_shapes=[pltpu.VMEM((half, B, B), f32), pltpu.SemaphoreType.DMA((2,))],
        compiler_params=pltpu.CompilerParams(vmem_limit_bytes=4 * MIB),
        cost_estimate=pl.CostEstimate(flops=0, bytes_accessed=half * 14 * B * B, transcendentals=0),
        name="gather_rows",
    )(mine, got)


def moved(x, along, by):
    pairs = []
    for a in range(SIDE):
        for c in range(SIDE):
            if along == 0:
                pairs.append((a * SIDE + c, (a + by) % SIDE * SIDE + c))
            else:
                pairs.append((a * SIDE + c, a * SIDE + (c + by) % SIDE))
    return lax.ppermute(x, "row", pairs)


def across(x, sections, by):
    return lax.ppermute(x, "section", [(i, (i + 2 * by) % sections) for i in range(sections)])


def partner(x, sections):
    return lax.ppermute(x, "section", [(i, i ^ 1) for i in range(sections)])


def add(a, b):
    return (a.astype(f32) + b.astype(f32)).astype(bf16)


def per_device(
    coupling,
    diag_inverse,
    pivot_inverse,
    cross_left,
    cross_right,
    cross_pivot,
    cross_owner,
    foreign_target_row,
    cross_count,
    local_left,
    local_right,
    local_pivot,
    local_target,
    adjoint_seed,
):
    sections = lax.axis_size("section")
    rows = coupling.shape[0]
    slots = cross_left.shape[0]
    half = rows // 2
    quarter = rows // 4
    me = lax.axis_index("row")

    owner = cross_owner[:, 0]
    dx = (owner // SIDE - me // SIDE) % SIDE
    dz = (owner % SIDE - me % SIDE) % SIDE
    second = foreign_target_row // half
    row = foreign_target_row % half
    a = jnp.where(second == 0, dx, dz)
    b = jnp.where(second == 0, dz, dx)
    upper = row // quarter
    spot = b * quarter + row % quarter
    n = SIDE * quarter
    group = 4 * n
    minus = (a == 3).astype(jnp.int32)
    cell = jnp.where(
        a == 2,
        second * 2 * n + upper * n + spot,
        jnp.where(
            a == 0,
            3 * group + second * 2 * n + upper * n + spot,
            jnp.where(minus == upper, 2 * group, group) + second * 2 * n + minus * n + spot,
        ),
    )
    slot = jnp.arange(slots, dtype=jnp.int32)
    live = slot < cross_count[0]
    word = cell | (cross_pivot << PIVOT_BIT) | (slot << SLOT_BIT)
    word = word | jnp.where(live, jnp.where(cell < group, 1 << FAR_BIT, 1 << NEAR_BIT), 0)
    local_word = local_target | (local_pivot << PIVOT_BIT)

    sums = functools.partial(cross_sums, index=word, table=pivot_inverse, left=cross_left, right=cross_right)
    far = sums(0, [n] * 4, FAR_BIT, live=slots // 4)
    ways = ((0, 1), (0, -1), (1, 1), (1, -1))
    far_in = [moved(x, *w) for x, w in zip(far, ways)]
    near = sums(group, [n] * 8 + [2 * n] * 2, NEAR_BIT, live=slots * 3 // 4)
    free_in = [moved(x, *w) for x, w in zip(near[:4], ways)]
    joined = [add(x, y) for x, y in zip(near[4:8], far_in)]
    joined_in = [moved(x, *w) for x, w in zip(joined, ways)]

    base, offsets = local_and_offset(
        local_word, pivot_inverse, coupling, local_left, local_right, diag_inverse, adjoint_seed, joined
    )

    arrivals = []
    for s in range(2):
        fp, fm = free_in[2 * s : 2 * s + 2]
        jp, jm = joined_in[2 * s : 2 * s + 2]
        arrivals += [jp, fm, fp, jm]
    tot_x, tot_z = first_totals(near[8], near[9], arrivals, [base])
    parts_x = [tot_x[0]] + [moved(tot_x[k], 1, k) for k in (2, 1, 3)]
    parts_z = [tot_z[0]] + [moved(tot_z[k], 0, k) for k in (2, 1, 3)]
    updated, keep, give = coupling_and_step(base, diag_inverse, offsets, parts_x, parts_z)
    chips = sections // 2
    got = partner(give, sections)
    maps = compose(chips, keep, offsets, got)
    maps = [maps[0]] + [across(maps[k], sections, k) for k in range(1, chips)]
    incoming = run_chains(maps)
    incoming = [incoming[0]] + [across(incoming[k], sections, k) for k in range(1, chips)]
    mine, other = expand(keep, offsets, got, incoming)
    adjoint = gather_rows(mine, partner(other, sections))
    return (updated, adjoint)


def solution(mesh):
    spread = ("section", "row")
    block = P(spread, None, None)
    line = P(spread)
    return jax.shard_map(
        per_device,
        mesh=mesh,
        in_specs=(
            block,
            block,
            block,
            block,
            block,
            line,
            P(spread, None),
            line,
            line,
            block,
            block,
            line,
            line,
            block,
        ),
        out_specs=(block, block),
        check_vma=False,
    )
```

```python
import functools

import jax
import jax.numpy as jnp
from jax import lax
from jax.experimental import pallas as pl
from jax.experimental.pallas import tpu as pltpu
from jax.sharding import PartitionSpec as P

B = 128
SIDE = 4
UNROLL = 16
CHUNKS = 8
CELL_MASK, PIVOT_BIT, FAR_BIT, NEAR_BIT, SLOT_BIT = 511, 9, 16, 17, 20
SECOND = ((0, 3), (1, 2), (0, 2), (1, 1), (0, 1), (1, 3))
MIB = 1 << 20

ANY = pl.BlockSpec(memory_space=pl.ANY)
HBM = pl.BlockSpec(memory_space=pltpu.HBM)
VMEM = pl.BlockSpec(memory_space=pltpu.VMEM)
SMEM = pl.BlockSpec(memory_space=pltpu.SMEM)

bf16 = jnp.bfloat16
f32 = jnp.float32


def mm(a, b):
    return jnp.dot(a, b, preferred_element_type=f32)


def mm_nt(a, b):
    return lax.dot_general(a, b, (((1,), (1,)), ((), ())), preferred_element_type=f32)


def split(x):
    high = x.astype(bf16)
    return high, (x - high.astype(f32)).astype(bf16)


def stay(x):
    return pltpu.with_memory_space_constraint(x, pltpu.HBM)


def bulk(left_ref, right_ref, left, right, lsem, rsem):
    per = left.shape[0] // CHUNKS
    pairs = []
    for k in range(CHUNKS):
        part = pl.ds(k * per, per)
        pair = (
            pltpu.make_async_copy(left_ref.at[part], left.at[part], lsem.at[k]),
            pltpu.make_async_copy(right_ref.at[part], right.at[part], rsem.at[k]),
        )
        for c in pair:
            c.start()
        pairs.append(pair)
    return pairs


def cross_kernel(first, sizes, flag, unroll, index_ref, table_ref, left_ref, right_ref, *refs):
    outs = refs[-8 - len(sizes) : -8]
    listed, left, right, total, table, lsem, rsem, tsem = refs[-8:]
    cells = sum(sizes)
    slots = left.shape[0]
    table_copy = pltpu.make_async_copy(table_ref, table, tsem)
    table_copy.start()
    bulk(left_ref, right_ref, left, right, lsem, rsem)

    def note(i, n):
        word = index_ref[i]
        listed[n] = word
        return n + ((word >> flag) & 1)

    count = lax.fori_loop(0, slots, note, 0, unroll=32)
    for u in range(unroll):
        listed[count + u] = first + cells

    def clear(c, _):
        total[c] = jnp.zeros((B, B), bf16)
        return 0

    lax.fori_loop(0, cells + 1, clear, 0, unroll=8)
    table_copy.wait()
    per = slots // CHUNKS

    def landed(k, _):
        part = pl.ds(k * per, per)
        pltpu.make_async_copy(left_ref.at[part], left.at[part], lsem.at[k]).wait()
        pltpu.make_async_copy(right_ref.at[part], right.at[part], rsem.at[k]).wait()
        return 0

    def work(r, ready):
        words = [listed[r * unroll + u] for u in range(unroll)]
        last = listed[jnp.minimum(r * unroll + unroll, count) - 1] >> SLOT_BIT
        lax.fori_loop(ready, last // per + 1, landed, 0)
        scaled = [mm(left[w >> SLOT_BIT], table[(w >> PIVOT_BIT) & 3]).astype(bf16) for w in words]
        updates = [mm(x, right[w >> SLOT_BIT]) for x, w in zip(scaled, words)]
        for w, u in zip(words, updates):
            c = (w & CELL_MASK) - first
            total[c] = (total[c].astype(f32) + u).astype(bf16)
        return last // per + 1

    ready = lax.fori_loop(0, (count + unroll - 1) // unroll, work, 0)
    lax.fori_loop(ready, CHUNKS, landed, 0)

    start = 0
    for out, size in zip(outs, sizes):

        def give(c, _, out=out, start=start):
            out[c] = total[start + c]
            return 0

        lax.fori_loop(0, size, give, 0, unroll=8)
        start += size


def cross_sums(first, sizes, flag, unroll, index, table, left, right, live):
    cells = sum(sizes)
    slots = left.shape[0]
    return pl.pallas_call(
        functools.partial(cross_kernel, first, sizes, flag, unroll),
        out_shape=[jax.ShapeDtypeStruct((n, B, B), bf16) for n in sizes],
        in_specs=[SMEM, HBM, HBM, HBM],
        out_specs=[VMEM] * len(sizes),
        scratch_shapes=[
            pltpu.SMEM((slots + unroll,), jnp.int32),
            pltpu.VMEM((slots, B, B), bf16),
            pltpu.VMEM((slots, B, B), bf16),
            pltpu.VMEM((cells + 1, B, B), bf16),
            pltpu.VMEM(table.shape, bf16),
            pltpu.SemaphoreType.DMA((CHUNKS,)),
            pltpu.SemaphoreType.DMA((CHUNKS,)),
            pltpu.SemaphoreType.DMA,
        ],
        compiler_params=pltpu.CompilerParams(vmem_limit_bytes=9 * MIB + cells * 4 * B * B),
        cost_estimate=pl.CostEstimate(
            flops=live * 4 * B**3, bytes_accessed=slots * 4 * B * B + cells * 2 * B * B, transcendentals=0
        ),
        name="cross_sums",
    )(index, stay(table), stay(left), stay(right))


def local_kernel(index_ref, table_ref, coupling_ref, left_ref, right_ref, diag_ref, seed_ref, *refs):
    base_ref, keep_ref, give_ref, held, left, right, table, lsem, rsem, tsem = refs[-10:]
    slots = left.shape[0]
    rows = coupling_ref.shape[0]
    half = rows // 2
    core = lax.axis_index("section") % 2
    table_copy = pltpu.make_async_copy(table_ref, table, tsem)
    table_copy.start()
    pairs = bulk(left_ref, right_ref, left, right, lsem, rsem)
    for r in range(rows):
        base_ref[r] = coupling_ref[r].astype(f32)

    def offset(r, _):
        dh, dl = split(diag_ref[r])
        sh, sl = split(seed_ref[r])
        o = mm_nt(sh, dh) + (mm_nt(sh, dl) + mm_nt(sl, dh))
        held[(r + core * half) % rows] = o.astype(bf16)
        return 0

    lax.fori_loop(0, rows, offset, 0, unroll=4)
    for i in range(half):
        keep_ref[i] = held[i]
        give_ref[i] = held[half + i]
    table_copy.wait()
    per = slots // CHUNKS
    for k, pair in enumerate(pairs):
        for c in pair:
            c.wait()

        def work(i, _, k=k):
            at = [k * per + i * UNROLL + u for u in range(UNROLL)]
            words = [index_ref[j] for j in at]
            scaled = [mm(left[j], table[(w >> PIVOT_BIT) & 3]).astype(bf16) for j, w in zip(at, words)]
            updates = [mm(x, right[j]).astype(bf16).astype(f32) for x, j in zip(scaled, at)]
            for w, u in zip(words, updates):
                t = w & CELL_MASK
                base_ref[t] = base_ref[t] - u
            return 0

        lax.fori_loop(0, per // UNROLL, work, 0)


def local_and_offset(index, table, coupling, left, right, diag, seed, order):
    slots = left.shape[0]
    rows = coupling.shape[0]
    return pl.pallas_call(
        local_kernel,
        out_shape=[jax.ShapeDtypeStruct((rows, B, B), f32)] + [jax.ShapeDtypeStruct((rows // 2, B, B), bf16)] * 2,
        in_specs=[SMEM, HBM, VMEM, HBM, HBM, VMEM, VMEM] + [ANY] * len(order),
        out_specs=[VMEM] * 3,
        scratch_shapes=[
            pltpu.VMEM((rows, B, B), bf16),
            pltpu.VMEM((slots, B, B), bf16),
            pltpu.VMEM((slots, B, B), bf16),
            pltpu.VMEM(table.shape, bf16),
            pltpu.SemaphoreType.DMA((CHUNKS,)),
            pltpu.SemaphoreType.DMA((CHUNKS,)),
            pltpu.SemaphoreType.DMA,
        ],
        compiler_params=pltpu.CompilerParams(vmem_limit_bytes=16 * MIB),
        cost_estimate=pl.CostEstimate(
            flops=slots * 4 * B**3, bytes_accessed=slots * 4 * B * B + rows * 16 * B * B, transcendentals=0
        ),
        name="local_and_offset",
    )(index, stay(table), coupling, stay(left), stay(right), diag, seed, *order)


def first_totals_kernel(own_x, own_z, *refs):
    outs = refs[-2 * SIDE :]
    q = own_x.shape[0] // (2 * SIDE)
    for s, own in enumerate((own_x, own_z)):
        plus, minus = refs[2 * s : 2 * s + 2]
        for half in range(2):
            for b in range(SIDE):
                t = own[pl.ds((half * SIDE + b) * q, q)].astype(f32)
                t = t + plus[pl.ds(((1 - half) * SIDE + b) * q, q)].astype(f32)
                t = t + minus[pl.ds((half * SIDE + b) * q, q)].astype(f32)
                outs[s * SIDE + b][pl.ds(half * q, q)] = t.astype(bf16)


def first_totals(own_x, own_z, arrivals, order):
    half = own_x.shape[0] // SIDE
    outs = pl.pallas_call(
        first_totals_kernel,
        out_shape=[jax.ShapeDtypeStruct((half, B, B), bf16)] * (2 * SIDE),
        in_specs=[VMEM] * 6 + [ANY] * len(order),
        out_specs=[VMEM] * (2 * SIDE),
        compiler_params=pltpu.CompilerParams(vmem_limit_bytes=9 * MIB),
        cost_estimate=pl.CostEstimate(flops=0, bytes_accessed=256 * 2 * B * B, transcendentals=0),
        name="first_totals",
    )(own_x, own_z, *arrivals, *order)
    return outs[:SIDE], outs[SIDE:]


def coupling_kernel(base_ref, diag_ref, *refs):
    new_ref, keep_ref, give_ref, held = refs[-4:]
    rows = base_ref.shape[0]
    half = rows // 2
    core = lax.axis_index("section") % 2
    for s in range(2):
        parts = [refs[s]] + [refs[2 + i] for i, (t, _) in enumerate(SECOND) if t == s]

        def finish(i, _, s=s, parts=parts):
            r = s * half + i
            t = base_ref[r]
            for p in parts:
                t = t - p[i].astype(f32)
            new_ref[r] = t
            th, tl = split(t)
            dh, dl = split(diag_ref[r])
            held[(r + core * half) % rows] = -(mm(dh, th) + (mm(dh, tl) + mm(dl, th))).astype(bf16)
            return 0

        lax.fori_loop(0, half, finish, 0, unroll=4)
    for i in range(half):
        keep_ref[i] = held[i]
        give_ref[i] = held[half + i]


def coupling_and_step(base, diag, own, parts):
    rows = base.shape[0]
    half = rows // 2
    return pl.pallas_call(
        coupling_kernel,
        out_shape=[
            jax.ShapeDtypeStruct((rows, B, B), f32),
            jax.ShapeDtypeStruct((half, B, B), bf16),
            jax.ShapeDtypeStruct((half, B, B), bf16),
        ],
        in_specs=[VMEM] * 10,
        out_specs=[VMEM] * 3,
        scratch_shapes=[pltpu.VMEM((rows, B, B), bf16)],
        compiler_params=pltpu.CompilerParams(vmem_limit_bytes=9 * MIB),
        cost_estimate=pl.CostEstimate(flops=rows * 6 * B**3, bytes_accessed=rows * 22 * B * B, transcendentals=0),
        name="coupling_and_step",
    )(base, diag, *own, *parts)


def compose_kernel(chips, keep_ref, offset_ref, got_ref, got_offset_ref, *outs):
    section = lax.axis_index("section")
    chip = section // 2
    half = keep_ref.shape[0]
    per = half // chips

    def compose(first):
        for k in range(chips):
            for j in range(per):
                i = (chip + k) % chips * per + j
                mine = (keep_ref[i], offset_ref[i])
                other = (got_ref[i], got_offset_ref[i])
                (ma, oa), (mb, ob) = (mine, other) if first else (other, mine)
                outs[k][j] = mm(ma, mb).astype(bf16)
                outs[k][per + j] = (oa.astype(f32) + mm_nt(ob, ma)).astype(bf16)

    @pl.when(section % 2 == 0)
    def _():
        compose(True)

    @pl.when(section % 2 == 1)
    def _():
        compose(False)


def compose(chips, keep, offsets, got, got_offsets):
    half = keep.shape[0]
    return pl.pallas_call(
        functools.partial(compose_kernel, chips),
        out_shape=[jax.ShapeDtypeStruct((2 * half // chips, B, B), bf16)] * chips,
        in_specs=[VMEM] * 4,
        out_specs=[VMEM] * chips,
        compiler_params=pltpu.CompilerParams(vmem_limit_bytes=4 * MIB),
        cost_estimate=pl.CostEstimate(flops=half * 4 * B**3, bytes_accessed=half * 12 * B * B, transcendentals=0),
        name="compose",
    )(keep, offsets, got, got_offsets)


def chain_kernel(chips, *refs):
    parts = refs[:chips]
    outs = refs[chips : 2 * chips]
    maps, incoming = refs[2 * chips :]
    chip = lax.axis_index("section") // 2
    per = outs[0].shape[0]
    for k in range(chips):
        for i in range(2 * per):
            maps[(chip - k + chips) % chips, i] = parts[k][i]
    current = [jnp.zeros((B, B), f32)] * per
    for c in range(chips - 1, -1, -1):
        for j in range(per):
            incoming[c, j] = current[j].astype(bf16)
            if c > 0:
                new = maps[c, per + j].astype(f32)
                if c < chips - 1:
                    high, low = split(current[j])
                    new = new + (mm_nt(high, maps[c, j]) + mm_nt(low, maps[c, j]))
                current[j] = new
    for k in range(chips):
        for j in range(per):
            outs[k][j] = incoming[(chip + k) % chips, j]


def run_chains(parts):
    chips = len(parts)
    per = parts[0].shape[0] // 2
    return pl.pallas_call(
        functools.partial(chain_kernel, chips),
        out_shape=[jax.ShapeDtypeStruct((per, B, B), bf16)] * chips,
        in_specs=[VMEM] * chips,
        out_specs=[VMEM] * chips,
        scratch_shapes=[pltpu.VMEM((chips, 2 * per, B, B), bf16), pltpu.VMEM((chips, per, B, B), bf16)],
        compiler_params=pltpu.CompilerParams(vmem_limit_bytes=4 * MIB),
        cost_estimate=pl.CostEstimate(
            flops=chips * per * 4 * B**3, bytes_accessed=chips * per * 6 * B * B, transcendentals=0
        ),
        name="run_chains",
    )(*parts)


def expand_kernel(chips, keep_ref, offset_ref, got_ref, got_offset_ref, *refs):
    parts = refs[:chips]
    mine_ref, other_ref = refs[chips:]
    section = lax.axis_index("section")
    chip = section // 2
    half = keep_ref.shape[0]
    per = half // chips

    def expand(first):
        for k in range(chips):
            for j in range(per):
                i = (chip - k + chips) % chips * per + j
                mine = (keep_ref[i], offset_ref[i])
                other = (got_ref[i], got_offset_ref[i])
                (ma, oa), (mb, ob) = (mine, other) if first else (other, mine)
                b = ob.astype(f32) + mm_nt(parts[k][j], mb)
                high, low = split(b)
                a = oa.astype(f32) + (mm_nt(high, ma) + mm_nt(low, ma))
                mine_ref[i] = a if first else b
                other_ref[i] = (b if first else a).astype(bf16)

    @pl.when(section % 2 == 0)
    def _():
        expand(True)

    @pl.when(section % 2 == 1)
    def _():
        expand(False)


def expand(keep, offsets, got, got_offsets, parts):
    chips = len(parts)
    half = keep.shape[0]
    return pl.pallas_call(
        functools.partial(expand_kernel, chips),
        out_shape=[jax.ShapeDtypeStruct((half, B, B), f32), jax.ShapeDtypeStruct((half, B, B), bf16)],
        in_specs=[VMEM] * (4 + chips),
        out_specs=[VMEM] * 2,
        compiler_params=pltpu.CompilerParams(vmem_limit_bytes=4 * MIB),
        cost_estimate=pl.CostEstimate(flops=half * 6 * B**3, bytes_accessed=half * 16 * B * B, transcendentals=0),
        name="expand",
    )(keep, offsets, got, got_offsets, *parts)


def gather_kernel(mine_ref, got_ref, out_ref, held, sem):
    half = mine_ref.shape[0]
    core = lax.axis_index("section") % 2
    own = pltpu.make_async_copy(mine_ref, out_ref.at[pl.ds(core * half, half)], sem.at[0])
    own.start()
    for i in range(half):
        held[i] = got_ref[i].astype(f32)
    rest = pltpu.make_async_copy(held, out_ref.at[pl.ds((1 - core) * half, half)], sem.at[1])
    rest.start()
    own.wait()
    rest.wait()


def gather_rows(mine, got):
    half = mine.shape[0]
    return pl.pallas_call(
        gather_kernel,
        out_shape=jax.ShapeDtypeStruct((2 * half, B, B), f32),
        in_specs=[VMEM, VMEM],
        out_specs=HBM,
        scratch_shapes=[pltpu.VMEM((half, B, B), f32), pltpu.SemaphoreType.DMA((2,))],
        compiler_params=pltpu.CompilerParams(vmem_limit_bytes=4 * MIB),
        cost_estimate=pl.CostEstimate(flops=0, bytes_accessed=half * 14 * B * B, transcendentals=0),
        name="gather_rows",
    )(mine, got)


def moved(x, along, by):
    pairs = []
    for a in range(SIDE):
        for c in range(SIDE):
            if along == 0:
                pairs.append((a * SIDE + c, (a + by) % SIDE * SIDE + c))
            else:
                pairs.append((a * SIDE + c, a * SIDE + (c + by) % SIDE))
    return lax.ppermute(x, "row", pairs)


def maps_across(x, sections, by):
    return lax.ppermute(x, "section", [(i, (i + 2 * by) % sections) for i in range(2, sections)])


def incoming_across(x, sections, by):
    pairs = [(i, (i + 2 * by) % sections) for i in range(sections)]
    return lax.ppermute(x, "section", [p for p in pairs if p[1] < sections - 2])


def partner(x, sections):
    return lax.ppermute(x, "section", [(i, i ^ 1) for i in range(sections)])


def add(a, b):
    return (a.astype(f32) + b.astype(f32)).astype(bf16)


def per_device(
    coupling,
    diag_inverse,
    pivot_inverse,
    cross_left,
    cross_right,
    cross_pivot,
    cross_owner,
    foreign_target_row,
    cross_count,
    local_left,
    local_right,
    local_pivot,
    local_target,
    adjoint_seed,
):
    sections = lax.axis_size("section")
    rows = coupling.shape[0]
    slots = cross_left.shape[0]
    half = rows // 2
    quarter = rows // 4
    me = lax.axis_index("row")

    owner = cross_owner[:, 0]
    dx = (owner // SIDE - me // SIDE) % SIDE
    dz = (owner % SIDE - me % SIDE) % SIDE
    second = foreign_target_row // half
    row = foreign_target_row % half
    a = jnp.where(second == 0, dx, dz)
    b = jnp.where(second == 0, dz, dx)
    upper = row // quarter
    spot = b * quarter + row % quarter
    n = SIDE * quarter
    group = 4 * n
    minus = (a == 3).astype(jnp.int32)
    cell = jnp.where(
        a == 2,
        second * 2 * n + upper * n + spot,
        jnp.where(
            a == 0,
            3 * group + second * 2 * n + upper * n + spot,
            group + (second * 2 + minus) * 2 * n + jnp.where(minus == upper, n, 0) + spot,
        ),
    )
    slot = jnp.arange(slots, dtype=jnp.int32)
    live = slot < cross_count[0]
    word = cell | (cross_pivot << PIVOT_BIT) | (slot << SLOT_BIT)
    word = word | jnp.where(live, jnp.where(cell < group, 1 << FAR_BIT, 1 << NEAR_BIT), 0)
    local_word = local_target | (local_pivot << PIVOT_BIT)

    sums = functools.partial(cross_sums, index=word, table=pivot_inverse, left=cross_left, right=cross_right)
    far = sums(0, [n] * 4, FAR_BIT, 8, live=slots // 4)
    ways = ((0, 1), (0, -1), (1, 1), (1, -1))
    far_in = [moved(x, *w) for x, w in zip(far, ways)]
    near = sums(group, [2 * n] * 6, NEAR_BIT, UNROLL, live=slots * 3 // 4)
    joined = [lax.dynamic_update_slice_in_dim(x, add(x[n:], y), n, 0) for x, y in zip(near, far_in)]
    arrivals = [moved(x, *w) for x, w in zip(joined, ways)]

    base, offsets, give_offsets = local_and_offset(
        local_word, pivot_inverse, coupling, local_left, local_right, diag_inverse, adjoint_seed, joined
    )
    got_offsets = partner(give_offsets, sections)

    tot_x, tot_z = first_totals(near[4], near[5], arrivals, [base, got_offsets])
    totals = (tot_x, tot_z)
    parts = [moved(totals[s][k], 1 - s, k) for s, k in SECOND]
    updated, keep, give = coupling_and_step(base, diag_inverse, (tot_x[0], tot_z[0]), parts)
    chips = sections // 2
    got = partner(give, sections)
    maps = compose(chips, keep, offsets, got, got_offsets)
    maps = [maps[0]] + [maps_across(maps[k], sections, k) for k in range(1, chips)]
    incoming = run_chains(maps)
    incoming = [incoming[0]] + [incoming_across(incoming[k], sections, k) for k in range(1, chips)]
    mine, other = expand(keep, offsets, got, got_offsets, incoming)
    adjoint = gather_rows(mine, partner(other, sections))
    return (updated, adjoint)


def solution(mesh):
    spread = ("section", "row")
    block = P(spread, None, None)
    line = P(spread)
    return jax.shard_map(
        per_device,
        mesh=mesh,
        in_specs=(
            block,
            block,
            block,
            block,
            block,
            line,
            P(spread, None),
            line,
            line,
            block,
            block,
            line,
            line,
            block,
        ),
        out_specs=(block, block),
        check_vma=False,
    )
```

```python
import functools

import jax
import jax.numpy as jnp
from jax import lax
from jax.experimental import pallas as pl
from jax.experimental.pallas import tpu as pltpu
from jax.sharding import PartitionSpec as P

B = 128
SIDE = 4
UNROLL = 16
CHUNKS = 8
CELL_MASK, PIVOT_BIT, FAR_BIT, NEAR_BIT, SLOT_BIT = 511, 9, 16, 17, 20
MIB = 1 << 20

ANY = pl.BlockSpec(memory_space=pl.ANY)
HBM = pl.BlockSpec(memory_space=pltpu.HBM)
VMEM = pl.BlockSpec(memory_space=pltpu.VMEM)
SMEM = pl.BlockSpec(memory_space=pltpu.SMEM)

bf16 = jnp.bfloat16
f32 = jnp.float32


def mm(a, b):
    return jnp.dot(a, b, preferred_element_type=f32)


def mm_nt(a, b):
    return lax.dot_general(a, b, (((1,), (1,)), ((), ())), preferred_element_type=f32)


def split(x):
    high = x.astype(bf16)
    return high, (x - high.astype(f32)).astype(bf16)


def stay(x):
    return pltpu.with_memory_space_constraint(x, pltpu.HBM)


def bulk(left_ref, right_ref, left, right, lsem, rsem):
    per = left.shape[0] // CHUNKS
    pairs = []
    for k in range(CHUNKS):
        part = pl.ds(k * per, per)
        pair = (
            pltpu.make_async_copy(left_ref.at[part], left.at[part], lsem.at[k]),
            pltpu.make_async_copy(right_ref.at[part], right.at[part], rsem.at[k]),
        )
        for c in pair:
            c.start()
        pairs.append(pair)
    return pairs


def sum_cells(first, flag, index_ref, listed, total, outs, ready, left, right, table):
    slots = left.shape[0]
    cells = total.shape[0] - 1

    def note(i, n):
        word = index_ref[i]
        listed[n] = word
        return n + ((word >> flag) & 1)

    count = lax.fori_loop(0, slots, note, 0, unroll=32)
    for u in range(UNROLL):
        listed[count + u] = first + cells

    def clear(c, _):
        total[c] = jnp.zeros((B, B), bf16)
        return 0

    lax.fori_loop(0, cells + 1, clear, 0, unroll=8)
    ready()

    def work(r, _):
        words = [listed[r * UNROLL + u] for u in range(UNROLL)]
        scaled = [mm(left[w >> SLOT_BIT], table[(w >> PIVOT_BIT) & 3]).astype(bf16) for w in words]
        updates = [mm(x, right[w >> SLOT_BIT]) for x, w in zip(scaled, words)]
        for w, u in zip(words, updates):
            c = (w & CELL_MASK) - first
            total[c] = (total[c].astype(f32) + u).astype(bf16)
        return 0

    lax.fori_loop(0, (count + UNROLL - 1) // UNROLL, work, 0)
    start = 0
    for out in outs:

        def give(c, _, out=out, start=start):
            out[c] = total[start + c]
            return 0

        lax.fori_loop(0, out.shape[0], give, 0, unroll=8)
        start += out.shape[0]


def far_kernel(first, index_ref, table_ref, left_ref, right_ref, *refs):
    *outs, left, right, table, listed, total, lsem, rsem, tsem = refs
    table_copy = pltpu.make_async_copy(table_ref, table, tsem)
    table_copy.start()
    pairs = bulk(left_ref, right_ref, left, right, lsem, rsem)

    def ready():
        table_copy.wait()
        for pair in pairs:
            for c in pair:
                c.wait()

    sum_cells(first, FAR_BIT, index_ref, listed, total, outs, ready, left, right, table)


def near_kernel(first, index_ref, table, left, right, *refs):
    *outs, listed, total = refs
    sum_cells(first, NEAR_BIT, index_ref, listed, total, outs, lambda: None, left, right, table)


def cell_shapes(sizes):
    return [jax.ShapeDtypeStruct((n, B, B), bf16) for n in sizes]


def far_sums(first, sizes, index, table, left, right):
    cells = sum(sizes)
    slots = left.shape[0]
    outs = pl.pallas_call(
        functools.partial(far_kernel, first),
        out_shape=cell_shapes(sizes) + [jax.ShapeDtypeStruct(x.shape, bf16) for x in (left, right, table)],
        in_specs=[SMEM, HBM, HBM, HBM],
        out_specs=[VMEM] * (len(sizes) + 3),
        scratch_shapes=[
            pltpu.SMEM((slots + UNROLL,), jnp.int32),
            pltpu.VMEM((cells + 1, B, B), bf16),
            pltpu.SemaphoreType.DMA((CHUNKS,)),
            pltpu.SemaphoreType.DMA((CHUNKS,)),
            pltpu.SemaphoreType.DMA,
        ],
        compiler_params=pltpu.CompilerParams(vmem_limit_bytes=9 * MIB + cells * 4 * B * B),
        cost_estimate=pl.CostEstimate(
            flops=slots * B**3, bytes_accessed=slots * 8 * B * B + cells * 2 * B * B, transcendentals=0
        ),
        name="far_sums",
    )(index, stay(table), stay(left), stay(right))
    return outs[: len(sizes)], outs[len(sizes) :]


def near_sums(first, sizes, index, held):
    left, right, table = held
    cells = sum(sizes)
    slots = left.shape[0]
    return pl.pallas_call(
        functools.partial(near_kernel, first),
        out_shape=cell_shapes(sizes),
        in_specs=[SMEM, VMEM, VMEM, VMEM],
        out_specs=[VMEM] * len(sizes),
        scratch_shapes=[pltpu.SMEM((slots + UNROLL,), jnp.int32), pltpu.VMEM((cells + 1, B, B), bf16)],
        compiler_params=pltpu.CompilerParams(vmem_limit_bytes=9 * MIB + cells * 4 * B * B),
        cost_estimate=pl.CostEstimate(
            flops=slots * 3 * B**3, bytes_accessed=slots * 4 * B * B + cells * 2 * B * B, transcendentals=0
        ),
        name="near_sums",
    )(index, table, left, right)


def local_kernel(index_ref, table_ref, coupling_ref, left_ref, right_ref, diag_ref, seed_ref, *refs):
    base_ref, keep_ref, give_ref, held, left, right, table, lsem, rsem, tsem = refs[-10:]
    slots = left.shape[0]
    rows = coupling_ref.shape[0]
    half = rows // 2
    core = lax.axis_index("section") % 2
    table_copy = pltpu.make_async_copy(table_ref, table, tsem)
    table_copy.start()
    pairs = bulk(left_ref, right_ref, left, right, lsem, rsem)
    for r in range(rows):
        base_ref[r] = coupling_ref[r].astype(f32)

    def offset(r, _):
        dh, dl = split(diag_ref[r])
        sh, sl = split(seed_ref[r])
        o = mm_nt(sh, dh) + (mm_nt(sh, dl) + mm_nt(sl, dh))
        held[(r + core * half) % rows] = o.astype(bf16)
        return 0

    lax.fori_loop(0, rows, offset, 0, unroll=4)
    for i in range(half):
        keep_ref[i] = held[i]
        give_ref[i] = held[half + i]
    table_copy.wait()
    per = slots // CHUNKS
    for k, pair in enumerate(pairs):
        for c in pair:
            c.wait()

        def work(i, _, k=k):
            at = [k * per + i * UNROLL + u for u in range(UNROLL)]
            words = [index_ref[j] for j in at]
            scaled = [mm(left[j], table[(w >> PIVOT_BIT) & 3]).astype(bf16) for j, w in zip(at, words)]
            updates = [mm(x, right[j]).astype(bf16).astype(f32) for x, j in zip(scaled, at)]
            for w, u in zip(words, updates):
                t = w & CELL_MASK
                base_ref[t] = base_ref[t] - u
            return 0

        lax.fori_loop(0, per // UNROLL, work, 0)


def local_and_offset(index, table, coupling, left, right, diag, seed, order):
    slots = left.shape[0]
    rows = coupling.shape[0]
    return pl.pallas_call(
        local_kernel,
        out_shape=[jax.ShapeDtypeStruct((rows, B, B), f32)] + [jax.ShapeDtypeStruct((rows // 2, B, B), bf16)] * 2,
        in_specs=[SMEM, HBM, VMEM, HBM, HBM, VMEM, VMEM] + [ANY] * len(order),
        out_specs=[VMEM] * 3,
        scratch_shapes=[
            pltpu.VMEM((rows, B, B), bf16),
            pltpu.VMEM((slots, B, B), bf16),
            pltpu.VMEM((slots, B, B), bf16),
            pltpu.VMEM(table.shape, bf16),
            pltpu.SemaphoreType.DMA((CHUNKS,)),
            pltpu.SemaphoreType.DMA((CHUNKS,)),
            pltpu.SemaphoreType.DMA,
        ],
        compiler_params=pltpu.CompilerParams(vmem_limit_bytes=16 * MIB),
        cost_estimate=pl.CostEstimate(
            flops=slots * 4 * B**3, bytes_accessed=slots * 4 * B * B + rows * 16 * B * B, transcendentals=0
        ),
        name="local_and_offset",
    )(index, stay(table), coupling, stay(left), stay(right), diag, seed, *order)


def first_totals_kernel(own, *refs):
    arrivals = (refs[:2], refs[2:4])
    outs = refs[-SIDE:]
    h = own.shape[0] // (2 * SIDE)
    for half in range(2):
        for b in range(SIDE):
            t = own[pl.ds((half * SIDE + b) * h, h)].astype(f32)
            for a in arrivals[half]:
                t = t + a[pl.ds(b * h, h)].astype(f32)
            outs[b][pl.ds(half * h, h)] = t.astype(bf16)


def first_totals(own, arrivals, order):
    rows = own.shape[0] // SIDE
    return pl.pallas_call(
        first_totals_kernel,
        out_shape=[jax.ShapeDtypeStruct((rows, B, B), bf16)] * SIDE,
        in_specs=[VMEM] * 5 + [ANY] * len(order),
        out_specs=[VMEM] * SIDE,
        compiler_params=pltpu.CompilerParams(vmem_limit_bytes=9 * MIB),
        cost_estimate=pl.CostEstimate(flops=0, bytes_accessed=256 * 2 * B * B, transcendentals=0),
        name="first_totals",
    )(own, *arrivals, *order)


def coupling_kernel(base_ref, diag_ref, *refs):
    new_ref, keep_ref, give_ref, held = refs[-4:]
    rows = base_ref.shape[0]
    half = rows // 2
    core = lax.axis_index("section") % 2
    parts = refs[:SIDE]

    def finish(r, _):
        t = base_ref[r]
        for p in parts:
            t = t - p[r].astype(f32)
        new_ref[r] = t
        th, tl = split(t)
        dh, dl = split(diag_ref[r])
        held[(r + core * half) % rows] = -(mm(dh, th) + (mm(dh, tl) + mm(dl, th))).astype(bf16)
        return 0

    lax.fori_loop(0, rows, finish, 0, unroll=4)
    for i in range(half):
        keep_ref[i] = held[i]
        give_ref[i] = held[half + i]


def coupling_and_step(base, diag, parts):
    rows = base.shape[0]
    half = rows // 2
    return pl.pallas_call(
        coupling_kernel,
        out_shape=[
            jax.ShapeDtypeStruct((rows, B, B), f32),
            jax.ShapeDtypeStruct((half, B, B), bf16),
            jax.ShapeDtypeStruct((half, B, B), bf16),
        ],
        in_specs=[VMEM] * (2 + SIDE),
        out_specs=[VMEM] * 3,
        scratch_shapes=[pltpu.VMEM((rows, B, B), bf16)],
        compiler_params=pltpu.CompilerParams(vmem_limit_bytes=9 * MIB),
        cost_estimate=pl.CostEstimate(flops=rows * 6 * B**3, bytes_accessed=rows * 22 * B * B, transcendentals=0),
        name="coupling_and_step",
    )(base, diag, *parts)


def compose_kernel(chips, keep_ref, offset_ref, got_ref, got_offset_ref, *outs):
    section = lax.axis_index("section")
    chip = section // 2
    half = keep_ref.shape[0]
    per = half // chips

    def compose(first):
        for k in range(chips):
            for j in range(per):
                i = (chip + k) % chips * per + j
                mine = (keep_ref[i], offset_ref[i])
                other = (got_ref[i], got_offset_ref[i])
                (ma, oa), (mb, ob) = (mine, other) if first else (other, mine)
                outs[k][j] = mm(ma, mb).astype(bf16)
                outs[k][per + j] = (oa.astype(f32) + mm_nt(ob, ma)).astype(bf16)

    @pl.when(section % 2 == 0)
    def _():
        compose(True)

    @pl.when(section % 2 == 1)
    def _():
        compose(False)


def compose(chips, keep, offsets, got, got_offsets):
    half = keep.shape[0]
    return pl.pallas_call(
        functools.partial(compose_kernel, chips),
        out_shape=[jax.ShapeDtypeStruct((2 * half // chips, B, B), bf16)] * chips,
        in_specs=[VMEM] * 4,
        out_specs=[VMEM] * chips,
        compiler_params=pltpu.CompilerParams(vmem_limit_bytes=4 * MIB),
        cost_estimate=pl.CostEstimate(flops=half * 4 * B**3, bytes_accessed=half * 12 * B * B, transcendentals=0),
        name="compose",
    )(keep, offsets, got, got_offsets)


def chain_kernel(chips, *refs):
    parts = refs[:chips]
    outs = refs[chips : 2 * chips]
    maps, incoming = refs[2 * chips :]
    chip = lax.axis_index("section") // 2
    per = outs[0].shape[0]
    for k in range(chips):
        for i in range(2 * per):
            maps[(chip - k + chips) % chips, i] = parts[k][i]
    current = [jnp.zeros((B, B), f32)] * per
    for c in range(chips - 1, -1, -1):
        for j in range(per):
            incoming[c, j] = current[j].astype(bf16)
            if c > 0:
                new = maps[c, per + j].astype(f32)
                if c < chips - 1:
                    high, low = split(current[j])
                    new = new + (mm_nt(high, maps[c, j]) + mm_nt(low, maps[c, j]))
                current[j] = new
    for k in range(chips):
        for j in range(per):
            outs[k][j] = incoming[(chip + k) % chips, j]


def run_chains(parts):
    chips = len(parts)
    per = parts[0].shape[0] // 2
    return pl.pallas_call(
        functools.partial(chain_kernel, chips),
        out_shape=[jax.ShapeDtypeStruct((per, B, B), bf16)] * chips,
        in_specs=[VMEM] * chips,
        out_specs=[VMEM] * chips,
        scratch_shapes=[pltpu.VMEM((chips, 2 * per, B, B), bf16), pltpu.VMEM((chips, per, B, B), bf16)],
        compiler_params=pltpu.CompilerParams(vmem_limit_bytes=4 * MIB),
        cost_estimate=pl.CostEstimate(
            flops=chips * per * 4 * B**3, bytes_accessed=chips * per * 6 * B * B, transcendentals=0
        ),
        name="run_chains",
    )(*parts)


def expand_kernel(chips, keep_ref, offset_ref, got_ref, got_offset_ref, *refs):
    parts = refs[:chips]
    mine_ref, other_ref = refs[chips:]
    section = lax.axis_index("section")
    chip = section // 2
    half = keep_ref.shape[0]
    per = half // chips

    def expand(first):
        for k in range(chips):
            for j in range(per):
                i = (chip - k + chips) % chips * per + j
                mine = (keep_ref[i], offset_ref[i])
                other = (got_ref[i], got_offset_ref[i])
                (ma, oa), (mb, ob) = (mine, other) if first else (other, mine)
                b = ob.astype(f32) + mm_nt(parts[k][j], mb)
                high, low = split(b)
                a = oa.astype(f32) + (mm_nt(high, ma) + mm_nt(low, ma))
                mine_ref[i] = a if first else b
                other_ref[i] = (b if first else a).astype(bf16)

    @pl.when(section % 2 == 0)
    def _():
        expand(True)

    @pl.when(section % 2 == 1)
    def _():
        expand(False)


def expand(keep, offsets, got, got_offsets, parts):
    chips = len(parts)
    half = keep.shape[0]
    return pl.pallas_call(
        functools.partial(expand_kernel, chips),
        out_shape=[jax.ShapeDtypeStruct((half, B, B), f32), jax.ShapeDtypeStruct((half, B, B), bf16)],
        in_specs=[VMEM] * (4 + chips),
        out_specs=[VMEM] * 2,
        compiler_params=pltpu.CompilerParams(vmem_limit_bytes=4 * MIB),
        cost_estimate=pl.CostEstimate(flops=half * 6 * B**3, bytes_accessed=half * 16 * B * B, transcendentals=0),
        name="expand",
    )(keep, offsets, got, got_offsets, *parts)


def gather_kernel(mine_ref, got_ref, out_ref, held, sem):
    half = mine_ref.shape[0]
    core = lax.axis_index("section") % 2
    own = pltpu.make_async_copy(mine_ref, out_ref.at[pl.ds(core * half, half)], sem.at[0])
    own.start()
    for i in range(half):
        held[i] = got_ref[i].astype(f32)
    rest = pltpu.make_async_copy(held, out_ref.at[pl.ds((1 - core) * half, half)], sem.at[1])
    rest.start()
    own.wait()
    rest.wait()


def gather_rows(mine, got):
    half = mine.shape[0]
    return pl.pallas_call(
        gather_kernel,
        out_shape=jax.ShapeDtypeStruct((2 * half, B, B), f32),
        in_specs=[VMEM, VMEM],
        out_specs=HBM,
        scratch_shapes=[pltpu.VMEM((half, B, B), f32), pltpu.SemaphoreType.DMA((2,))],
        compiler_params=pltpu.CompilerParams(vmem_limit_bytes=4 * MIB),
        cost_estimate=pl.CostEstimate(flops=0, bytes_accessed=half * 14 * B * B, transcendentals=0),
        name="gather_rows",
    )(mine, got)


def moved(x, stage, by, sections):
    pairs = []
    for s in range(sections):
        for a in range(SIDE):
            for c in range(SIDE):
                if (s + stage) % 2 == 0:
                    to = (a + by) % SIDE * SIDE + c
                else:
                    to = a * SIDE + (c + by) % SIDE
                pairs.append((s * SIDE * SIDE + a * SIDE + c, s * SIDE * SIDE + to))
    return lax.ppermute(x, ("section", "row"), pairs)


def across(x, sections, by):
    return lax.ppermute(x, "section", [(i, (i + 2 * by) % sections) for i in range(sections)])


def partner(x, sections):
    return lax.ppermute(x, "section", [(i, i ^ 1) for i in range(sections)])


def add(a, b):
    return (a.astype(f32) + b.astype(f32)).astype(bf16)


def per_device(
    coupling,
    diag_inverse,
    pivot_inverse,
    cross_left,
    cross_right,
    cross_pivot,
    cross_owner,
    foreign_target_row,
    cross_count,
    local_left,
    local_right,
    local_pivot,
    local_target,
    adjoint_seed,
):
    sections = lax.axis_size("section")
    rows = coupling.shape[0]
    slots = cross_left.shape[0]
    half = rows // 2
    me = lax.axis_index("row")
    odd = lax.axis_index("section") % 2

    owner = cross_owner[:, 0]
    dx = (owner // SIDE - me // SIDE) % SIDE
    dz = (owner % SIDE - me % SIDE) % SIDE
    a = jnp.where(odd == 0, dx, dz)
    b = jnp.where(odd == 0, dz, dx)
    upper = foreign_target_row // half
    spot = b * half + foreign_target_row % half
    n = SIDE * half
    group = 2 * n
    minus = (a == 3).astype(jnp.int32)
    cell = spot + jnp.where(
        a == 2,
        upper * n,
        jnp.where(a == 0, 3 * group + upper * n, jnp.where(minus == upper, 2 * group, group) + minus * n),
    )
    slot = jnp.arange(slots, dtype=jnp.int32)
    live = slot < cross_count[0]
    word = cell | (cross_pivot << PIVOT_BIT) | (slot << SLOT_BIT)
    word = word | jnp.where(live, jnp.where(cell < group, 1 << FAR_BIT, 1 << NEAR_BIT), 0)
    local_word = local_target | (local_pivot << PIVOT_BIT)

    far, on_chip = far_sums(0, [n] * 2, word, pivot_inverse, cross_left, cross_right)
    far_in = [moved(x, 0, w, sections) for x, w in zip(far, (1, -1))]
    near = near_sums(group, [n] * 4 + [2 * n], word, on_chip)
    alone_in = [moved(x, 0, w, sections) for x, w in zip(near[:2], (1, -1))]
    joined = [add(x, y) for x, y in zip(near[2:4], far_in)]
    joined_in = [moved(x, 0, w, sections) for x, w in zip(joined, (1, -1))]

    base, offsets, give_offsets = local_and_offset(
        local_word, pivot_inverse, coupling, local_left, local_right, diag_inverse, adjoint_seed, joined
    )
    got_offsets = partner(give_offsets, sections)

    arrivals = (joined_in[0], alone_in[1], alone_in[0], joined_in[1])
    totals = first_totals(near[4], arrivals, [base, got_offsets])
    parts = [totals[0]] + [moved(totals[k], 1, k, sections) for k in (2, 1, 3)]
    updated, keep, give = coupling_and_step(base, diag_inverse, parts)
    chips = sections // 2
    got = partner(give, sections)
    maps = compose(chips, keep, offsets, got, got_offsets)
    maps = [maps[0]] + [across(maps[k], sections, k) for k in range(1, chips)]
    incoming = run_chains(maps)
    incoming = [incoming[0]] + [across(incoming[k], sections, k) for k in range(1, chips)]
    mine, other = expand(keep, offsets, got, got_offsets, incoming)
    adjoint = gather_rows(mine, partner(other, sections))
    return (updated, adjoint)


def solution(mesh):
    spread = ("section", "row")
    block = P(spread, None, None)
    line = P(spread)
    return jax.shard_map(
        per_device,
        mesh=mesh,
        in_specs=(
            block,
            block,
            block,
            block,
            block,
            line,
            P(spread, None),
            line,
            line,
            block,
            block,
            line,
            line,
            block,
        ),
        out_specs=(block, block),
        check_vma=False,
    )
```

```python
import functools

import jax
import jax.numpy as jnp
from jax import lax
from jax.experimental import pallas as pl
from jax.experimental.pallas import tpu as pltpu
from jax.sharding import PartitionSpec as P

B = 128
SIDE = 4
UNROLL = 16
CHUNKS = 8
CELL_MASK, PIVOT_BIT, FAR_BIT, NEAR_BIT, SLOT_BIT = 511, 9, 16, 17, 20
MIB = 1 << 20

ANY = pl.BlockSpec(memory_space=pl.ANY)
HBM = pl.BlockSpec(memory_space=pltpu.HBM)
VMEM = pl.BlockSpec(memory_space=pltpu.VMEM)
SMEM = pl.BlockSpec(memory_space=pltpu.SMEM)

bf16 = jnp.bfloat16
f32 = jnp.float32


def mm(a, b):
    return jnp.dot(a, b, preferred_element_type=f32)


def mm_nt(a, b):
    return lax.dot_general(a, b, (((1,), (1,)), ((), ())), preferred_element_type=f32)


def split(x):
    high = x.astype(bf16)
    return high, (x - high.astype(f32)).astype(bf16)


def stay(x):
    return pltpu.with_memory_space_constraint(x, pltpu.HBM)


def bulk(left_ref, right_ref, left, right, lsem, rsem):
    per = left.shape[0] // CHUNKS
    pairs = []
    for k in range(CHUNKS):
        part = pl.ds(k * per, per)
        pair = (
            pltpu.make_async_copy(left_ref.at[part], left.at[part], lsem.at[k]),
            pltpu.make_async_copy(right_ref.at[part], right.at[part], rsem.at[k]),
        )
        for c in pair:
            c.start()
        pairs.append(pair)
    return pairs


def sum_cells(first, flag, index_ref, listed, total, outs, ready, left, right, table):
    slots = left.shape[0]
    cells = total.shape[0] - 1

    def note(i, n):
        word = index_ref[i]
        listed[n] = word
        return n + ((word >> flag) & 1)

    count = lax.fori_loop(0, slots, note, 0, unroll=32)
    for u in range(UNROLL):
        listed[count + u] = first + cells

    def clear(c, _):
        total[c] = jnp.zeros((B, B), bf16)
        return 0

    lax.fori_loop(0, cells + 1, clear, 0, unroll=8)
    ready()

    def work(r, _):
        words = [listed[r * UNROLL + u] for u in range(UNROLL)]
        scaled = [mm(left[w >> SLOT_BIT], table[(w >> PIVOT_BIT) & 3]).astype(bf16) for w in words]
        updates = [mm(x, right[w >> SLOT_BIT]) for x, w in zip(scaled, words)]
        for w, u in zip(words, updates):
            c = (w & CELL_MASK) - first
            total[c] = (total[c].astype(f32) + u).astype(bf16)
        return 0

    lax.fori_loop(0, (count + UNROLL - 1) // UNROLL, work, 0)
    start = 0
    for out in outs:

        def give(c, _, out=out, start=start):
            out[c] = total[start + c]
            return 0

        lax.fori_loop(0, out.shape[0], give, 0, unroll=8)
        start += out.shape[0]


def far_kernel(first, index_ref, table_ref, left_ref, right_ref, *refs):
    *outs, left, right, table, index, listed, total, lsem, rsem, tsem, isem = refs
    index_copy = pltpu.make_async_copy(index_ref, index, isem)
    index_copy.start()
    pairs = bulk(left_ref, right_ref, left, right, lsem, rsem)
    table_copy = pltpu.make_async_copy(table_ref, table, tsem)
    table_copy.start()
    index_copy.wait()

    def ready():
        table_copy.wait()
        for pair in pairs:
            for c in pair:
                c.wait()

    sum_cells(first, FAR_BIT, index, listed, total, outs, ready, left, right, table)


def near_kernel(first, index_ref, table, left, right, *refs):
    *outs, listed, total = refs
    sum_cells(first, NEAR_BIT, index_ref, listed, total, outs, lambda: None, left, right, table)


def cell_shapes(sizes):
    return [jax.ShapeDtypeStruct((n, B, B), bf16) for n in sizes]


def far_sums(first, sizes, index, table, left, right):
    cells = sum(sizes)
    slots = left.shape[0]
    outs = pl.pallas_call(
        functools.partial(far_kernel, first),
        out_shape=cell_shapes(sizes) + [jax.ShapeDtypeStruct(x.shape, bf16) for x in (left, right, table)],
        in_specs=[VMEM, HBM, HBM, HBM],
        out_specs=[VMEM] * (len(sizes) + 3),
        scratch_shapes=[
            pltpu.SMEM((slots,), jnp.int32),
            pltpu.SMEM((slots + UNROLL,), jnp.int32),
            pltpu.VMEM((cells + 1, B, B), bf16),
            pltpu.SemaphoreType.DMA((CHUNKS,)),
            pltpu.SemaphoreType.DMA((CHUNKS,)),
            pltpu.SemaphoreType.DMA,
            pltpu.SemaphoreType.DMA,
        ],
        compiler_params=pltpu.CompilerParams(vmem_limit_bytes=9 * MIB + cells * 4 * B * B),
        cost_estimate=pl.CostEstimate(
            flops=slots * B**3, bytes_accessed=slots * 8 * B * B + cells * 2 * B * B, transcendentals=0
        ),
        name="far_sums",
    )(index, stay(table), stay(left), stay(right))
    return outs[: len(sizes)], outs[len(sizes) :]


def near_sums(first, sizes, index, held):
    left, right, table = held
    cells = sum(sizes)
    slots = left.shape[0]
    return pl.pallas_call(
        functools.partial(near_kernel, first),
        out_shape=cell_shapes(sizes),
        in_specs=[SMEM, VMEM, VMEM, VMEM],
        out_specs=[VMEM] * len(sizes),
        scratch_shapes=[pltpu.SMEM((slots + UNROLL,), jnp.int32), pltpu.VMEM((cells + 1, B, B), bf16)],
        compiler_params=pltpu.CompilerParams(vmem_limit_bytes=9 * MIB + cells * 4 * B * B),
        cost_estimate=pl.CostEstimate(
            flops=slots * 3 * B**3, bytes_accessed=slots * 4 * B * B + cells * 2 * B * B, transcendentals=0
        ),
        name="near_sums",
    )(index, table, left, right)


def local_kernel(index_ref, table_ref, coupling_ref, left_ref, right_ref, diag_ref, seed_ref, *refs):
    base_ref, keep_ref, give_ref, held, left, right, table, lsem, rsem, tsem = refs[-10:]
    slots = left.shape[0]
    rows = coupling_ref.shape[0]
    half = rows // 2
    core = lax.axis_index("section") % 2
    table_copy = pltpu.make_async_copy(table_ref, table, tsem)
    table_copy.start()
    pairs = bulk(left_ref, right_ref, left, right, lsem, rsem)
    for r in range(rows):
        base_ref[r] = coupling_ref[r].astype(f32)

    def offset(r, _):
        dh, dl = split(diag_ref[r])
        sh, sl = split(seed_ref[r])
        o = mm_nt(sh, dh) + (mm_nt(sh, dl) + mm_nt(sl, dh))
        held[(r + core * half) % rows] = o.astype(bf16)
        return 0

    lax.fori_loop(0, rows, offset, 0, unroll=4)
    for i in range(half):
        keep_ref[i] = held[i]
        give_ref[i] = held[half + i]
    table_copy.wait()
    per = slots // CHUNKS
    for k, pair in enumerate(pairs):
        for c in pair:
            c.wait()

        def work(i, _, k=k):
            at = [k * per + i * UNROLL + u for u in range(UNROLL)]
            words = [index_ref[j] for j in at]
            scaled = [mm(left[j], table[(w >> PIVOT_BIT) & 3]).astype(bf16) for j, w in zip(at, words)]
            updates = [mm(x, right[j]).astype(bf16).astype(f32) for x, j in zip(scaled, at)]
            for w, u in zip(words, updates):
                t = w & CELL_MASK
                base_ref[t] = base_ref[t] - u
            return 0

        lax.fori_loop(0, per // UNROLL, work, 0)


def local_and_offset(index, table, coupling, left, right, diag, seed, order):
    slots = left.shape[0]
    rows = coupling.shape[0]
    return pl.pallas_call(
        local_kernel,
        out_shape=[jax.ShapeDtypeStruct((rows, B, B), f32)] + [jax.ShapeDtypeStruct((rows // 2, B, B), bf16)] * 2,
        in_specs=[SMEM, HBM, VMEM, HBM, HBM, VMEM, VMEM] + [ANY] * len(order),
        out_specs=[VMEM] * 3,
        scratch_shapes=[
            pltpu.VMEM((rows, B, B), bf16),
            pltpu.VMEM((slots, B, B), bf16),
            pltpu.VMEM((slots, B, B), bf16),
            pltpu.VMEM(table.shape, bf16),
            pltpu.SemaphoreType.DMA((CHUNKS,)),
            pltpu.SemaphoreType.DMA((CHUNKS,)),
            pltpu.SemaphoreType.DMA,
        ],
        compiler_params=pltpu.CompilerParams(vmem_limit_bytes=16 * MIB),
        cost_estimate=pl.CostEstimate(
            flops=slots * 4 * B**3, bytes_accessed=slots * 4 * B * B + rows * 16 * B * B, transcendentals=0
        ),
        name="local_and_offset",
    )(index, stay(table), coupling, stay(left), stay(right), diag, seed, *order)


def first_totals_kernel(own, *refs):
    arrivals = (refs[:2], refs[2:4])
    outs = refs[-2 * SIDE + 1 :]
    h = own.shape[0] // (2 * SIDE)
    for half in range(2):
        for b in range(SIDE):
            t = own[pl.ds((half * SIDE + b) * h, h)].astype(f32)
            for a in arrivals[half]:
                t = t + a[pl.ds(b * h, h)].astype(f32)
            if b == 0:
                outs[0][pl.ds(half * h, h)] = t.astype(bf16)
            else:
                outs[2 * b - 1 + half][...] = t.astype(bf16)


def first_totals(own, arrivals, order):
    rows = own.shape[0] // SIDE
    return pl.pallas_call(
        first_totals_kernel,
        out_shape=cell_shapes([rows] + [rows // 2] * (2 * SIDE - 2)),
        in_specs=[VMEM] * 5 + [ANY] * len(order),
        out_specs=[VMEM] * (2 * SIDE - 1),
        compiler_params=pltpu.CompilerParams(vmem_limit_bytes=9 * MIB),
        cost_estimate=pl.CostEstimate(flops=0, bytes_accessed=256 * 2 * B * B, transcendentals=0),
        name="first_totals",
    )(own, *arrivals, *order)


def coupling_kernel(base_ref, diag_ref, own_ref, *refs):
    parts = (refs[:2], refs[2:4])
    new_ref, keep_ref, give_ref, new, held, sem = refs[4:]
    rows = base_ref.shape[0]
    half = rows // 2
    group = half // 2
    core = lax.axis_index("section") % 2
    copies = []
    for g in range(rows // group):

        def finish(i, _, g=g):
            r = g * group + i
            t = base_ref[r] - own_ref[r].astype(f32)
            for p in parts[g * group // half]:
                t = t - p[g * group % half + i].astype(f32)
            new[r] = t
            th, tl = split(t)
            dh, dl = split(diag_ref[r])
            held[(r + core * half) % rows] = -(mm(dh, th) + (mm(dh, tl) + mm(dl, th))).astype(bf16)
            return 0

        lax.fori_loop(0, group, finish, 0, unroll=True)
        part = pl.ds(g * group, group)
        copies.append(pltpu.make_async_copy(new.at[part], new_ref.at[part], sem.at[g]))
        copies[-1].start()
    for i in range(half):
        keep_ref[i] = held[i]
        give_ref[i] = held[half + i]
    for c in copies:
        c.wait()


def coupling_and_step(base, diag, own, parts):
    rows = base.shape[0]
    half = rows // 2
    return pl.pallas_call(
        coupling_kernel,
        out_shape=[jax.ShapeDtypeStruct((rows, B, B), f32)] + cell_shapes([half, half]),
        in_specs=[VMEM] * 7,
        out_specs=[HBM, VMEM, VMEM],
        scratch_shapes=[
            pltpu.VMEM((rows, B, B), f32),
            pltpu.VMEM((rows, B, B), bf16),
            pltpu.SemaphoreType.DMA((4,)),
        ],
        compiler_params=pltpu.CompilerParams(vmem_limit_bytes=9 * MIB),
        cost_estimate=pl.CostEstimate(flops=rows * 6 * B**3, bytes_accessed=rows * 22 * B * B, transcendentals=0),
        name="coupling_and_step",
    )(base, diag, own, *parts)


def compose_kernel(chips, keep_ref, offset_ref, got_ref, got_offset_ref, *outs):
    section = lax.axis_index("section")
    chip = section // 2
    half = keep_ref.shape[0]
    per = half // chips

    def compose(first):
        for k in range(chips):
            for j in range(per):
                i = (chip + k) % chips * per + j
                mine = (keep_ref[i], offset_ref[i])
                other = (got_ref[i], got_offset_ref[i])
                (ma, oa), (mb, ob) = (mine, other) if first else (other, mine)
                outs[k][j] = mm(ma, mb).astype(bf16)
                outs[k][per + j] = (oa.astype(f32) + mm_nt(ob, ma)).astype(bf16)

    @pl.when(section % 2 == 0)
    def _():
        compose(True)

    @pl.when(section % 2 == 1)
    def _():
        compose(False)


def compose(chips, keep, offsets, got, got_offsets):
    half = keep.shape[0]
    return pl.pallas_call(
        functools.partial(compose_kernel, chips),
        out_shape=[jax.ShapeDtypeStruct((2 * half // chips, B, B), bf16)] * chips,
        in_specs=[VMEM] * 4,
        out_specs=[VMEM] * chips,
        compiler_params=pltpu.CompilerParams(vmem_limit_bytes=4 * MIB),
        cost_estimate=pl.CostEstimate(flops=half * 4 * B**3, bytes_accessed=half * 12 * B * B, transcendentals=0),
        name="compose",
    )(keep, offsets, got, got_offsets)


def chain_kernel(chips, *refs):
    parts = refs[:chips]
    outs = refs[chips : 2 * chips]
    maps, incoming = refs[2 * chips :]
    chip = lax.axis_index("section") // 2
    per = outs[0].shape[0]
    for k in range(chips):
        for i in range(2 * per):
            maps[(chip - k + chips) % chips, i] = parts[k][i]
    current = [jnp.zeros((B, B), f32)] * per
    for c in range(chips - 1, -1, -1):
        for j in range(per):
            incoming[c, j] = current[j].astype(bf16)
            if c > 0:
                new = maps[c, per + j].astype(f32)
                if c < chips - 1:
                    high, low = split(current[j])
                    new = new + (mm_nt(high, maps[c, j]) + mm_nt(low, maps[c, j]))
                current[j] = new
    for k in range(chips):
        for j in range(per):
            outs[k][j] = incoming[(chip + k) % chips, j]


def run_chains(parts):
    chips = len(parts)
    per = parts[0].shape[0] // 2
    return pl.pallas_call(
        functools.partial(chain_kernel, chips),
        out_shape=[jax.ShapeDtypeStruct((per, B, B), bf16)] * chips,
        in_specs=[VMEM] * chips,
        out_specs=[VMEM] * chips,
        scratch_shapes=[pltpu.VMEM((chips, 2 * per, B, B), bf16), pltpu.VMEM((chips, per, B, B), bf16)],
        compiler_params=pltpu.CompilerParams(vmem_limit_bytes=4 * MIB),
        cost_estimate=pl.CostEstimate(
            flops=chips * per * 4 * B**3, bytes_accessed=chips * per * 6 * B * B, transcendentals=0
        ),
        name="run_chains",
    )(*parts)


def expand_kernel(chips, keep_ref, offset_ref, got_ref, got_offset_ref, *refs):
    parts = refs[:chips]
    mine_ref, other_ref = refs[chips:]
    section = lax.axis_index("section")
    chip = section // 2
    half = keep_ref.shape[0]
    per = half // chips

    def expand(first):
        for k in range(chips):
            for j in range(per):
                i = (chip - k + chips) % chips * per + j
                mine = (keep_ref[i], offset_ref[i])
                other = (got_ref[i], got_offset_ref[i])
                (ma, oa), (mb, ob) = (mine, other) if first else (other, mine)
                b = ob.astype(f32) + mm_nt(parts[k][j], mb)
                high, low = split(b)
                a = oa.astype(f32) + (mm_nt(high, ma) + mm_nt(low, ma))
                mine_ref[i] = a if first else b
                other_ref[i] = (b if first else a).astype(bf16)

    @pl.when(section % 2 == 0)
    def _():
        expand(True)

    @pl.when(section % 2 == 1)
    def _():
        expand(False)


def expand(keep, offsets, got, got_offsets, parts):
    chips = len(parts)
    half = keep.shape[0]
    return pl.pallas_call(
        functools.partial(expand_kernel, chips),
        out_shape=[jax.ShapeDtypeStruct((half, B, B), f32), jax.ShapeDtypeStruct((half, B, B), bf16)],
        in_specs=[VMEM] * (4 + chips),
        out_specs=[VMEM] * 2,
        compiler_params=pltpu.CompilerParams(vmem_limit_bytes=4 * MIB),
        cost_estimate=pl.CostEstimate(flops=half * 6 * B**3, bytes_accessed=half * 16 * B * B, transcendentals=0),
        name="expand",
    )(keep, offsets, got, got_offsets, *parts)


def gather_kernel(mine_ref, got_ref, out_ref, held, sem):
    half = mine_ref.shape[0]
    core = lax.axis_index("section") % 2
    own = pltpu.make_async_copy(mine_ref, out_ref.at[pl.ds(core * half, half)], sem.at[0])
    own.start()
    for i in range(half):
        held[i] = got_ref[i].astype(f32)
    rest = pltpu.make_async_copy(held, out_ref.at[pl.ds((1 - core) * half, half)], sem.at[1])
    rest.start()
    own.wait()
    rest.wait()


def gather_rows(mine, got):
    half = mine.shape[0]
    return pl.pallas_call(
        gather_kernel,
        out_shape=jax.ShapeDtypeStruct((2 * half, B, B), f32),
        in_specs=[VMEM, VMEM],
        out_specs=HBM,
        scratch_shapes=[pltpu.VMEM((half, B, B), f32), pltpu.SemaphoreType.DMA((2,))],
        compiler_params=pltpu.CompilerParams(vmem_limit_bytes=4 * MIB),
        cost_estimate=pl.CostEstimate(flops=0, bytes_accessed=half * 14 * B * B, transcendentals=0),
        name="gather_rows",
    )(mine, got)


def moved(x, stage, by, sections):
    pairs = []
    for s in range(sections):
        for a in range(SIDE):
            for c in range(SIDE):
                if (s + stage) % 2 == 0:
                    to = (a + by) % SIDE * SIDE + c
                else:
                    to = a * SIDE + (c + by) % SIDE
                pairs.append((s * SIDE * SIDE + a * SIDE + c, s * SIDE * SIDE + to))
    return lax.ppermute(x, ("section", "row"), pairs)


def across(x, sections, by):
    return lax.ppermute(x, "section", [(i, (i + 2 * by) % sections) for i in range(sections)])


def partner(x, sections):
    return lax.ppermute(x, "section", [(i, i ^ 1) for i in range(sections)])


def add(a, b):
    return (a.astype(f32) + b.astype(f32)).astype(bf16)


def per_device(
    coupling,
    diag_inverse,
    pivot_inverse,
    cross_left,
    cross_right,
    cross_pivot,
    cross_owner,
    foreign_target_row,
    cross_count,
    local_left,
    local_right,
    local_pivot,
    local_target,
    adjoint_seed,
):
    sections = lax.axis_size("section")
    rows = coupling.shape[0]
    slots = cross_left.shape[0]
    half = rows // 2
    me = lax.axis_index("row")
    odd = lax.axis_index("section") % 2

    owner = cross_owner[:, 0]
    dx = (owner // SIDE - me // SIDE) % SIDE
    dz = (owner % SIDE - me % SIDE) % SIDE
    a = jnp.where(odd == 0, dx, dz)
    b = jnp.where(odd == 0, dz, dx)
    upper = foreign_target_row // half
    spot = b * half + foreign_target_row % half
    n = SIDE * half
    group = 2 * n
    minus = (a == 3).astype(jnp.int32)
    cell = spot + jnp.where(
        a == 2,
        upper * n,
        jnp.where(a == 0, 3 * group + upper * n, jnp.where(minus == upper, 2 * group, group) + minus * n),
    )
    slot = jnp.arange(slots, dtype=jnp.int32)
    live = slot < cross_count[0]
    word = cell | (cross_pivot << PIVOT_BIT) | (slot << SLOT_BIT)
    word = word | jnp.where(live, jnp.where(cell < group, 1 << FAR_BIT, 1 << NEAR_BIT), 0)
    local_word = local_target | (local_pivot << PIVOT_BIT)

    far, on_chip = far_sums(0, [n] * 2, word, pivot_inverse, cross_left, cross_right)
    far_in = [moved(x, 0, w, sections) for x, w in zip(far, (1, -1))]
    near = near_sums(group, [n] * 4 + [2 * n], word, on_chip)
    alone_in = [moved(x, 0, w, sections) for x, w in zip(near[:2], (1, -1))]
    joined = [add(x, y) for x, y in zip(near[2:4], far_in)]
    joined_in = [moved(x, 0, w, sections) for x, w in zip(joined, (1, -1))]

    base, offsets, give_offsets = local_and_offset(
        local_word, pivot_inverse, coupling, local_left, local_right, diag_inverse, adjoint_seed, joined
    )
    got_offsets = partner(give_offsets, sections)

    arrivals = (joined_in[0], alone_in[1], alone_in[0], joined_in[1])
    own, one_low, one_high, two_low, two_high, three_low, three_high = first_totals(near[4], arrivals, [base, got_offsets])
    passed = [moved(two_low, 1, 1, sections), moved(two_high, 1, -1, sections)]
    alone = [moved(three_low, 1, -1, sections), moved(one_high, 1, 1, sections)]
    joined = [add(one_low, passed[0]), add(three_high, passed[1])]
    joined = [moved(joined[0], 1, 1, sections), moved(joined[1], 1, -1, sections)]
    parts = (joined[0], alone[0], alone[1], joined[1])
    updated, keep, give = coupling_and_step(base, diag_inverse, own, parts)
    chips = sections // 2
    got = partner(give, sections)
    maps = compose(chips, keep, offsets, got, got_offsets)
    maps = [maps[0]] + [across(maps[k], sections, k) for k in range(1, chips)]
    incoming = run_chains(maps)
    incoming = [incoming[0]] + [across(incoming[k], sections, k) for k in range(1, chips)]
    mine, other = expand(keep, offsets, got, got_offsets, incoming)
    adjoint = gather_rows(mine, partner(other, sections))
    return (updated, adjoint)


def solution(mesh):
    spread = ("section", "row")
    block = P(spread, None, None)
    line = P(spread)
    return jax.shard_map(
        per_device,
        mesh=mesh,
        in_specs=(
            block,
            block,
            block,
            block,
            block,
            line,
            P(spread, None),
            line,
            line,
            block,
            block,
            line,
            line,
            block,
        ),
        out_specs=(block, block),
        check_vma=False,
    )
```

```python
import functools

import jax
import jax.numpy as jnp
from jax import lax
from jax.experimental import pallas as pl
from jax.experimental.pallas import tpu as pltpu
from jax.sharding import PartitionSpec as P

B = 128
SIDE = 4
UNROLL = 16
CHUNKS = 8
CELL_MASK, PIVOT_BIT, FAR_BIT, NEAR_BIT, SLOT_BIT = 511, 9, 16, 17, 20
MIB = 1 << 20

ANY = pl.BlockSpec(memory_space=pl.ANY)
HBM = pl.BlockSpec(memory_space=pltpu.HBM)
VMEM = pl.BlockSpec(memory_space=pltpu.VMEM)
SMEM = pl.BlockSpec(memory_space=pltpu.SMEM)

bf16 = jnp.bfloat16
f32 = jnp.float32


def mm(a, b):
    return jnp.dot(a, b, preferred_element_type=f32)


def mm_nt(a, b):
    return lax.dot_general(a, b, (((1,), (1,)), ((), ())), preferred_element_type=f32)


def split(x):
    high = x.astype(bf16)
    return high, (x - high.astype(f32)).astype(bf16)


def stay(x):
    return pltpu.with_memory_space_constraint(x, pltpu.HBM)


def bulk(left_ref, right_ref, left, right, lsem, rsem):
    per = left.shape[0] // CHUNKS
    pairs = []
    for k in range(CHUNKS):
        part = pl.ds(k * per, per)
        pair = (
            pltpu.make_async_copy(left_ref.at[part], left.at[part], lsem.at[k]),
            pltpu.make_async_copy(right_ref.at[part], right.at[part], rsem.at[k]),
        )
        for c in pair:
            c.start()
        pairs.append(pair)
    return pairs


def sum_cells(first, flag, index_ref, listed, total, outs, ready, left, right, table):
    slots = left.shape[0]
    cells = total.shape[0] - 1

    def note(i, n):
        word = index_ref[i]
        listed[n] = word
        return n + ((word >> flag) & 1)

    count = lax.fori_loop(0, slots, note, 0, unroll=32)
    for u in range(UNROLL):
        listed[count + u] = first + cells

    def clear(c, _):
        total[c] = jnp.zeros((B, B), bf16)
        return 0

    lax.fori_loop(0, cells + 1, clear, 0, unroll=8)
    ready()

    def work(r, _):
        words = [listed[r * UNROLL + u] for u in range(UNROLL)]
        scaled = [mm(left[w >> SLOT_BIT], table[(w >> PIVOT_BIT) & 3]).astype(bf16) for w in words]
        updates = [mm(x, right[w >> SLOT_BIT]) for x, w in zip(scaled, words)]
        for w, u in zip(words, updates):
            c = (w & CELL_MASK) - first
            total[c] = (total[c].astype(f32) + u).astype(bf16)
        return 0

    lax.fori_loop(0, (count + UNROLL - 1) // UNROLL, work, 0)
    start = 0
    for out in outs:

        def give(c, _, out=out, start=start):
            out[c] = total[start + c]
            return 0

        lax.fori_loop(0, out.shape[0], give, 0, unroll=8)
        start += out.shape[0]


def far_kernel(first, index_ref, table_ref, left_ref, right_ref, *refs):
    *outs, left, right, table, index, listed, total, lsem, rsem, tsem, isem = refs
    index_copy = pltpu.make_async_copy(index_ref, index, isem)
    index_copy.start()
    pairs = bulk(left_ref, right_ref, left, right, lsem, rsem)
    table_copy = pltpu.make_async_copy(table_ref, table, tsem)
    table_copy.start()
    index_copy.wait()

    def ready():
        table_copy.wait()
        for pair in pairs:
            for c in pair:
                c.wait()

    sum_cells(first, FAR_BIT, index, listed, total, outs, ready, left, right, table)


def near_kernel(first, index_ref, table, left, right, *refs):
    *outs, listed, total = refs
    sum_cells(first, NEAR_BIT, index_ref, listed, total, outs, lambda: None, left, right, table)


def cell_shapes(sizes):
    return [jax.ShapeDtypeStruct((n, B, B), bf16) for n in sizes]


def far_sums(first, sizes, index, table, left, right):
    cells = sum(sizes)
    slots = left.shape[0]
    outs = pl.pallas_call(
        functools.partial(far_kernel, first),
        out_shape=cell_shapes(sizes) + [jax.ShapeDtypeStruct(x.shape, bf16) for x in (left, right, table)],
        in_specs=[VMEM, HBM, HBM, HBM],
        out_specs=[VMEM] * (len(sizes) + 3),
        scratch_shapes=[
            pltpu.SMEM((slots,), jnp.int32),
            pltpu.SMEM((slots + UNROLL,), jnp.int32),
            pltpu.VMEM((cells + 1, B, B), bf16),
            pltpu.SemaphoreType.DMA((CHUNKS,)),
            pltpu.SemaphoreType.DMA((CHUNKS,)),
            pltpu.SemaphoreType.DMA,
            pltpu.SemaphoreType.DMA,
        ],
        compiler_params=pltpu.CompilerParams(vmem_limit_bytes=9 * MIB + cells * 4 * B * B),
        cost_estimate=pl.CostEstimate(
            flops=slots * B**3, bytes_accessed=slots * 8 * B * B + cells * 2 * B * B, transcendentals=0
        ),
        name="far_sums",
    )(index, stay(table), stay(left), stay(right))
    return outs[: len(sizes)], outs[len(sizes) :]


def near_sums(first, sizes, index, held):
    left, right, table = held
    cells = sum(sizes)
    slots = left.shape[0]
    return pl.pallas_call(
        functools.partial(near_kernel, first),
        out_shape=cell_shapes(sizes),
        in_specs=[SMEM, VMEM, VMEM, VMEM],
        out_specs=[VMEM] * len(sizes),
        scratch_shapes=[pltpu.SMEM((slots + UNROLL,), jnp.int32), pltpu.VMEM((cells + 1, B, B), bf16)],
        compiler_params=pltpu.CompilerParams(vmem_limit_bytes=9 * MIB + cells * 4 * B * B),
        cost_estimate=pl.CostEstimate(
            flops=slots * 3 * B**3, bytes_accessed=slots * 4 * B * B + cells * 2 * B * B, transcendentals=0
        ),
        name="near_sums",
    )(index, table, left, right)


def local_kernel(index_ref, table_ref, coupling_ref, left_ref, right_ref, diag_ref, seed_ref, *refs):
    base_ref, keep_ref, give_ref, held, left, right, table, lsem, rsem, tsem = refs[-10:]
    slots = left.shape[0]
    rows = coupling_ref.shape[0]
    half = rows // 2
    core = lax.axis_index("section") % 2
    table_copy = pltpu.make_async_copy(table_ref, table, tsem)
    table_copy.start()
    pairs = bulk(left_ref, right_ref, left, right, lsem, rsem)
    for r in range(rows):
        base_ref[r] = coupling_ref[r].astype(f32)

    def offset(r, _):
        dh, dl = split(diag_ref[r])
        sh, sl = split(seed_ref[r])
        o = mm_nt(sh, dh) + (mm_nt(sh, dl) + mm_nt(sl, dh))
        held[(r + core * half) % rows] = o.astype(bf16)
        return 0

    lax.fori_loop(0, rows, offset, 0, unroll=4)
    for i in range(half):
        keep_ref[i] = held[i]
        give_ref[i] = held[half + i]
    table_copy.wait()
    per = slots // CHUNKS
    for k, pair in enumerate(pairs):
        for c in pair:
            c.wait()

        def work(i, _, k=k):
            at = [k * per + i * UNROLL + u for u in range(UNROLL)]
            words = [index_ref[j] for j in at]
            scaled = [mm(left[j], table[(w >> PIVOT_BIT) & 3]).astype(bf16) for j, w in zip(at, words)]
            updates = [mm(x, right[j]).astype(bf16).astype(f32) for x, j in zip(scaled, at)]
            for w, u in zip(words, updates):
                t = w & CELL_MASK
                base_ref[t] = base_ref[t] - u
            return 0

        lax.fori_loop(0, per // UNROLL, work, 0)


def local_and_offset(index, table, coupling, left, right, diag, seed, order):
    slots = left.shape[0]
    rows = coupling.shape[0]
    return pl.pallas_call(
        local_kernel,
        out_shape=[jax.ShapeDtypeStruct((rows, B, B), f32)] + [jax.ShapeDtypeStruct((rows // 2, B, B), bf16)] * 2,
        in_specs=[SMEM, HBM, VMEM, HBM, HBM, VMEM, VMEM] + [ANY] * len(order),
        out_specs=[VMEM] * 3,
        scratch_shapes=[
            pltpu.VMEM((rows, B, B), bf16),
            pltpu.VMEM((slots, B, B), bf16),
            pltpu.VMEM((slots, B, B), bf16),
            pltpu.VMEM(table.shape, bf16),
            pltpu.SemaphoreType.DMA((CHUNKS,)),
            pltpu.SemaphoreType.DMA((CHUNKS,)),
            pltpu.SemaphoreType.DMA,
        ],
        compiler_params=pltpu.CompilerParams(vmem_limit_bytes=16 * MIB),
        cost_estimate=pl.CostEstimate(
            flops=slots * 4 * B**3, bytes_accessed=slots * 4 * B * B + rows * 16 * B * B, transcendentals=0
        ),
        name="local_and_offset",
    )(index, stay(table), coupling, stay(left), stay(right), diag, seed, *order)


def first_totals_kernel(own, *refs):
    arrivals = (refs[:2], refs[2:4])
    outs = refs[-SIDE:]
    h = own.shape[0] // (2 * SIDE)
    for half in range(2):
        for b in range(SIDE):
            t = own[pl.ds((half * SIDE + b) * h, h)].astype(f32)
            for a in arrivals[half]:
                t = t + a[pl.ds(b * h, h)].astype(f32)
            outs[b][pl.ds(half * h, h)] = t.astype(bf16)


def first_totals(own, arrivals, order):
    rows = own.shape[0] // SIDE
    return pl.pallas_call(
        first_totals_kernel,
        out_shape=[jax.ShapeDtypeStruct((rows, B, B), bf16)] * SIDE,
        in_specs=[VMEM] * 5 + [ANY] * len(order),
        out_specs=[VMEM] * SIDE,
        compiler_params=pltpu.CompilerParams(vmem_limit_bytes=9 * MIB),
        cost_estimate=pl.CostEstimate(flops=0, bytes_accessed=256 * 2 * B * B, transcendentals=0),
        name="first_totals",
    )(own, *arrivals, *order)


def coupling_kernel(base_ref, diag_ref, *refs):
    parts = refs[:SIDE]
    new_ref, keep_ref, give_ref, new, held, sem = refs[4:]
    rows = base_ref.shape[0]
    half = rows // 2
    group = half // 2
    core = lax.axis_index("section") % 2
    copies = []
    for g in range(rows // group):

        def finish(i, _, g=g):
            r = g * group + i
            t = base_ref[r]
            for p in parts:
                t = t - p[r].astype(f32)
            new[r] = t
            th, tl = split(t)
            dh, dl = split(diag_ref[r])
            held[(r + core * half) % rows] = -(mm(dh, th) + (mm(dh, tl) + mm(dl, th))).astype(bf16)
            return 0

        lax.fori_loop(0, group, finish, 0, unroll=True)
        part = pl.ds(g * group, group)
        copies.append(pltpu.make_async_copy(new.at[part], new_ref.at[part], sem.at[g]))
        copies[-1].start()
    for i in range(half):
        keep_ref[i] = held[i]
        give_ref[i] = held[half + i]
    for c in copies:
        c.wait()


def coupling_and_step(base, diag, parts):
    rows = base.shape[0]
    half = rows // 2
    return pl.pallas_call(
        coupling_kernel,
        out_shape=[jax.ShapeDtypeStruct((rows, B, B), f32)] + cell_shapes([half, half]),
        in_specs=[VMEM] * (2 + SIDE),
        out_specs=[HBM, VMEM, VMEM],
        scratch_shapes=[
            pltpu.VMEM((rows, B, B), f32),
            pltpu.VMEM((rows, B, B), bf16),
            pltpu.SemaphoreType.DMA((4,)),
        ],
        compiler_params=pltpu.CompilerParams(vmem_limit_bytes=9 * MIB),
        cost_estimate=pl.CostEstimate(flops=rows * 6 * B**3, bytes_accessed=rows * 22 * B * B, transcendentals=0),
        name="coupling_and_step",
    )(base, diag, *parts)


def compose_kernel(chips, keep_ref, offset_ref, got_ref, got_offset_ref, *outs):
    section = lax.axis_index("section")
    chip = section // 2
    half = keep_ref.shape[0]
    per = half // chips

    def compose(first):
        for k in range(chips):
            for j in range(per):
                i = (chip + k) % chips * per + j
                mine = (keep_ref[i], offset_ref[i])
                other = (got_ref[i], got_offset_ref[i])
                (ma, oa), (mb, ob) = (mine, other) if first else (other, mine)
                outs[k][j] = mm(ma, mb).astype(bf16)
                outs[k][per + j] = (oa.astype(f32) + mm_nt(ob, ma)).astype(bf16)

    @pl.when(section % 2 == 0)
    def _():
        compose(True)

    @pl.when(section % 2 == 1)
    def _():
        compose(False)


def compose(chips, keep, offsets, got, got_offsets):
    half = keep.shape[0]
    return pl.pallas_call(
        functools.partial(compose_kernel, chips),
        out_shape=[jax.ShapeDtypeStruct((2 * half // chips, B, B), bf16)] * chips,
        in_specs=[VMEM] * 4,
        out_specs=[VMEM] * chips,
        compiler_params=pltpu.CompilerParams(vmem_limit_bytes=4 * MIB),
        cost_estimate=pl.CostEstimate(flops=half * 4 * B**3, bytes_accessed=half * 12 * B * B, transcendentals=0),
        name="compose",
    )(keep, offsets, got, got_offsets)


def chain_kernel(chips, *refs):
    parts = refs[:chips]
    outs = refs[chips : 2 * chips]
    maps, incoming = refs[2 * chips :]
    chip = lax.axis_index("section") // 2
    per = outs[0].shape[0]
    for k in range(chips):
        for i in range(2 * per):
            maps[(chip - k + chips) % chips, i] = parts[k][i]
    current = [jnp.zeros((B, B), f32)] * per
    for c in range(chips - 1, -1, -1):
        for j in range(per):
            incoming[c, j] = current[j].astype(bf16)
            if c > 0:
                new = maps[c, per + j].astype(f32)
                if c < chips - 1:
                    high, low = split(current[j])
                    new = new + (mm_nt(high, maps[c, j]) + mm_nt(low, maps[c, j]))
                current[j] = new
    for k in range(chips):
        for j in range(per):
            outs[k][j] = incoming[(chip + k) % chips, j]


def run_chains(parts):
    chips = len(parts)
    per = parts[0].shape[0] // 2
    return pl.pallas_call(
        functools.partial(chain_kernel, chips),
        out_shape=[jax.ShapeDtypeStruct((per, B, B), bf16)] * chips,
        in_specs=[VMEM] * chips,
        out_specs=[VMEM] * chips,
        scratch_shapes=[pltpu.VMEM((chips, 2 * per, B, B), bf16), pltpu.VMEM((chips, per, B, B), bf16)],
        compiler_params=pltpu.CompilerParams(vmem_limit_bytes=4 * MIB),
        cost_estimate=pl.CostEstimate(
            flops=chips * per * 4 * B**3, bytes_accessed=chips * per * 6 * B * B, transcendentals=0
        ),
        name="run_chains",
    )(*parts)


def expand_kernel(chips, keep_ref, offset_ref, got_ref, got_offset_ref, *refs):
    parts = refs[:chips]
    mine_ref, other_ref = refs[chips:]
    section = lax.axis_index("section")
    chip = section // 2
    half = keep_ref.shape[0]
    per = half // chips

    def expand(first):
        for k in range(chips):
            for j in range(per):
                i = (chip - k + chips) % chips * per + j
                mine = (keep_ref[i], offset_ref[i])
                other = (got_ref[i], got_offset_ref[i])
                (ma, oa), (mb, ob) = (mine, other) if first else (other, mine)
                b = ob.astype(f32) + mm_nt(parts[k][j], mb)
                a = oa.astype(f32) + mm_nt(b.astype(bf16), ma)
                mine_ref[i] = a if first else b
                other_ref[i] = (b if first else a).astype(bf16)

    @pl.when(section % 2 == 0)
    def _():
        expand(True)

    @pl.when(section % 2 == 1)
    def _():
        expand(False)


def expand(keep, offsets, got, got_offsets, parts):
    chips = len(parts)
    half = keep.shape[0]
    return pl.pallas_call(
        functools.partial(expand_kernel, chips),
        out_shape=[jax.ShapeDtypeStruct((half, B, B), f32), jax.ShapeDtypeStruct((half, B, B), bf16)],
        in_specs=[VMEM] * (4 + chips),
        out_specs=[VMEM] * 2,
        compiler_params=pltpu.CompilerParams(vmem_limit_bytes=4 * MIB),
        cost_estimate=pl.CostEstimate(flops=half * 6 * B**3, bytes_accessed=half * 16 * B * B, transcendentals=0),
        name="expand",
    )(keep, offsets, got, got_offsets, *parts)


def store_kernel(mine_ref, out_ref, sem):
    half = mine_ref.shape[0]
    core = lax.axis_index("section") % 2
    copy = pltpu.make_async_copy(mine_ref, out_ref.at[pl.ds(core * half, half)], sem)
    copy.start()
    copy.wait()


def store_rows(mine):
    half = mine.shape[0]
    return pl.pallas_call(
        store_kernel,
        out_shape=jax.ShapeDtypeStruct((2 * half, B, B), f32),
        in_specs=[VMEM],
        out_specs=HBM,
        scratch_shapes=[pltpu.SemaphoreType.DMA],
        compiler_params=pltpu.CompilerParams(vmem_limit_bytes=2 * MIB),
        cost_estimate=pl.CostEstimate(flops=0, bytes_accessed=half * 8 * B * B, transcendentals=0),
        name="store_rows",
    )(mine)


def add_kernel(got_ref, part_ref, out_ref, held, sem):
    half = got_ref.shape[0]
    group = half // 2
    core = lax.axis_index("section") % 2
    copies = []
    for g in range(2):
        for i in range(g * group, (g + 1) * group):
            held[i] = got_ref[i].astype(f32)
        to = out_ref.at[pl.ds((1 - core) * half + g * group, group)]
        copies.append(pltpu.make_async_copy(held.at[pl.ds(g * group, group)], to, sem.at[g]))
        copies[-1].start()
    for c in copies:
        c.wait()


def add_rows(got, part):
    half = got.shape[0]
    return pl.pallas_call(
        add_kernel,
        out_shape=jax.ShapeDtypeStruct(part.shape, f32),
        in_specs=[VMEM, HBM],
        out_specs=HBM,
        scratch_shapes=[pltpu.VMEM((half, B, B), f32), pltpu.SemaphoreType.DMA((2,))],
        input_output_aliases={1: 0},
        compiler_params=pltpu.CompilerParams(vmem_limit_bytes=4 * MIB),
        cost_estimate=pl.CostEstimate(flops=0, bytes_accessed=half * 6 * B * B, transcendentals=0),
        name="add_rows",
    )(got, part)


def moved(x, stage, by, sections):
    pairs = []
    for s in range(sections):
        for a in range(SIDE):
            for c in range(SIDE):
                if (s + stage) % 2 == 0:
                    to = (a + by) % SIDE * SIDE + c
                else:
                    to = a * SIDE + (c + by) % SIDE
                pairs.append((s * SIDE * SIDE + a * SIDE + c, s * SIDE * SIDE + to))
    return lax.ppermute(x, ("section", "row"), pairs)


def across(x, sections, by):
    return lax.ppermute(x, "section", [(i, (i + 2 * by) % sections) for i in range(sections)])


def partner(x, sections):
    return lax.ppermute(x, "section", [(i, i ^ 1) for i in range(sections)])


def add(a, b):
    return (a.astype(f32) + b.astype(f32)).astype(bf16)


def per_device(
    coupling,
    diag_inverse,
    pivot_inverse,
    cross_left,
    cross_right,
    cross_pivot,
    cross_owner,
    foreign_target_row,
    cross_count,
    local_left,
    local_right,
    local_pivot,
    local_target,
    adjoint_seed,
):
    sections = lax.axis_size("section")
    rows = coupling.shape[0]
    slots = cross_left.shape[0]
    half = rows // 2
    me = lax.axis_index("row")
    odd = lax.axis_index("section") % 2

    owner = cross_owner[:, 0]
    dx = (owner // SIDE - me // SIDE) % SIDE
    dz = (owner % SIDE - me % SIDE) % SIDE
    a = jnp.where(odd == 0, dx, dz)
    b = jnp.where(odd == 0, dz, dx)
    upper = foreign_target_row // half
    spot = b * half + foreign_target_row % half
    n = SIDE * half
    group = 2 * n
    minus = (a == 3).astype(jnp.int32)
    cell = spot + jnp.where(
        a == 2,
        upper * n,
        jnp.where(a == 0, 3 * group + upper * n, jnp.where(minus == upper, 2 * group, group) + minus * n),
    )
    slot = jnp.arange(slots, dtype=jnp.int32)
    live = slot < cross_count[0]
    word = cell | (cross_pivot << PIVOT_BIT) | (slot << SLOT_BIT)
    word = word | jnp.where(live, jnp.where(cell < group, 1 << FAR_BIT, 1 << NEAR_BIT), 0)
    local_word = local_target | (local_pivot << PIVOT_BIT)

    far, on_chip = far_sums(0, [n] * 2, word, pivot_inverse, cross_left, cross_right)
    far_in = [moved(x, 0, w, sections) for x, w in zip(far, (1, -1))]
    near = near_sums(group, [n] * 4 + [2 * n], word, on_chip)
    alone_in = [moved(x, 0, w, sections) for x, w in zip(near[:2], (1, -1))]
    joined = [add(x, y) for x, y in zip(near[2:4], far_in)]
    joined_in = [moved(x, 0, w, sections) for x, w in zip(joined, (1, -1))]

    base, offsets, give_offsets = local_and_offset(
        local_word, pivot_inverse, coupling, local_left, local_right, diag_inverse, adjoint_seed, joined
    )
    got_offsets = partner(give_offsets, sections)

    arrivals = (joined_in[0], alone_in[1], alone_in[0], joined_in[1])
    totals = first_totals(near[4], arrivals, [base, got_offsets])
    parts = [totals[0]] + [moved(totals[k], 1, k, sections) for k in (2, 1, 3)]
    updated, keep, give = coupling_and_step(base, diag_inverse, parts)
    chips = sections // 2
    got = partner(give, sections)
    maps = compose(chips, keep, offsets, got, got_offsets)
    maps = [maps[0]] + [across(maps[k], sections, k) for k in range(1, chips)]
    incoming = run_chains(maps)
    incoming = [incoming[0]] + [across(incoming[k], sections, k) for k in range(1, chips)]
    mine, other = expand(keep, offsets, got, got_offsets, incoming)
    adjoint = add_rows(partner(other, sections), store_rows(mine))
    return (updated, adjoint)


def solution(mesh):
    spread = ("section", "row")
    block = P(spread, None, None)
    line = P(spread)
    return jax.shard_map(
        per_device,
        mesh=mesh,
        in_specs=(
            block,
            block,
            block,
            block,
            block,
            line,
            P(spread, None),
            line,
            line,
            block,
            block,
            line,
            line,
            block,
        ),
        out_specs=(block, block),
        check_vma=False,
    )
```

```python
import functools

import jax
import jax.numpy as jnp
from jax import lax
from jax.experimental import pallas as pl
from jax.experimental.pallas import tpu as pltpu
from jax.sharding import PartitionSpec as P

B = 128
SIDE = 4
UNROLL = 16
CHUNKS = 8
SIDE_BIT = 2
PLACES = sum(p << (3 * i) for i, p in enumerate((6, 7, 4, 2, 0, 1, 3, 5)))
CELL_MASK, PIVOT_BIT, FAR_BIT, NEAR_BIT, SLOT_BIT = 511, 9, 16, 17, 20
ORDER = (0, 2, 1, 3)
MIB = 1 << 20

ANY = pl.BlockSpec(memory_space=pl.ANY)
HBM = pl.BlockSpec(memory_space=pltpu.HBM)
VMEM = pl.BlockSpec(memory_space=pltpu.VMEM)
SMEM = pl.BlockSpec(memory_space=pltpu.SMEM)

bf16 = jnp.bfloat16
f32 = jnp.float32


def mm(a, b):
    return jnp.dot(a, b, preferred_element_type=f32)


def mm_nt(a, b):
    return lax.dot_general(a, b, (((1,), (1,)), ((), ())), preferred_element_type=f32)


def split(x):
    high = x.astype(bf16)
    return high, (x - high.astype(f32)).astype(bf16)


def stay(x):
    return pltpu.with_memory_space_constraint(x, pltpu.HBM)


def bulk(left_ref, right_ref, left, right, lsem, rsem):
    per = left.shape[0] // CHUNKS
    pairs = []
    for k in range(CHUNKS):
        part = pl.ds(k * per, per)
        pair = (
            pltpu.make_async_copy(left_ref.at[part], left.at[part], lsem.at[k]),
            pltpu.make_async_copy(right_ref.at[part], right.at[part], rsem.at[k]),
        )
        for c in pair:
            c.start()
        pairs.append(pair)
    return pairs


def sum_cells(first, flag, index_ref, listed, total, outs, ready, left, right, table):
    slots = left.shape[0]
    cells = total.shape[0] - 1

    def note(i, n):
        word = index_ref[i]
        listed[n] = word
        return n + ((word >> flag) & 1)

    count = lax.fori_loop(0, slots, note, 0, unroll=32)
    for u in range(UNROLL):
        listed[count + u] = first + cells

    def clear(c, _):
        total[c] = jnp.zeros((B, B), bf16)
        return 0

    lax.fori_loop(0, cells + 1, clear, 0, unroll=8)
    ready()

    def work(r, _):
        words = [listed[r * UNROLL + u] for u in range(UNROLL)]
        scaled = [mm(left[w >> SLOT_BIT], table[(w >> PIVOT_BIT) & 3]).astype(bf16) for w in words]
        updates = [mm(x, right[w >> SLOT_BIT]) for x, w in zip(scaled, words)]
        for w, u in zip(words, updates):
            c = (w & CELL_MASK) - first
            total[c] = (total[c].astype(f32) + u).astype(bf16)
        return 0

    lax.fori_loop(0, (count + UNROLL - 1) // UNROLL, work, 0)
    start = 0
    for out in outs:

        def give(c, _, out=out, start=start):
            out[c] = total[start + c]
            return 0

        lax.fori_loop(0, out.shape[0], give, 0, unroll=8)
        start += out.shape[0]


def far_kernel(half, owner_ref, target_ref, pivot_ref, count_ref, table_ref, left_ref, right_ref, *refs):
    *outs, left, right, table, index_ref, owner, target, pivot, index, listed, total, lsem, rsem, tsem, isem = refs
    slots = left.shape[0]
    given = [
        pltpu.make_async_copy(x, y, isem.at[k])
        for k, (x, y) in enumerate(((owner_ref, owner), (target_ref, target), (pivot_ref, pivot)))
    ]
    for c in given:
        c.start()
    pairs = bulk(left_ref, right_ref, left, right, lsem, rsem)
    table_copy = pltpu.make_async_copy(table_ref, table, tsem)
    table_copy.start()
    for c in given:
        c.wait()

    odd = lax.axis_index("section") % 2
    me = lax.axis_index("row")
    first_shift = jnp.where(odd == 0, SIDE_BIT, 0)
    second_shift = SIDE_BIT - first_shift
    first_me, second_me = me >> first_shift, me >> second_shift
    live = count_ref[0]
    half_bit = half.bit_length() - 1
    per_bit = half_bit + SIDE_BIT

    def word(i, _):
        a = ((owner[i] >> first_shift) - first_me) & (SIDE - 1)
        b = ((owner[i] >> second_shift) - second_me) & (SIDE - 1)
        place = (PLACES >> (3 * (2 * a + (target[i] >> half_bit)))) & 7
        cell = (place << per_bit) | (b << half_bit) | (target[i] & (half - 1))
        flag = jnp.where(a == 2, 1 << FAR_BIT, 1 << NEAR_BIT)
        flag = jnp.where(i < live, flag, 0)
        index[i] = cell | (pivot[i] << PIVOT_BIT) | (i << SLOT_BIT) | flag
        return 0

    lax.fori_loop(0, slots, word, 0, unroll=16)
    index_copy = pltpu.make_async_copy(index, index_ref, isem.at[3])
    index_copy.start()

    def ready():
        table_copy.wait()
        for pair in pairs:
            for c in pair:
                c.wait()

    sum_cells(0, FAR_BIT, index, listed, total, outs, ready, left, right, table)
    index_copy.wait()


def near_kernel(first, index_ref, table, left, right, *refs):
    *outs, listed, total = refs
    sum_cells(first, NEAR_BIT, index_ref, listed, total, outs, lambda: None, left, right, table)


def cell_shapes(sizes):
    return [jax.ShapeDtypeStruct((n, B, B), bf16) for n in sizes]


def far_sums(sizes, half, owner, target, pivot, count, table, left, right):
    cells = sum(sizes)
    slots = left.shape[0]
    shapes = [jax.ShapeDtypeStruct(x.shape, x.dtype) for x in (left, right, table, pivot)]
    outs = pl.pallas_call(
        functools.partial(far_kernel, half),
        out_shape=cell_shapes(sizes) + shapes,
        in_specs=[HBM] * 3 + [SMEM] + [HBM] * 3,
        out_specs=[VMEM] * (len(sizes) + 3) + [HBM],
        scratch_shapes=[
            pltpu.SMEM((slots,), jnp.int32),
            pltpu.SMEM((slots,), jnp.int32),
            pltpu.SMEM((slots,), jnp.int32),
            pltpu.SMEM((slots,), jnp.int32),
            pltpu.SMEM((slots + UNROLL,), jnp.int32),
            pltpu.VMEM((cells + 1, B, B), bf16),
            pltpu.SemaphoreType.DMA((CHUNKS,)),
            pltpu.SemaphoreType.DMA((CHUNKS,)),
            pltpu.SemaphoreType.DMA,
            pltpu.SemaphoreType.DMA((4,)),
        ],
        compiler_params=pltpu.CompilerParams(vmem_limit_bytes=9 * MIB + cells * 4 * B * B),
        cost_estimate=pl.CostEstimate(
            flops=slots * B**3, bytes_accessed=slots * 8 * B * B + cells * 2 * B * B, transcendentals=0
        ),
        name="far_sums",
    )(stay(owner), stay(target), stay(pivot), count, stay(table), stay(left), stay(right))
    return outs[: len(sizes)], outs[len(sizes) : -1], outs[-1]


def near_sums(first, sizes, index, held):
    left, right, table = held
    cells = sum(sizes)
    slots = left.shape[0]
    return pl.pallas_call(
        functools.partial(near_kernel, first),
        out_shape=cell_shapes(sizes),
        in_specs=[SMEM, VMEM, VMEM, VMEM],
        out_specs=[VMEM] * len(sizes),
        scratch_shapes=[pltpu.SMEM((slots + UNROLL,), jnp.int32), pltpu.VMEM((cells + 1, B, B), bf16)],
        compiler_params=pltpu.CompilerParams(vmem_limit_bytes=9 * MIB + cells * 4 * B * B),
        cost_estimate=pl.CostEstimate(
            flops=slots * 3 * B**3, bytes_accessed=slots * 4 * B * B + cells * 2 * B * B, transcendentals=0
        ),
        name="near_sums",
    )(index, table, left, right)


def local_kernel(index_ref, table_ref, coupling_ref, left_ref, right_ref, diag_ref, seed_ref, *refs):
    base_ref, keep_ref, give_ref, held, left, right, table, lsem, rsem, tsem = refs[-10:]
    slots = left.shape[0]
    rows = coupling_ref.shape[0]
    half = rows // 2
    core = lax.axis_index("section") % 2
    table_copy = pltpu.make_async_copy(table_ref, table, tsem)
    table_copy.start()
    pairs = bulk(left_ref, right_ref, left, right, lsem, rsem)
    for r in range(rows):
        base_ref[r] = coupling_ref[r].astype(f32)

    def offset(r, _):
        dh, dl = split(diag_ref[r])
        sh, sl = split(seed_ref[r])
        o = mm_nt(sh, dh) + (mm_nt(sh, dl) + mm_nt(sl, dh))
        held[(r + core * half) % rows] = o.astype(bf16)
        return 0

    lax.fori_loop(0, rows, offset, 0, unroll=4)
    for i in range(half):
        keep_ref[i] = held[i]
        give_ref[i] = held[half + i]
    table_copy.wait()
    per = slots // CHUNKS
    for k, pair in enumerate(pairs):
        for c in pair:
            c.wait()

        def work(i, _, k=k):
            at = [k * per + i * UNROLL + u for u in range(UNROLL)]
            words = [index_ref[j] for j in at]
            scaled = [mm(left[j], table[(w >> PIVOT_BIT) & 3]).astype(bf16) for j, w in zip(at, words)]
            updates = [mm(x, right[j]).astype(bf16).astype(f32) for x, j in zip(scaled, at)]
            for w, u in zip(words, updates):
                t = w & CELL_MASK
                base_ref[t] = base_ref[t] - u
            return 0

        lax.fori_loop(0, per // UNROLL, work, 0)


def local_and_offset(index, table, coupling, left, right, diag, seed, order):
    slots = left.shape[0]
    rows = coupling.shape[0]
    return pl.pallas_call(
        local_kernel,
        out_shape=[jax.ShapeDtypeStruct((rows, B, B), f32)] + [jax.ShapeDtypeStruct((rows // 2, B, B), bf16)] * 2,
        in_specs=[SMEM, HBM, VMEM, HBM, HBM, VMEM, VMEM] + [ANY] * len(order),
        out_specs=[VMEM] * 3,
        scratch_shapes=[
            pltpu.VMEM((rows, B, B), bf16),
            pltpu.VMEM((slots, B, B), bf16),
            pltpu.VMEM((slots, B, B), bf16),
            pltpu.VMEM(table.shape, bf16),
            pltpu.SemaphoreType.DMA((CHUNKS,)),
            pltpu.SemaphoreType.DMA((CHUNKS,)),
            pltpu.SemaphoreType.DMA,
        ],
        compiler_params=pltpu.CompilerParams(vmem_limit_bytes=16 * MIB),
        cost_estimate=pl.CostEstimate(
            flops=slots * 4 * B**3, bytes_accessed=slots * 4 * B * B + rows * 16 * B * B, transcendentals=0
        ),
        name="local_and_offset",
    )(index, stay(table), coupling, stay(left), stay(right), diag, seed, *order)


def first_totals_kernel(own, *refs):
    arrivals = (refs[:2], refs[2:4])
    outs = refs[-SIDE:]
    h = own.shape[0] // (2 * SIDE)
    for half in range(2):
        for b in range(SIDE):
            t = own[pl.ds((half * SIDE + b) * h, h)].astype(f32)
            for a in arrivals[half]:
                t = t + a[pl.ds(b * h, h)].astype(f32)
            outs[b][pl.ds(half * h, h)] = t.astype(bf16)


def first_totals(own, arrivals, order):
    rows = own.shape[0] // SIDE
    return pl.pallas_call(
        first_totals_kernel,
        out_shape=[jax.ShapeDtypeStruct((rows, B, B), bf16)] * SIDE,
        in_specs=[VMEM] * 5 + [ANY] * len(order),
        out_specs=[VMEM] * SIDE,
        compiler_params=pltpu.CompilerParams(vmem_limit_bytes=9 * MIB),
        cost_estimate=pl.CostEstimate(flops=0, bytes_accessed=256 * 2 * B * B, transcendentals=0),
        name="first_totals",
    )(own, *arrivals, *order)


def coupling_kernel(base_ref, diag_ref, *refs):
    parts = refs[:SIDE]
    new_ref, keep_ref, give_ref, new, held, sem = refs[4:]
    rows = base_ref.shape[0]
    half = rows // 2
    group = half // 2
    core = lax.axis_index("section") % 2
    copies = []
    for g in range(rows // group):

        def finish(i, _, g=g):
            r = g * group + i
            t = base_ref[r]
            for p in parts:
                t = t - p[r].astype(f32)
            new[r] = t
            th, tl = split(t)
            dh, dl = split(diag_ref[r])
            held[(r + core * half) % rows] = -(mm(dh, th) + (mm(dh, tl) + mm(dl, th))).astype(bf16)
            return 0

        lax.fori_loop(0, group, finish, 0, unroll=True)
        part = pl.ds(g * group, group)
        copies.append(pltpu.make_async_copy(new.at[part], new_ref.at[part], sem.at[g]))
        copies[-1].start()
    for i in range(half):
        keep_ref[i] = held[i]
        give_ref[i] = held[half + i]
    for c in copies:
        c.wait()


def coupling_and_step(base, diag, parts):
    rows = base.shape[0]
    half = rows // 2
    return pl.pallas_call(
        coupling_kernel,
        out_shape=[jax.ShapeDtypeStruct((rows, B, B), f32)] + cell_shapes([half, half]),
        in_specs=[VMEM] * (2 + SIDE),
        out_specs=[HBM, VMEM, VMEM],
        scratch_shapes=[
            pltpu.VMEM((rows, B, B), f32),
            pltpu.VMEM((rows, B, B), bf16),
            pltpu.SemaphoreType.DMA((4,)),
        ],
        compiler_params=pltpu.CompilerParams(vmem_limit_bytes=9 * MIB),
        cost_estimate=pl.CostEstimate(flops=rows * 6 * B**3, bytes_accessed=rows * 22 * B * B, transcendentals=0),
        name="coupling_and_step",
    )(base, diag, *parts)


def compose_kernel(chips, keep_ref, offset_ref, got_ref, got_offset_ref, *outs):
    section = lax.axis_index("section")
    chip = section // 2
    half = keep_ref.shape[0]
    per = half // chips

    def compose(first):
        for k in range(chips):
            for j in range(per):
                i = (chip + k) % chips * per + j
                mine = (keep_ref[i], offset_ref[i])
                other = (got_ref[i], got_offset_ref[i])
                (ma, oa), (mb, ob) = (mine, other) if first else (other, mine)
                outs[k][j] = mm(ma, mb).astype(bf16)
                outs[k][per + j] = (oa.astype(f32) + mm_nt(ob, ma)).astype(bf16)

    @pl.when(section % 2 == 0)
    def _():
        compose(True)

    @pl.when(section % 2 == 1)
    def _():
        compose(False)


def compose(chips, keep, offsets, got, got_offsets):
    half = keep.shape[0]
    return pl.pallas_call(
        functools.partial(compose_kernel, chips),
        out_shape=[jax.ShapeDtypeStruct((2 * half // chips, B, B), bf16)] * chips,
        in_specs=[VMEM] * 4,
        out_specs=[VMEM] * chips,
        compiler_params=pltpu.CompilerParams(vmem_limit_bytes=4 * MIB),
        cost_estimate=pl.CostEstimate(flops=half * 4 * B**3, bytes_accessed=half * 12 * B * B, transcendentals=0),
        name="compose",
    )(keep, offsets, got, got_offsets)


def chain_kernel(chips, *refs):
    parts = refs[:chips]
    outs = refs[chips : 2 * chips]
    maps, incoming = refs[2 * chips :]
    chip = lax.axis_index("section") // 2
    per = outs[0].shape[0]
    for part, k in zip(parts, ORDER):
        for i in range(2 * per):
            maps[(chip - k + chips) % chips, i] = part[i]
    current = [jnp.zeros((B, B), f32)] * per
    for c in range(chips - 1, -1, -1):
        for j in range(per):
            incoming[c, j] = current[j].astype(bf16)
            if c > 0:
                new = maps[c, per + j].astype(f32)
                if c < chips - 1:
                    high, low = split(current[j])
                    new = new + (mm_nt(high, maps[c, j]) + mm_nt(low, maps[c, j]))
                current[j] = new
    for k in range(chips):
        for j in range(per):
            outs[k][j] = incoming[(chip + k) % chips, j]


def run_chains(parts):
    chips = len(parts)
    per = parts[0].shape[0] // 2
    return pl.pallas_call(
        functools.partial(chain_kernel, chips),
        out_shape=[jax.ShapeDtypeStruct((per, B, B), bf16)] * chips,
        in_specs=[VMEM] * chips,
        out_specs=[VMEM] * chips,
        scratch_shapes=[pltpu.VMEM((chips, 2 * per, B, B), bf16), pltpu.VMEM((chips, per, B, B), bf16)],
        compiler_params=pltpu.CompilerParams(vmem_limit_bytes=4 * MIB),
        cost_estimate=pl.CostEstimate(
            flops=chips * per * 4 * B**3, bytes_accessed=chips * per * 6 * B * B, transcendentals=0
        ),
        name="run_chains",
    )(*parts)


def expand_kernel(chips, keep_ref, offset_ref, got_ref, got_offset_ref, *refs):
    parts = refs[:chips]
    mine_ref, other_ref = refs[chips:]
    section = lax.axis_index("section")
    chip = section // 2
    half = keep_ref.shape[0]
    per = half // chips

    def expand(first):
        for part, k in zip(parts, ORDER):
            for j in range(per):
                i = (chip - k + chips) % chips * per + j
                mine = (keep_ref[i], offset_ref[i])
                other = (got_ref[i], got_offset_ref[i])
                (ma, oa), (mb, ob) = (mine, other) if first else (other, mine)
                b = ob.astype(f32) + mm_nt(part[j], mb)
                a = oa.astype(f32) + mm_nt(b.astype(bf16), ma)
                mine_ref[i] = a if first else b
                other_ref[i] = (b if first else a).astype(bf16)

    @pl.when(section % 2 == 0)
    def _():
        expand(True)

    @pl.when(section % 2 == 1)
    def _():
        expand(False)


def expand(keep, offsets, got, got_offsets, parts):
    chips = len(parts)
    half = keep.shape[0]
    return pl.pallas_call(
        functools.partial(expand_kernel, chips),
        out_shape=[jax.ShapeDtypeStruct((half, B, B), f32), jax.ShapeDtypeStruct((half, B, B), bf16)],
        in_specs=[VMEM] * (4 + chips),
        out_specs=[VMEM] * 2,
        compiler_params=pltpu.CompilerParams(vmem_limit_bytes=4 * MIB),
        cost_estimate=pl.CostEstimate(flops=half * 6 * B**3, bytes_accessed=half * 16 * B * B, transcendentals=0),
        name="expand",
    )(keep, offsets, got, got_offsets, *parts)


def store_kernel(mine_ref, out_ref, sem):
    half = mine_ref.shape[0]
    core = lax.axis_index("section") % 2
    copy = pltpu.make_async_copy(mine_ref, out_ref.at[pl.ds(core * half, half)], sem)
    copy.start()
    copy.wait()


def store_rows(mine):
    half = mine.shape[0]
    return pl.pallas_call(
        store_kernel,
        out_shape=jax.ShapeDtypeStruct((2 * half, B, B), f32),
        in_specs=[VMEM],
        out_specs=HBM,
        scratch_shapes=[pltpu.SemaphoreType.DMA],
        compiler_params=pltpu.CompilerParams(vmem_limit_bytes=2 * MIB),
        cost_estimate=pl.CostEstimate(flops=0, bytes_accessed=half * 8 * B * B, transcendentals=0),
        name="store_rows",
    )(mine)


def add_kernel(got_ref, part_ref, out_ref, held, sem):
    half = got_ref.shape[0]
    group = half // 2
    core = lax.axis_index("section") % 2
    copies = []
    for g in range(2):
        for i in range(g * group, (g + 1) * group):
            held[i] = got_ref[i].astype(f32)
        to = out_ref.at[pl.ds((1 - core) * half + g * group, group)]
        copies.append(pltpu.make_async_copy(held.at[pl.ds(g * group, group)], to, sem.at[g]))
        copies[-1].start()
    for c in copies:
        c.wait()


def add_rows(got, part):
    half = got.shape[0]
    return pl.pallas_call(
        add_kernel,
        out_shape=jax.ShapeDtypeStruct(part.shape, f32),
        in_specs=[VMEM, HBM],
        out_specs=HBM,
        scratch_shapes=[pltpu.VMEM((half, B, B), f32), pltpu.SemaphoreType.DMA((2,))],
        input_output_aliases={1: 0},
        compiler_params=pltpu.CompilerParams(vmem_limit_bytes=4 * MIB),
        cost_estimate=pl.CostEstimate(flops=0, bytes_accessed=half * 6 * B * B, transcendentals=0),
        name="add_rows",
    )(got, part)


def moved(x, stage, by, sections):
    pairs = []
    for s in range(sections):
        for a in range(SIDE):
            for c in range(SIDE):
                if (s + stage) % 2 == 0:
                    to = (a + by) % SIDE * SIDE + c
                else:
                    to = a * SIDE + (c + by) % SIDE
                pairs.append((s * SIDE * SIDE + a * SIDE + c, s * SIDE * SIDE + to))
    return lax.ppermute(x, ("section", "row"), pairs)


def across(x, sections, by):
    return lax.ppermute(x, "section", [(i, (i + 2 * by) % sections) for i in range(sections)])


def partner(x, sections):
    return lax.ppermute(x, "section", [(i, i ^ 1) for i in range(sections)])


def add(a, b):
    return (a.astype(f32) + b.astype(f32)).astype(bf16)


def per_device(
    coupling,
    diag_inverse,
    pivot_inverse,
    cross_left,
    cross_right,
    cross_pivot,
    cross_owner,
    foreign_target_row,
    cross_count,
    local_left,
    local_right,
    local_pivot,
    local_target,
    adjoint_seed,
):
    sections = lax.axis_size("section")
    rows = coupling.shape[0]
    half = rows // 2
    n = SIDE * half
    group = 2 * n
    local_word = local_target | (local_pivot << PIVOT_BIT)

    far, on_chip, word = far_sums(
        [n] * 2,
        half,
        cross_owner[:, 0],
        foreign_target_row,
        cross_pivot,
        cross_count,
        pivot_inverse,
        cross_left,
        cross_right,
    )
    far_in = [moved(x, 0, w, sections) for x, w in zip(far, (1, -1))]
    near = near_sums(group, [n] * 4 + [2 * n], word, on_chip)
    alone_in = [moved(x, 0, w, sections) for x, w in zip(near[:2], (1, -1))]
    joined = [add(x, y) for x, y in zip(near[2:4], far_in)]
    joined_in = [moved(x, 0, w, sections) for x, w in zip(joined, (1, -1))]

    base, offsets, give_offsets = local_and_offset(
        local_word, pivot_inverse, coupling, local_left, local_right, diag_inverse, adjoint_seed, joined
    )
    got_offsets = partner(give_offsets, sections)

    arrivals = (joined_in[0], alone_in[1], alone_in[0], joined_in[1])
    totals = first_totals(near[4], arrivals, [base, got_offsets])
    parts = [totals[0]] + [moved(totals[k], 1, k, sections) for k in (2, 1, 3)]
    updated, keep, give = coupling_and_step(base, diag_inverse, parts)
    chips = sections // 2
    got = partner(give, sections)
    maps = compose(chips, keep, offsets, got, got_offsets)
    maps = [across(maps[k], sections, k) if k else maps[0] for k in ORDER]
    incoming = run_chains(maps)
    incoming = [across(incoming[k], sections, k) if k else incoming[0] for k in ORDER]
    mine, other = expand(keep, offsets, got, got_offsets, incoming)
    adjoint = add_rows(partner(other, sections), store_rows(mine))
    return (updated, adjoint)


def solution(mesh):
    spread = ("section", "row")
    block = P(spread, None, None)
    line = P(spread)
    return jax.shard_map(
        per_device,
        mesh=mesh,
        in_specs=(
            block,
            block,
            block,
            block,
            block,
            line,
            P(spread, None),
            line,
            line,
            block,
            block,
            line,
            line,
            block,
        ),
        out_specs=(block, block),
        check_vma=False,
    )
```

```python
import functools

import jax
import jax.numpy as jnp
from jax import lax
from jax.experimental import pallas as pl
from jax.experimental.pallas import tpu as pltpu
from jax.sharding import PartitionSpec as P

B = 128
SIDE = 4
UNROLL = 16
CHUNKS = 8
SIDE_BIT = 2
PLACES = sum(p << (3 * i) for i, p in enumerate((6, 7, 4, 2, 0, 1, 3, 5)))
CELL_MASK, PIVOT_BIT, FAR_BIT, NEAR_BIT, SLOT_BIT = 511, 9, 16, 17, 20
ORDER = (0, 2, 1, 3)
MIB = 1 << 20

ANY = pl.BlockSpec(memory_space=pl.ANY)
HBM = pl.BlockSpec(memory_space=pltpu.HBM)
VMEM = pl.BlockSpec(memory_space=pltpu.VMEM)
SMEM = pl.BlockSpec(memory_space=pltpu.SMEM)

bf16 = jnp.bfloat16
f32 = jnp.float32


def mm(a, b):
    return jnp.dot(a, b, preferred_element_type=f32)


def mm_nt(a, b):
    return lax.dot_general(a, b, (((1,), (1,)), ((), ())), preferred_element_type=f32)


def split(x):
    high = x.astype(bf16)
    return high, (x - high.astype(f32)).astype(bf16)


def stay(x):
    return pltpu.with_memory_space_constraint(x, pltpu.HBM)


def bulk(left_ref, right_ref, left, right, lsem, rsem):
    per = left.shape[0] // CHUNKS
    pairs = []
    for k in range(CHUNKS):
        part = pl.ds(k * per, per)
        pair = (
            pltpu.make_async_copy(left_ref.at[part], left.at[part], lsem.at[k]),
            pltpu.make_async_copy(right_ref.at[part], right.at[part], rsem.at[k]),
        )
        for c in pair:
            c.start()
        pairs.append(pair)
    return pairs


def sum_cells(first, flag, index_ref, listed, total, outs, left, right, table, landed=None):
    slots = left.shape[0]
    cells = total.shape[0] - 1

    def note(i, n):
        word = index_ref[i]
        listed[n] = word
        return n + ((word >> flag) & 1)

    count = lax.fori_loop(0, slots, note, 0, unroll=32)
    for u in range(UNROLL):
        listed[count + u] = first + cells

    def clear(c, _):
        total[c] = jnp.zeros((B, B), bf16)
        return 0

    lax.fori_loop(0, cells + 1, clear, 0, unroll=8)
    rounds = (count + UNROLL - 1) // UNROLL

    def words_of(r):
        return [listed[r * UNROLL + u] for u in range(UNROLL)]

    def scale(w):
        return mm(left[w >> SLOT_BIT], table[(w >> PIVOT_BIT) & 3]).astype(bf16)

    def sum_up(words, scaled):
        updates = [mm(x, right[w >> SLOT_BIT]) for x, w in zip(scaled, words)]
        for w, u in zip(words, updates):
            c = (w & CELL_MASK) - first
            total[c] = (total[c].astype(f32) + u).astype(bf16)

    if landed is None:

        def both(r, _):
            words = words_of(r)
            sum_up(words, [scale(w) for w in words])
            return 0

        lax.fori_loop(0, rounds, both, 0)
    else:
        scaled, left_landed, right_landed = landed
        left_landed()

        def early(r, _):
            for u, x in enumerate([scale(w) for w in words_of(r)]):
                scaled[r * UNROLL + u] = x
            return 0

        lax.fori_loop(0, rounds, early, 0)
        right_landed()

        def late(r, _):
            sum_up(words_of(r), [scaled[r * UNROLL + u] for u in range(UNROLL)])
            return 0

        lax.fori_loop(0, rounds, late, 0)
    start = 0
    for out in outs:

        def give(c, _, out=out, start=start):
            out[c] = total[start + c]
            return 0

        lax.fori_loop(0, out.shape[0], give, 0, unroll=8)
        start += out.shape[0]


def far_kernel(half, owner_ref, target_ref, pivot_ref, count_ref, table_ref, left_ref, right_ref, *refs):
    *outs, left, right, table, index_ref = refs[:-12]
    owner, target, pivot, count, index, listed, scaled, total, lsem, rsem, tsem, isem = refs[-12:]
    slots = left.shape[0]
    given = [
        pltpu.make_async_copy(x, y, isem.at[k])
        for k, (x, y) in enumerate(
            ((owner_ref, owner), (target_ref, target), (pivot_ref, pivot), (count_ref, count))
        )
    ]
    for c in given:
        c.start()
    table_copy = pltpu.make_async_copy(table_ref, table, tsem)
    table_copy.start()
    per = slots // CHUNKS
    chunks = [pl.ds(k * per, per) for k in range(CHUNKS)]
    lefts = [pltpu.make_async_copy(left_ref.at[c], left.at[c], lsem.at[k]) for k, c in enumerate(chunks)]
    rights = [pltpu.make_async_copy(right_ref.at[c], right.at[c], rsem.at[k]) for k, c in enumerate(chunks)]
    for c in lefts + rights:
        c.start()
    for c in given:
        c.wait()

    odd = lax.axis_index("section") % 2
    me = lax.axis_index("row")
    first_shift = jnp.where(odd == 0, SIDE_BIT, 0)
    second_shift = SIDE_BIT - first_shift
    first_me, second_me = me >> first_shift, me >> second_shift
    live = count[0]
    half_bit = half.bit_length() - 1
    per_bit = half_bit + SIDE_BIT

    def word(i, _):
        a = ((owner[i] >> first_shift) - first_me) & (SIDE - 1)
        b = ((owner[i] >> second_shift) - second_me) & (SIDE - 1)
        place = (PLACES >> (3 * (2 * a + (target[i] >> half_bit)))) & 7
        cell = (place << per_bit) | (b << half_bit) | (target[i] & (half - 1))
        flag = jnp.where(a == 2, 1 << FAR_BIT, 1 << NEAR_BIT)
        flag = jnp.where(i < live, flag, 0)
        index[i] = cell | (pivot[i] << PIVOT_BIT) | (i << SLOT_BIT) | flag
        return 0

    lax.fori_loop(0, slots, word, 0, unroll=16)
    index_copy = pltpu.make_async_copy(index, index_ref, isem.at[4])
    index_copy.start()

    def left_landed():
        table_copy.wait()
        for c in lefts:
            c.wait()

    def right_landed():
        for c in rights:
            c.wait()

    landed = (scaled, left_landed, right_landed)
    sum_cells(0, FAR_BIT, index, listed, total, outs, left, right, table, landed)
    index_copy.wait()


def near_kernel(first, index_ref, table, left, right, *refs):
    *outs, listed, total = refs
    sum_cells(first, NEAR_BIT, index_ref, listed, total, outs, left, right, table)


def cell_shapes(sizes):
    return [jax.ShapeDtypeStruct((n, B, B), bf16) for n in sizes]


def far_sums(sizes, half, owner, target, pivot, count, table, left, right):
    cells = sum(sizes)
    slots = left.shape[0]
    shapes = [jax.ShapeDtypeStruct(x.shape, x.dtype) for x in (left, right, table, pivot)]
    outs = pl.pallas_call(
        functools.partial(far_kernel, half),
        out_shape=cell_shapes(sizes) + shapes,
        in_specs=[HBM] * 3 + [ANY] + [HBM] * 3,
        out_specs=[VMEM] * (len(sizes) + 3) + [HBM],
        scratch_shapes=[
            pltpu.SMEM((slots,), jnp.int32),
            pltpu.SMEM((slots,), jnp.int32),
            pltpu.SMEM((slots,), jnp.int32),
            pltpu.SMEM((1,), jnp.int32),
            pltpu.SMEM((slots,), jnp.int32),
            pltpu.SMEM((slots + UNROLL,), jnp.int32),
            pltpu.VMEM((slots + UNROLL, B, B), bf16),
            pltpu.VMEM((cells + 1, B, B), bf16),
            pltpu.SemaphoreType.DMA((CHUNKS,)),
            pltpu.SemaphoreType.DMA((CHUNKS,)),
            pltpu.SemaphoreType.DMA,
            pltpu.SemaphoreType.DMA((5,)),
        ],
        compiler_params=pltpu.CompilerParams(vmem_limit_bytes=14 * MIB + cells * 4 * B * B),
        cost_estimate=pl.CostEstimate(
            flops=slots * B**3, bytes_accessed=slots * 8 * B * B + cells * 2 * B * B, transcendentals=0
        ),
        name="far_sums",
    )(stay(owner), stay(target), stay(pivot), count, stay(table), stay(left), stay(right))
    return outs[: len(sizes)], outs[len(sizes) : -1], outs[-1]


def near_sums(first, sizes, index, held):
    left, right, table = held
    cells = sum(sizes)
    slots = left.shape[0]
    return pl.pallas_call(
        functools.partial(near_kernel, first),
        out_shape=cell_shapes(sizes),
        in_specs=[SMEM, VMEM, VMEM, VMEM],
        out_specs=[VMEM] * len(sizes),
        scratch_shapes=[pltpu.SMEM((slots + UNROLL,), jnp.int32), pltpu.VMEM((cells + 1, B, B), bf16)],
        compiler_params=pltpu.CompilerParams(vmem_limit_bytes=9 * MIB + cells * 4 * B * B),
        cost_estimate=pl.CostEstimate(
            flops=slots * 3 * B**3, bytes_accessed=slots * 4 * B * B + cells * 2 * B * B, transcendentals=0
        ),
        name="near_sums",
    )(index, table, left, right)


def local_kernel(index_ref, table_ref, coupling_ref, left_ref, right_ref, diag_ref, seed_ref, *refs):
    base_ref, keep_ref, give_ref, held, left, right, table, lsem, rsem, tsem = refs[-10:]
    slots = left.shape[0]
    rows = coupling_ref.shape[0]
    half = rows // 2
    core = lax.axis_index("section") % 2
    table_copy = pltpu.make_async_copy(table_ref, table, tsem)
    table_copy.start()
    pairs = bulk(left_ref, right_ref, left, right, lsem, rsem)
    for r in range(rows):
        base_ref[r] = coupling_ref[r].astype(f32)

    def offset(r, _):
        dh, dl = split(diag_ref[r])
        sh, sl = split(seed_ref[r])
        o = mm_nt(sh, dh) + (mm_nt(sh, dl) + mm_nt(sl, dh))
        held[(r + core * half) % rows] = o.astype(bf16)
        return 0

    lax.fori_loop(0, rows, offset, 0, unroll=4)
    for i in range(half):
        keep_ref[i] = held[i]
        give_ref[i] = held[half + i]
    table_copy.wait()
    per = slots // CHUNKS
    for k, pair in enumerate(pairs):
        for c in pair:
            c.wait()

        def work(i, _, k=k):
            at = [k * per + i * UNROLL + u for u in range(UNROLL)]
            words = [index_ref[j] for j in at]
            scaled = [mm(left[j], table[(w >> PIVOT_BIT) & 3]).astype(bf16) for j, w in zip(at, words)]
            updates = [mm(x, right[j]).astype(bf16).astype(f32) for x, j in zip(scaled, at)]
            for w, u in zip(words, updates):
                t = w & CELL_MASK
                base_ref[t] = base_ref[t] - u
            return 0

        lax.fori_loop(0, per // UNROLL, work, 0)


def local_and_offset(index, table, coupling, left, right, diag, seed, order):
    slots = left.shape[0]
    rows = coupling.shape[0]
    return pl.pallas_call(
        local_kernel,
        out_shape=[jax.ShapeDtypeStruct((rows, B, B), f32)] + [jax.ShapeDtypeStruct((rows // 2, B, B), bf16)] * 2,
        in_specs=[SMEM, HBM, VMEM, HBM, HBM, VMEM, VMEM] + [ANY] * len(order),
        out_specs=[VMEM] * 3,
        scratch_shapes=[
            pltpu.VMEM((rows, B, B), bf16),
            pltpu.VMEM((slots, B, B), bf16),
            pltpu.VMEM((slots, B, B), bf16),
            pltpu.VMEM(table.shape, bf16),
            pltpu.SemaphoreType.DMA((CHUNKS,)),
            pltpu.SemaphoreType.DMA((CHUNKS,)),
            pltpu.SemaphoreType.DMA,
        ],
        compiler_params=pltpu.CompilerParams(vmem_limit_bytes=16 * MIB),
        cost_estimate=pl.CostEstimate(
            flops=slots * 4 * B**3, bytes_accessed=slots * 4 * B * B + rows * 16 * B * B, transcendentals=0
        ),
        name="local_and_offset",
    )(index, stay(table), coupling, stay(left), stay(right), diag, seed, *order)


def first_totals_kernel(own, *refs):
    arrivals = (refs[:2], refs[2:4])
    outs = refs[-SIDE:]
    h = own.shape[0] // (2 * SIDE)
    for half in range(2):
        for b in range(SIDE):
            t = own[pl.ds((half * SIDE + b) * h, h)].astype(f32)
            for a in arrivals[half]:
                t = t + a[pl.ds(b * h, h)].astype(f32)
            outs[b][pl.ds(half * h, h)] = t.astype(bf16)


def first_totals(own, arrivals, order):
    rows = own.shape[0] // SIDE
    return pl.pallas_call(
        first_totals_kernel,
        out_shape=[jax.ShapeDtypeStruct((rows, B, B), bf16)] * SIDE,
        in_specs=[VMEM] * 5 + [ANY] * len(order),
        out_specs=[VMEM] * SIDE,
        compiler_params=pltpu.CompilerParams(vmem_limit_bytes=9 * MIB),
        cost_estimate=pl.CostEstimate(flops=0, bytes_accessed=256 * 2 * B * B, transcendentals=0),
        name="first_totals",
    )(own, *arrivals, *order)


def coupling_kernel(base_ref, diag_ref, *refs):
    parts = refs[:SIDE]
    new_ref, keep_ref, give_ref, new, held, sem = refs[4:]
    rows = base_ref.shape[0]
    half = rows // 2
    group = half // 2
    core = lax.axis_index("section") % 2
    copies = []
    for g in range(rows // group):

        def finish(i, _, g=g):
            r = g * group + i
            t = base_ref[r]
            for p in parts:
                t = t - p[r].astype(f32)
            new[r] = t
            th, tl = split(t)
            dh, dl = split(diag_ref[r])
            held[(r + core * half) % rows] = -(mm(dh, th) + (mm(dh, tl) + mm(dl, th))).astype(bf16)
            return 0

        lax.fori_loop(0, group, finish, 0, unroll=True)
        part = pl.ds(g * group, group)
        copies.append(pltpu.make_async_copy(new.at[part], new_ref.at[part], sem.at[g]))
        copies[-1].start()
    for i in range(half):
        keep_ref[i] = held[i]
        give_ref[i] = held[half + i]
    for c in copies:
        c.wait()


def coupling_and_step(base, diag, parts):
    rows = base.shape[0]
    half = rows // 2
    return pl.pallas_call(
        coupling_kernel,
        out_shape=[jax.ShapeDtypeStruct((rows, B, B), f32)] + cell_shapes([half, half]),
        in_specs=[VMEM] * (2 + SIDE),
        out_specs=[HBM, VMEM, VMEM],
        scratch_shapes=[
            pltpu.VMEM((rows, B, B), f32),
            pltpu.VMEM((rows, B, B), bf16),
            pltpu.SemaphoreType.DMA((4,)),
        ],
        compiler_params=pltpu.CompilerParams(vmem_limit_bytes=9 * MIB),
        cost_estimate=pl.CostEstimate(flops=rows * 6 * B**3, bytes_accessed=rows * 22 * B * B, transcendentals=0),
        name="coupling_and_step",
    )(base, diag, *parts)


def compose_kernel(chips, keep_ref, offset_ref, got_ref, got_offset_ref, *outs):
    section = lax.axis_index("section")
    chip = section // 2
    half = keep_ref.shape[0]
    per = half // chips

    def compose(first):
        for k in range(chips):
            for j in range(per):
                i = (chip + k) % chips * per + j
                mine = (keep_ref[i], offset_ref[i])
                other = (got_ref[i], got_offset_ref[i])
                (ma, oa), (mb, ob) = (mine, other) if first else (other, mine)
                outs[k][j] = mm(ma, mb).astype(bf16)
                outs[k][per + j] = (oa.astype(f32) + mm_nt(ob, ma)).astype(bf16)

    @pl.when(section % 2 == 0)
    def _():
        compose(True)

    @pl.when(section % 2 == 1)
    def _():
        compose(False)


def compose(chips, keep, offsets, got, got_offsets):
    half = keep.shape[0]
    return pl.pallas_call(
        functools.partial(compose_kernel, chips),
        out_shape=[jax.ShapeDtypeStruct((2 * half // chips, B, B), bf16)] * chips,
        in_specs=[VMEM] * 4,
        out_specs=[VMEM] * chips,
        compiler_params=pltpu.CompilerParams(vmem_limit_bytes=4 * MIB),
        cost_estimate=pl.CostEstimate(flops=half * 4 * B**3, bytes_accessed=half * 12 * B * B, transcendentals=0),
        name="compose",
    )(keep, offsets, got, got_offsets)


def chain_kernel(chips, *refs):
    parts = refs[:chips]
    outs = refs[chips : 2 * chips]
    maps, incoming = refs[2 * chips :]
    chip = lax.axis_index("section") // 2
    per = outs[0].shape[0]
    for part, k in zip(parts, ORDER):
        for i in range(2 * per):
            maps[(chip - k + chips) % chips, i] = part[i]
    current = [jnp.zeros((B, B), f32)] * per
    for c in range(chips - 1, -1, -1):
        for j in range(per):
            incoming[c, j] = current[j].astype(bf16)
            if c > 0:
                new = maps[c, per + j].astype(f32)
                if c < chips - 1:
                    high, low = split(current[j])
                    new = new + (mm_nt(high, maps[c, j]) + mm_nt(low, maps[c, j]))
                current[j] = new
    for k in range(chips):
        for j in range(per):
            outs[k][j] = incoming[(chip + k) % chips, j]


def run_chains(parts):
    chips = len(parts)
    per = parts[0].shape[0] // 2
    return pl.pallas_call(
        functools.partial(chain_kernel, chips),
        out_shape=[jax.ShapeDtypeStruct((per, B, B), bf16)] * chips,
        in_specs=[VMEM] * chips,
        out_specs=[VMEM] * chips,
        scratch_shapes=[pltpu.VMEM((chips, 2 * per, B, B), bf16), pltpu.VMEM((chips, per, B, B), bf16)],
        compiler_params=pltpu.CompilerParams(vmem_limit_bytes=4 * MIB),
        cost_estimate=pl.CostEstimate(
            flops=chips * per * 4 * B**3, bytes_accessed=chips * per * 6 * B * B, transcendentals=0
        ),
        name="run_chains",
    )(*parts)


def expand_kernel(chips, keep_ref, offset_ref, got_ref, got_offset_ref, *refs):
    parts = refs[:chips]
    mine_ref, other_ref = refs[chips:]
    section = lax.axis_index("section")
    chip = section // 2
    half = keep_ref.shape[0]
    per = half // chips

    def expand(first):
        for part, k in zip(parts, ORDER):
            for j in range(per):
                i = (chip - k + chips) % chips * per + j
                mine = (keep_ref[i], offset_ref[i])
                other = (got_ref[i], got_offset_ref[i])
                (ma, oa), (mb, ob) = (mine, other) if first else (other, mine)
                b = ob.astype(f32) + mm_nt(part[j], mb)
                a = oa.astype(f32) + mm_nt(b.astype(bf16), ma)
                mine_ref[i] = a if first else b
                other_ref[i] = (b if first else a).astype(bf16)

    @pl.when(section % 2 == 0)
    def _():
        expand(True)

    @pl.when(section % 2 == 1)
    def _():
        expand(False)


def expand(keep, offsets, got, got_offsets, parts):
    chips = len(parts)
    half = keep.shape[0]
    return pl.pallas_call(
        functools.partial(expand_kernel, chips),
        out_shape=[jax.ShapeDtypeStruct((half, B, B), f32), jax.ShapeDtypeStruct((half, B, B), bf16)],
        in_specs=[VMEM] * (4 + chips),
        out_specs=[VMEM] * 2,
        compiler_params=pltpu.CompilerParams(vmem_limit_bytes=4 * MIB),
        cost_estimate=pl.CostEstimate(flops=half * 6 * B**3, bytes_accessed=half * 16 * B * B, transcendentals=0),
        name="expand",
    )(keep, offsets, got, got_offsets, *parts)


def store_kernel(mine_ref, out_ref, sem):
    half = mine_ref.shape[0]
    core = lax.axis_index("section") % 2
    copy = pltpu.make_async_copy(mine_ref, out_ref.at[pl.ds(core * half, half)], sem)
    copy.start()
    copy.wait()


def store_rows(mine):
    half = mine.shape[0]
    return pl.pallas_call(
        store_kernel,
        out_shape=jax.ShapeDtypeStruct((2 * half, B, B), f32),
        in_specs=[VMEM],
        out_specs=HBM,
        scratch_shapes=[pltpu.SemaphoreType.DMA],
        compiler_params=pltpu.CompilerParams(vmem_limit_bytes=2 * MIB),
        cost_estimate=pl.CostEstimate(flops=0, bytes_accessed=half * 8 * B * B, transcendentals=0),
        name="store_rows",
    )(mine)


def add_kernel(got_ref, part_ref, out_ref, held, sem):
    half = got_ref.shape[0]
    group = half // 2
    core = lax.axis_index("section") % 2
    copies = []
    for g in range(2):
        for i in range(g * group, (g + 1) * group):
            held[i] = got_ref[i].astype(f32)
        to = out_ref.at[pl.ds((1 - core) * half + g * group, group)]
        copies.append(pltpu.make_async_copy(held.at[pl.ds(g * group, group)], to, sem.at[g]))
        copies[-1].start()
    for c in copies:
        c.wait()


def add_rows(got, part):
    half = got.shape[0]
    return pl.pallas_call(
        add_kernel,
        out_shape=jax.ShapeDtypeStruct(part.shape, f32),
        in_specs=[VMEM, HBM],
        out_specs=HBM,
        scratch_shapes=[pltpu.VMEM((half, B, B), f32), pltpu.SemaphoreType.DMA((2,))],
        input_output_aliases={1: 0},
        compiler_params=pltpu.CompilerParams(vmem_limit_bytes=4 * MIB),
        cost_estimate=pl.CostEstimate(flops=0, bytes_accessed=half * 6 * B * B, transcendentals=0),
        name="add_rows",
    )(got, part)


def moved(x, stage, by, sections):
    pairs = []
    for s in range(sections):
        for a in range(SIDE):
            for c in range(SIDE):
                if (s + stage) % 2 == 0:
                    to = (a + by) % SIDE * SIDE + c
                else:
                    to = a * SIDE + (c + by) % SIDE
                pairs.append((s * SIDE * SIDE + a * SIDE + c, s * SIDE * SIDE + to))
    return lax.ppermute(x, ("section", "row"), pairs)


def across(x, sections, by):
    return lax.ppermute(x, "section", [(i, (i + 2 * by) % sections) for i in range(sections)])


def partner(x, sections):
    return lax.ppermute(x, "section", [(i, i ^ 1) for i in range(sections)])


def add(a, b):
    return (a.astype(f32) + b.astype(f32)).astype(bf16)


def per_device(
    coupling,
    diag_inverse,
    pivot_inverse,
    cross_left,
    cross_right,
    cross_pivot,
    cross_owner,
    foreign_target_row,
    cross_count,
    local_left,
    local_right,
    local_pivot,
    local_target,
    adjoint_seed,
):
    sections = lax.axis_size("section")
    rows = coupling.shape[0]
    half = rows // 2
    n = SIDE * half
    group = 2 * n
    local_word = local_target | (local_pivot << PIVOT_BIT)

    far, on_chip, word = far_sums(
        [n] * 2,
        half,
        cross_owner[:, 0],
        foreign_target_row,
        cross_pivot,
        cross_count,
        pivot_inverse,
        cross_left,
        cross_right,
    )
    far_in = [moved(x, 0, w, sections) for x, w in zip(far, (1, -1))]
    near = near_sums(group, [n] * 4 + [2 * n], word, on_chip)
    alone_in = [moved(x, 0, w, sections) for x, w in zip(near[:2], (1, -1))]
    joined = [add(x, y) for x, y in zip(near[2:4], far_in)]
    joined_in = [moved(x, 0, w, sections) for x, w in zip(joined, (1, -1))]

    base, offsets, give_offsets = local_and_offset(
        local_word, pivot_inverse, coupling, local_left, local_right, diag_inverse, adjoint_seed, joined
    )
    got_offsets = partner(give_offsets, sections)

    arrivals = (joined_in[0], alone_in[1], alone_in[0], joined_in[1])
    totals = first_totals(near[4], arrivals, [base, got_offsets])
    parts = [totals[0]] + [moved(totals[k], 1, k, sections) for k in (2, 1, 3)]
    updated, keep, give = coupling_and_step(base, diag_inverse, parts)
    chips = sections // 2
    got = partner(give, sections)
    maps = compose(chips, keep, offsets, got, got_offsets)
    maps = [across(maps[k], sections, k) if k else maps[0] for k in ORDER]
    incoming = run_chains(maps)
    incoming = [across(incoming[k], sections, k) if k else incoming[0] for k in ORDER]
    mine, other = expand(keep, offsets, got, got_offsets, incoming)
    adjoint = add_rows(partner(other, sections), store_rows(mine))
    return (updated, adjoint)


def solution(mesh):
    spread = ("section", "row")
    block = P(spread, None, None)
    line = P(spread)
    return jax.shard_map(
        per_device,
        mesh=mesh,
        in_specs=(
            block,
            block,
            block,
            block,
            block,
            line,
            P(spread, None),
            line,
            line,
            block,
            block,
            line,
            line,
            block,
        ),
        out_specs=(block, block),
        check_vma=False,
    )
```

```python
import functools

import jax
import jax.numpy as jnp
from jax import lax
from jax.experimental import pallas as pl
from jax.experimental.pallas import tpu as pltpu
from jax.sharding import PartitionSpec as P

B = 128
SIDE = 4
UNROLL = 16
CHUNKS = 8
SIDE_BIT = 2
PLACES = sum(p << (3 * i) for i, p in enumerate((6, 7, 4, 2, 0, 1, 3, 5)))
CELL_MASK, PIVOT_BIT, FAR_BIT, NEAR_BIT, SLOT_BIT = 511, 9, 16, 17, 20
ORDER = (0, 2, 1, 3)
MIB = 1 << 20

ANY = pl.BlockSpec(memory_space=pl.ANY)
HBM = pl.BlockSpec(memory_space=pltpu.HBM)
VMEM = pl.BlockSpec(memory_space=pltpu.VMEM)
SMEM = pl.BlockSpec(memory_space=pltpu.SMEM)

bf16 = jnp.bfloat16
f32 = jnp.float32


def mm(a, b):
    return jnp.dot(a, b, preferred_element_type=f32)


def mm_nt(a, b):
    return lax.dot_general(a, b, (((1,), (1,)), ((), ())), preferred_element_type=f32)


def split(x):
    high = x.astype(bf16)
    return high, (x - high.astype(f32)).astype(bf16)


def stay(x):
    return pltpu.with_memory_space_constraint(x, pltpu.HBM)


def bulk(left_ref, right_ref, left, right, lsem, rsem):
    per = left.shape[0] // CHUNKS
    pairs = []
    for k in range(CHUNKS):
        part = pl.ds(k * per, per)
        pair = (
            pltpu.make_async_copy(left_ref.at[part], left.at[part], lsem.at[k]),
            pltpu.make_async_copy(right_ref.at[part], right.at[part], rsem.at[k]),
        )
        for c in pair:
            c.start()
        pairs.append(pair)
    return pairs


def sum_cells(first, flag, index_ref, listed, total, outs, ready, left, right, table):
    slots = left.shape[0]
    cells = total.shape[0] - 1

    def note(i, n):
        word = index_ref[i]
        listed[n] = word
        return n + ((word >> flag) & 1)

    count = lax.fori_loop(0, slots, note, 0, unroll=32)
    for u in range(UNROLL):
        listed[count + u] = first + cells

    def clear(c, _):
        total[c] = jnp.zeros((B, B), bf16)
        return 0

    lax.fori_loop(0, cells + 1, clear, 0, unroll=8)
    ready()

    def work(r, _):
        words = [listed[r * UNROLL + u] for u in range(UNROLL)]
        scaled = [mm(left[w >> SLOT_BIT], table[(w >> PIVOT_BIT) & 3]).astype(bf16) for w in words]
        updates = [mm(x, right[w >> SLOT_BIT]) for x, w in zip(scaled, words)]
        for w, u in zip(words, updates):
            c = (w & CELL_MASK) - first
            total[c] = (total[c].astype(f32) + u).astype(bf16)
        return 0

    lax.fori_loop(0, (count + UNROLL - 1) // UNROLL, work, 0)
    start = 0
    for out in outs:

        def give(c, _, out=out, start=start):
            out[c] = total[start + c]
            return 0

        lax.fori_loop(0, out.shape[0], give, 0, unroll=8)
        start += out.shape[0]


def far_kernel(half, owner_ref, target_ref, pivot_ref, count_ref, table_ref, left_ref, right_ref, *refs):
    *outs, left, right, table, index_ref, owner, target, pivot, index, listed, total, lsem, rsem, tsem, isem = refs
    slots = left.shape[0]
    given = [
        pltpu.make_async_copy(x, y, isem.at[k])
        for k, (x, y) in enumerate(((owner_ref, owner), (target_ref, target), (pivot_ref, pivot)))
    ]
    for c in given:
        c.start()
    pairs = bulk(left_ref, right_ref, left, right, lsem, rsem)
    table_copy = pltpu.make_async_copy(table_ref, table, tsem)
    table_copy.start()
    for c in given:
        c.wait()

    odd = lax.axis_index("section") % 2
    me = lax.axis_index("row")
    first_shift = jnp.where(odd == 0, SIDE_BIT, 0)
    second_shift = SIDE_BIT - first_shift
    first_me, second_me = me >> first_shift, me >> second_shift
    live = count_ref[0]
    half_bit = half.bit_length() - 1
    per_bit = half_bit + SIDE_BIT

    def word(i, _):
        a = ((owner[i] >> first_shift) - first_me) & (SIDE - 1)
        b = ((owner[i] >> second_shift) - second_me) & (SIDE - 1)
        place = (PLACES >> (3 * (2 * a + (target[i] >> half_bit)))) & 7
        cell = (place << per_bit) | (b << half_bit) | (target[i] & (half - 1))
        flag = jnp.where(a == 2, 1 << FAR_BIT, 1 << NEAR_BIT)
        flag = jnp.where(i < live, flag, 0)
        index[i] = cell | (pivot[i] << PIVOT_BIT) | (i << SLOT_BIT) | flag
        return 0

    lax.fori_loop(0, slots, word, 0, unroll=16)
    index_copy = pltpu.make_async_copy(index, index_ref, isem.at[3])
    index_copy.start()

    def ready():
        table_copy.wait()
        for pair in pairs:
            for c in pair:
                c.wait()

    sum_cells(0, FAR_BIT, index, listed, total, outs, ready, left, right, table)
    index_copy.wait()


def near_kernel(first, index_ref, table, left, right, *refs):
    *outs, listed, total = refs
    sum_cells(first, NEAR_BIT, index_ref, listed, total, outs, lambda: None, left, right, table)


def cell_shapes(sizes):
    return [jax.ShapeDtypeStruct((n, B, B), bf16) for n in sizes]


def far_sums(sizes, half, owner, target, pivot, count, table, left, right):
    cells = sum(sizes)
    slots = left.shape[0]
    shapes = [jax.ShapeDtypeStruct(x.shape, x.dtype) for x in (left, right, table, pivot)]
    outs = pl.pallas_call(
        functools.partial(far_kernel, half),
        out_shape=cell_shapes(sizes) + shapes,
        in_specs=[HBM] * 3 + [SMEM] + [HBM] * 3,
        out_specs=[VMEM] * (len(sizes) + 3) + [HBM],
        scratch_shapes=[
            pltpu.SMEM((slots,), jnp.int32),
            pltpu.SMEM((slots,), jnp.int32),
            pltpu.SMEM((slots,), jnp.int32),
            pltpu.SMEM((slots,), jnp.int32),
            pltpu.SMEM((slots + UNROLL,), jnp.int32),
            pltpu.VMEM((cells + 1, B, B), bf16),
            pltpu.SemaphoreType.DMA((CHUNKS,)),
            pltpu.SemaphoreType.DMA((CHUNKS,)),
            pltpu.SemaphoreType.DMA,
            pltpu.SemaphoreType.DMA((4,)),
        ],
        compiler_params=pltpu.CompilerParams(vmem_limit_bytes=9 * MIB + cells * 4 * B * B),
        cost_estimate=pl.CostEstimate(
            flops=slots * B**3, bytes_accessed=slots * 8 * B * B + cells * 2 * B * B, transcendentals=0
        ),
        name="far_sums",
    )(stay(owner), stay(target), stay(pivot), count, stay(table), stay(left), stay(right))
    return outs[: len(sizes)], outs[len(sizes) : -1], outs[-1]


def near_sums(first, sizes, index, held):
    left, right, table = held
    cells = sum(sizes)
    slots = left.shape[0]
    return pl.pallas_call(
        functools.partial(near_kernel, first),
        out_shape=cell_shapes(sizes),
        in_specs=[SMEM, VMEM, VMEM, VMEM],
        out_specs=[VMEM] * len(sizes),
        scratch_shapes=[pltpu.SMEM((slots + UNROLL,), jnp.int32), pltpu.VMEM((cells + 1, B, B), bf16)],
        compiler_params=pltpu.CompilerParams(vmem_limit_bytes=9 * MIB + cells * 4 * B * B),
        cost_estimate=pl.CostEstimate(
            flops=slots * 3 * B**3, bytes_accessed=slots * 4 * B * B + cells * 2 * B * B, transcendentals=0
        ),
        name="near_sums",
    )(index, table, left, right)


def local_kernel(index_ref, table_ref, coupling_ref, left_ref, right_ref, diag_ref, seed_ref, *refs):
    base_ref, keep_ref, give_ref, held, left, right, table, lsem, rsem, tsem = refs[-10:]
    slots = left.shape[0]
    rows = coupling_ref.shape[0]
    half = rows // 2
    core = lax.axis_index("section") % 2
    table_copy = pltpu.make_async_copy(table_ref, table, tsem)
    table_copy.start()
    pairs = bulk(left_ref, right_ref, left, right, lsem, rsem)
    for r in range(rows):
        base_ref[r] = coupling_ref[r].astype(f32)

    def offset(r, _):
        dh, dl = split(diag_ref[r])
        sh, sl = split(seed_ref[r])
        o = mm_nt(sh, dh) + (mm_nt(sh, dl) + mm_nt(sl, dh))
        held[(r + core * half) % rows] = o.astype(bf16)
        return 0

    lax.fori_loop(0, rows, offset, 0, unroll=4)
    for i in range(half):
        keep_ref[i] = held[i]
        give_ref[i] = held[half + i]
    table_copy.wait()
    per = slots // CHUNKS
    for k, pair in enumerate(pairs):
        for c in pair:
            c.wait()

        def work(i, _, k=k):
            at = [k * per + i * UNROLL + u for u in range(UNROLL)]
            words = [index_ref[j] for j in at]
            scaled = [mm(left[j], table[(w >> PIVOT_BIT) & 3]).astype(bf16) for j, w in zip(at, words)]
            updates = [mm(x, right[j]).astype(bf16).astype(f32) for x, j in zip(scaled, at)]
            for w, u in zip(words, updates):
                t = w & CELL_MASK
                base_ref[t] = base_ref[t] - u
            return 0

        lax.fori_loop(0, per // UNROLL, work, 0)


def local_and_offset(index, table, coupling, left, right, diag, seed, order):
    slots = left.shape[0]
    rows = coupling.shape[0]
    return pl.pallas_call(
        local_kernel,
        out_shape=[jax.ShapeDtypeStruct((rows, B, B), f32)] + [jax.ShapeDtypeStruct((rows // 2, B, B), bf16)] * 2,
        in_specs=[SMEM, HBM, VMEM, HBM, HBM, VMEM, VMEM] + [ANY] * len(order),
        out_specs=[VMEM] * 3,
        scratch_shapes=[
            pltpu.VMEM((rows, B, B), bf16),
            pltpu.VMEM((slots, B, B), bf16),
            pltpu.VMEM((slots, B, B), bf16),
            pltpu.VMEM(table.shape, bf16),
            pltpu.SemaphoreType.DMA((CHUNKS,)),
            pltpu.SemaphoreType.DMA((CHUNKS,)),
            pltpu.SemaphoreType.DMA,
        ],
        compiler_params=pltpu.CompilerParams(vmem_limit_bytes=16 * MIB),
        cost_estimate=pl.CostEstimate(
            flops=slots * 4 * B**3, bytes_accessed=slots * 4 * B * B + rows * 16 * B * B, transcendentals=0
        ),
        name="local_and_offset",
    )(index, stay(table), coupling, stay(left), stay(right), diag, seed, *order)


def first_totals_kernel(own, *refs):
    arrivals = (refs[2:4], refs[:2])
    outs = refs[-SIDE:]
    h = own.shape[0] // (2 * SIDE)
    for half in range(2):
        for b in range(SIDE):
            t = own[pl.ds((half * SIDE + b) * h, h)].astype(f32)
            for a in arrivals[half]:
                t = t + a[pl.ds(b * h, h)].astype(f32)
            outs[b][pl.ds(half * h, h)] = t.astype(bf16)


def first_totals(own, arrivals, order):
    rows = own.shape[0] // SIDE
    return pl.pallas_call(
        first_totals_kernel,
        out_shape=[jax.ShapeDtypeStruct((rows, B, B), bf16)] * SIDE,
        in_specs=[VMEM] * 5 + [ANY] * len(order),
        out_specs=[VMEM] * SIDE,
        compiler_params=pltpu.CompilerParams(vmem_limit_bytes=9 * MIB),
        cost_estimate=pl.CostEstimate(flops=0, bytes_accessed=256 * 2 * B * B, transcendentals=0),
        name="first_totals",
    )(own, *arrivals, *order)


def coupling_kernel(base_ref, diag_ref, *refs):
    parts = refs[:SIDE]
    new_ref, keep_ref, give_ref, new, held, sem = refs[4:]
    rows = base_ref.shape[0]
    half = rows // 2
    group = half // 2
    core = lax.axis_index("section") % 2
    copies = []
    for g in range(rows // group):

        def finish(i, _, g=g):
            r = g * group + i
            t = base_ref[r]
            for p in parts:
                t = t - p[r].astype(f32)
            new[r] = t
            th, tl = split(t)
            dh, dl = split(diag_ref[r])
            held[(r + core * half) % rows] = -(mm(dh, th) + (mm(dh, tl) + mm(dl, th))).astype(bf16)
            return 0

        lax.fori_loop(0, group, finish, 0, unroll=True)
        part = pl.ds(g * group, group)
        copies.append(pltpu.make_async_copy(new.at[part], new_ref.at[part], sem.at[g]))
        copies[-1].start()
    for i in range(half):
        keep_ref[i] = held[i]
        give_ref[i] = held[half + i]
    for c in copies:
        c.wait()


def coupling_and_step(base, diag, parts):
    rows = base.shape[0]
    half = rows // 2
    return pl.pallas_call(
        coupling_kernel,
        out_shape=[jax.ShapeDtypeStruct((rows, B, B), f32)] + cell_shapes([half, half]),
        in_specs=[VMEM] * (2 + SIDE),
        out_specs=[HBM, VMEM, VMEM],
        scratch_shapes=[
            pltpu.VMEM((rows, B, B), f32),
            pltpu.VMEM((rows, B, B), bf16),
            pltpu.SemaphoreType.DMA((4,)),
        ],
        compiler_params=pltpu.CompilerParams(vmem_limit_bytes=9 * MIB),
        cost_estimate=pl.CostEstimate(flops=rows * 6 * B**3, bytes_accessed=rows * 22 * B * B, transcendentals=0),
        name="coupling_and_step",
    )(base, diag, *parts)


def compose_kernel(chips, keep_ref, offset_ref, got_ref, got_offset_ref, *outs):
    section = lax.axis_index("section")
    chip = section // 2
    half = keep_ref.shape[0]
    per = half // chips

    def compose(first):
        for k in range(chips):
            for j in range(per):
                i = (chip + k) % chips * per + j
                mine = (keep_ref[i], offset_ref[i])
                other = (got_ref[i], got_offset_ref[i])
                (ma, oa), (mb, ob) = (mine, other) if first else (other, mine)
                outs[k][j] = mm(ma, mb).astype(bf16)
                outs[k][per + j] = (oa.astype(f32) + mm_nt(ob, ma)).astype(bf16)

    @pl.when(section % 2 == 0)
    def _():
        compose(True)

    @pl.when(section % 2 == 1)
    def _():
        compose(False)


def compose(chips, keep, offsets, got, got_offsets):
    half = keep.shape[0]
    return pl.pallas_call(
        functools.partial(compose_kernel, chips),
        out_shape=[jax.ShapeDtypeStruct((2 * half // chips, B, B), bf16)] * chips,
        in_specs=[VMEM] * 4,
        out_specs=[VMEM] * chips,
        compiler_params=pltpu.CompilerParams(vmem_limit_bytes=4 * MIB),
        cost_estimate=pl.CostEstimate(flops=half * 4 * B**3, bytes_accessed=half * 12 * B * B, transcendentals=0),
        name="compose",
    )(keep, offsets, got, got_offsets)


def chain_kernel(chips, *refs):
    parts = refs[:chips]
    outs = refs[chips : 2 * chips]
    maps, incoming = refs[2 * chips :]
    chip = lax.axis_index("section") // 2
    per = outs[0].shape[0]
    for part, k in zip(parts, ORDER):
        for i in range(2 * per):
            maps[(chip - k + chips) % chips, i] = part[i]
    current = [jnp.zeros((B, B), f32)] * per
    for c in range(chips - 1, -1, -1):
        for j in range(per):
            incoming[c, j] = current[j].astype(bf16)
            if c > 0:
                new = maps[c, per + j].astype(f32)
                if c < chips - 1:
                    high, low = split(current[j])
                    new = new + (mm_nt(high, maps[c, j]) + mm_nt(low, maps[c, j]))
                current[j] = new
    for k in range(chips):
        for j in range(per):
            outs[k][j] = incoming[(chip + k) % chips, j]


def run_chains(parts):
    chips = len(parts)
    per = parts[0].shape[0] // 2
    return pl.pallas_call(
        functools.partial(chain_kernel, chips),
        out_shape=[jax.ShapeDtypeStruct((per, B, B), bf16)] * chips,
        in_specs=[VMEM] * chips,
        out_specs=[VMEM] * chips,
        scratch_shapes=[pltpu.VMEM((chips, 2 * per, B, B), bf16), pltpu.VMEM((chips, per, B, B), bf16)],
        compiler_params=pltpu.CompilerParams(vmem_limit_bytes=4 * MIB),
        cost_estimate=pl.CostEstimate(
            flops=chips * per * 4 * B**3, bytes_accessed=chips * per * 6 * B * B, transcendentals=0
        ),
        name="run_chains",
    )(*parts)


def expand_kernel(chips, keep_ref, offset_ref, got_ref, got_offset_ref, *refs):
    parts = refs[:chips]
    mine_ref, other_ref = refs[chips:]
    section = lax.axis_index("section")
    chip = section // 2
    half = keep_ref.shape[0]
    per = half // chips

    def expand(first):
        for part, k in zip(parts, ORDER):
            for j in range(per):
                i = (chip - k + chips) % chips * per + j
                mine = (keep_ref[i], offset_ref[i])
                other = (got_ref[i], got_offset_ref[i])
                (ma, oa), (mb, ob) = (mine, other) if first else (other, mine)
                b = ob.astype(f32) + mm_nt(part[j], mb)
                a = oa.astype(f32) + mm_nt(b.astype(bf16), ma)
                mine_ref[i] = a if first else b
                other_ref[i] = (b if first else a).astype(bf16)

    @pl.when(section % 2 == 0)
    def _():
        expand(True)

    @pl.when(section % 2 == 1)
    def _():
        expand(False)


def expand(keep, offsets, got, got_offsets, parts):
    chips = len(parts)
    half = keep.shape[0]
    return pl.pallas_call(
        functools.partial(expand_kernel, chips),
        out_shape=[jax.ShapeDtypeStruct((half, B, B), f32), jax.ShapeDtypeStruct((half, B, B), bf16)],
        in_specs=[VMEM] * (4 + chips),
        out_specs=[VMEM] * 2,
        compiler_params=pltpu.CompilerParams(vmem_limit_bytes=4 * MIB),
        cost_estimate=pl.CostEstimate(flops=half * 6 * B**3, bytes_accessed=half * 16 * B * B, transcendentals=0),
        name="expand",
    )(keep, offsets, got, got_offsets, *parts)


def store_kernel(mine_ref, out_ref, sem):
    half = mine_ref.shape[0]
    core = lax.axis_index("section") % 2
    copy = pltpu.make_async_copy(mine_ref, out_ref.at[pl.ds(core * half, half)], sem)
    copy.start()
    copy.wait()


def store_rows(mine):
    half = mine.shape[0]
    return pl.pallas_call(
        store_kernel,
        out_shape=jax.ShapeDtypeStruct((2 * half, B, B), f32),
        in_specs=[VMEM],
        out_specs=HBM,
        scratch_shapes=[pltpu.SemaphoreType.DMA],
        compiler_params=pltpu.CompilerParams(vmem_limit_bytes=2 * MIB),
        cost_estimate=pl.CostEstimate(flops=0, bytes_accessed=half * 8 * B * B, transcendentals=0),
        name="store_rows",
    )(mine)


def add_kernel(got_ref, part_ref, out_ref, held, sem):
    half = got_ref.shape[0]
    group = half // 2
    core = lax.axis_index("section") % 2
    copies = []
    for g in range(2):
        for i in range(g * group, (g + 1) * group):
            held[i] = got_ref[i].astype(f32)
        to = out_ref.at[pl.ds((1 - core) * half + g * group, group)]
        copies.append(pltpu.make_async_copy(held.at[pl.ds(g * group, group)], to, sem.at[g]))
        copies[-1].start()
    for c in copies:
        c.wait()


def add_rows(got, part):
    half = got.shape[0]
    return pl.pallas_call(
        add_kernel,
        out_shape=jax.ShapeDtypeStruct(part.shape, f32),
        in_specs=[VMEM, HBM],
        out_specs=HBM,
        scratch_shapes=[pltpu.VMEM((half, B, B), f32), pltpu.SemaphoreType.DMA((2,))],
        input_output_aliases={1: 0},
        compiler_params=pltpu.CompilerParams(vmem_limit_bytes=4 * MIB),
        cost_estimate=pl.CostEstimate(flops=0, bytes_accessed=half * 6 * B * B, transcendentals=0),
        name="add_rows",
    )(got, part)


def moved(x, stage, by, sections):
    pairs = []
    for s in range(sections):
        for a in range(SIDE):
            for c in range(SIDE):
                if (s + stage) % 2 == 0:
                    to = (a + by) % SIDE * SIDE + c
                else:
                    to = a * SIDE + (c + by) % SIDE
                pairs.append((s * SIDE * SIDE + a * SIDE + c, s * SIDE * SIDE + to))
    return lax.ppermute(x, ("section", "row"), pairs)


def across(x, sections, by):
    return lax.ppermute(x, "section", [(i, (i + 2 * by) % sections) for i in range(sections)])


def partner(x, sections):
    return lax.ppermute(x, "section", [(i, i ^ 1) for i in range(sections)])


def add(a, b):
    return (a.astype(f32) + b.astype(f32)).astype(bf16)


def per_device(
    coupling,
    diag_inverse,
    pivot_inverse,
    cross_left,
    cross_right,
    cross_pivot,
    cross_owner,
    foreign_target_row,
    cross_count,
    local_left,
    local_right,
    local_pivot,
    local_target,
    adjoint_seed,
):
    sections = lax.axis_size("section")
    rows = coupling.shape[0]
    half = rows // 2
    n = SIDE * half
    group = 2 * n
    local_word = local_target | (local_pivot << PIVOT_BIT)

    far, on_chip, word = far_sums(
        [n] * 2,
        half,
        cross_owner[:, 0],
        foreign_target_row,
        cross_pivot,
        cross_count,
        pivot_inverse,
        cross_left,
        cross_right,
    )
    near = near_sums(group, [n] * 4 + [2 * n], word, on_chip)
    minus_in, plus_in = [], []
    for arrived, k, by in ((minus_in, 1, -1), (plus_in, 0, 1)):
        far_in = moved(far[k], 0, by, sections)
        arrived.append(moved(near[k], 0, by, sections))
        joined = add(near[2 + k], far_in)
        arrived += [moved(joined, 0, by, sections), joined]

    base, offsets, give_offsets = local_and_offset(
        local_word, pivot_inverse, coupling, local_left, local_right, diag_inverse, adjoint_seed, [minus_in[2], plus_in[2]]
    )
    got_offsets = partner(give_offsets, sections)

    arrivals = (minus_in[1], plus_in[0], minus_in[0], plus_in[1])
    totals = first_totals(near[4], arrivals, [base, got_offsets])
    parts = [totals[0]] + [moved(totals[k], 1, k, sections) for k in (2, 1, 3)]
    updated, keep, give = coupling_and_step(base, diag_inverse, parts)
    chips = sections // 2
    got = partner(give, sections)
    maps = compose(chips, keep, offsets, got, got_offsets)
    maps = [across(maps[k], sections, k) if k else maps[0] for k in ORDER]
    incoming = run_chains(maps)
    incoming = [across(incoming[k], sections, k) if k else incoming[0] for k in ORDER]
    mine, other = expand(keep, offsets, got, got_offsets, incoming)
    adjoint = add_rows(partner(other, sections), store_rows(mine))
    return (updated, adjoint)


def solution(mesh):
    spread = ("section", "row")
    block = P(spread, None, None)
    line = P(spread)
    return jax.shard_map(
        per_device,
        mesh=mesh,
        in_specs=(
            block,
            block,
            block,
            block,
            block,
            line,
            P(spread, None),
            line,
            line,
            block,
            block,
            line,
            line,
            block,
        ),
        out_specs=(block, block),
        check_vma=False,
    )
```

```python
import functools

import jax
import jax.numpy as jnp
from jax import lax
from jax.experimental import pallas as pl
from jax.experimental.pallas import tpu as pltpu
from jax.sharding import PartitionSpec as P

B = 128
SIDE = 4
UNROLL = 16
CHUNKS = 8
SIDE_BIT = 2
PLACES = sum(p << (3 * i) for i, p in enumerate((6, 7, 4, 2, 0, 1, 3, 5)))
CELL_MASK, PIVOT_BIT, FAR_BIT, NEAR_BIT, SLOT_BIT = 511, 9, 16, 17, 20
ORDER = (0, 2, 1, 3)
MIB = 1 << 20

ANY = pl.BlockSpec(memory_space=pl.ANY)
HBM = pl.BlockSpec(memory_space=pltpu.HBM)
VMEM = pl.BlockSpec(memory_space=pltpu.VMEM)
SMEM = pl.BlockSpec(memory_space=pltpu.SMEM)

bf16 = jnp.bfloat16
f32 = jnp.float32


def mm(a, b):
    return jnp.dot(a, b, preferred_element_type=f32)


def mm_nt(a, b):
    return lax.dot_general(a, b, (((1,), (1,)), ((), ())), preferred_element_type=f32)


def split(x):
    high = x.astype(bf16)
    return high, (x - high.astype(f32)).astype(bf16)


def stay(x):
    return pltpu.with_memory_space_constraint(x, pltpu.HBM)


def bulk(left_ref, right_ref, left, right, lsem, rsem):
    per = left.shape[0] // CHUNKS
    pairs = []
    for k in range(CHUNKS):
        part = pl.ds(k * per, per)
        pair = (
            pltpu.make_async_copy(left_ref.at[part], left.at[part], lsem.at[k]),
            pltpu.make_async_copy(right_ref.at[part], right.at[part], rsem.at[k]),
        )
        for c in pair:
            c.start()
        pairs.append(pair)
    return pairs


def sum_cells(first, flag, index_ref, listed, total, outs, ready, left, right, table):
    slots = left.shape[0]
    cells = total.shape[0] - 1

    def note(i, n):
        word = index_ref[i]
        listed[n] = word
        return n + ((word >> flag) & 1)

    count = lax.fori_loop(0, slots, note, 0, unroll=32)
    for u in range(UNROLL):
        listed[count + u] = first + cells

    def clear(c, _):
        total[c] = jnp.zeros((B, B), bf16)
        return 0

    lax.fori_loop(0, cells + 1, clear, 0, unroll=8)
    ready()

    def work(r, _):
        words = [listed[r * UNROLL + u] for u in range(UNROLL)]
        scaled = [mm(left[w >> SLOT_BIT], table[(w >> PIVOT_BIT) & 3]).astype(bf16) for w in words]
        updates = [mm(x, right[w >> SLOT_BIT]) for x, w in zip(scaled, words)]
        for w, u in zip(words, updates):
            c = (w & CELL_MASK) - first
            total[c] = (total[c].astype(f32) + u).astype(bf16)
        return 0

    lax.fori_loop(0, (count + UNROLL - 1) // UNROLL, work, 0)
    start = 0
    for out in outs:

        def give(c, _, out=out, start=start):
            out[c] = total[start + c]
            return 0

        lax.fori_loop(0, out.shape[0], give, 0, unroll=8)
        start += out.shape[0]


def far_kernel(half, owner_ref, target_ref, pivot_ref, count_ref, table_ref, left_ref, right_ref, *refs):
    *outs, left, right, table, index_ref, owner, target, pivot, index, listed, total, lsem, rsem, tsem, isem = refs
    slots = left.shape[0]
    given = [
        pltpu.make_async_copy(x, y, isem.at[k])
        for k, (x, y) in enumerate(((owner_ref, owner), (target_ref, target), (pivot_ref, pivot)))
    ]
    for c in given:
        c.start()
    pairs = bulk(left_ref, right_ref, left, right, lsem, rsem)
    table_copy = pltpu.make_async_copy(table_ref, table, tsem)
    table_copy.start()
    for c in given:
        c.wait()

    odd = lax.axis_index("section") % 2
    me = lax.axis_index("row")
    first_shift = jnp.where(odd == 0, SIDE_BIT, 0)
    second_shift = SIDE_BIT - first_shift
    first_me, second_me = me >> first_shift, me >> second_shift
    live = count_ref[0]
    half_bit = half.bit_length() - 1
    per_bit = half_bit + SIDE_BIT

    def word(i, _):
        a = ((owner[i] >> first_shift) - first_me) & (SIDE - 1)
        b = ((owner[i] >> second_shift) - second_me) & (SIDE - 1)
        place = (PLACES >> (3 * (2 * a + (target[i] >> half_bit)))) & 7
        cell = (place << per_bit) | (b << half_bit) | (target[i] & (half - 1))
        flag = jnp.where(a == 2, 1 << FAR_BIT, 1 << NEAR_BIT)
        flag = jnp.where(i < live, flag, 0)
        index[i] = cell | (pivot[i] << PIVOT_BIT) | (i << SLOT_BIT) | flag
        return 0

    lax.fori_loop(0, slots, word, 0, unroll=16)
    index_copy = pltpu.make_async_copy(index, index_ref, isem.at[3])
    index_copy.start()

    def ready():
        table_copy.wait()
        for pair in pairs:
            for c in pair:
                c.wait()

    sum_cells(0, FAR_BIT, index, listed, total, outs, ready, left, right, table)
    index_copy.wait()


def near_kernel(first, index_ref, table, left, right, *refs):
    *outs, listed, total = refs
    sum_cells(first, NEAR_BIT, index_ref, listed, total, outs, lambda: None, left, right, table)


def cell_shapes(sizes):
    return [jax.ShapeDtypeStruct((n, B, B), bf16) for n in sizes]


def far_sums(sizes, half, owner, target, pivot, count, table, left, right):
    cells = sum(sizes)
    slots = left.shape[0]
    shapes = [jax.ShapeDtypeStruct(x.shape, x.dtype) for x in (left, right, table, pivot)]
    outs = pl.pallas_call(
        functools.partial(far_kernel, half),
        out_shape=cell_shapes(sizes) + shapes,
        in_specs=[HBM] * 3 + [SMEM] + [HBM] * 3,
        out_specs=[VMEM] * (len(sizes) + 3) + [HBM],
        scratch_shapes=[
            pltpu.SMEM((slots,), jnp.int32),
            pltpu.SMEM((slots,), jnp.int32),
            pltpu.SMEM((slots,), jnp.int32),
            pltpu.SMEM((slots,), jnp.int32),
            pltpu.SMEM((slots + UNROLL,), jnp.int32),
            pltpu.VMEM((cells + 1, B, B), bf16),
            pltpu.SemaphoreType.DMA((CHUNKS,)),
            pltpu.SemaphoreType.DMA((CHUNKS,)),
            pltpu.SemaphoreType.DMA,
            pltpu.SemaphoreType.DMA((4,)),
        ],
        compiler_params=pltpu.CompilerParams(vmem_limit_bytes=9 * MIB + cells * 4 * B * B),
        cost_estimate=pl.CostEstimate(
            flops=slots * B**3, bytes_accessed=slots * 8 * B * B + cells * 2 * B * B, transcendentals=0
        ),
        name="far_sums",
    )(stay(owner), stay(target), stay(pivot), count, stay(table), stay(left), stay(right))
    return outs[: len(sizes)], outs[len(sizes) : -1], outs[-1]


def near_sums(first, sizes, index, held):
    left, right, table = held
    cells = sum(sizes)
    slots = left.shape[0]
    return pl.pallas_call(
        functools.partial(near_kernel, first),
        out_shape=cell_shapes(sizes),
        in_specs=[SMEM, VMEM, VMEM, VMEM],
        out_specs=[VMEM] * len(sizes),
        scratch_shapes=[pltpu.SMEM((slots + UNROLL,), jnp.int32), pltpu.VMEM((cells + 1, B, B), bf16)],
        compiler_params=pltpu.CompilerParams(vmem_limit_bytes=9 * MIB + cells * 4 * B * B),
        cost_estimate=pl.CostEstimate(
            flops=slots * 3 * B**3, bytes_accessed=slots * 4 * B * B + cells * 2 * B * B, transcendentals=0
        ),
        name="near_sums",
    )(index, table, left, right)


def local_kernel(index_ref, table_ref, coupling_ref, left_ref, right_ref, diag_ref, seed_ref, *refs):
    base_ref, keep_ref, give_ref, held, left, right, table, lsem, rsem, tsem = refs[-10:]
    slots = left.shape[0]
    rows = coupling_ref.shape[0]
    half = rows // 2
    core = lax.axis_index("section") % 2
    table_copy = pltpu.make_async_copy(table_ref, table, tsem)
    table_copy.start()
    pairs = bulk(left_ref, right_ref, left, right, lsem, rsem)
    for r in range(rows):
        base_ref[r] = coupling_ref[r].astype(f32)

    def offset(r, _):
        dh, dl = split(diag_ref[r])
        sh, sl = split(seed_ref[r])
        o = mm_nt(sh, dh) + (mm_nt(sh, dl) + mm_nt(sl, dh))
        held[(r + core * half) % rows] = o.astype(bf16)
        return 0

    lax.fori_loop(0, rows, offset, 0, unroll=4)
    for i in range(half):
        keep_ref[i] = held[i]
        give_ref[i] = held[half + i]
    table_copy.wait()
    per = slots // CHUNKS
    for k, pair in enumerate(pairs):
        for c in pair:
            c.wait()

        def work(i, _, k=k):
            at = [k * per + i * UNROLL + u for u in range(UNROLL)]
            words = [index_ref[j] for j in at]
            scaled = [mm(left[j], table[(w >> PIVOT_BIT) & 3]).astype(bf16) for j, w in zip(at, words)]
            updates = [mm(x, right[j]).astype(bf16).astype(f32) for x, j in zip(scaled, at)]
            for w, u in zip(words, updates):
                t = w & CELL_MASK
                base_ref[t] = base_ref[t] - u
            return 0

        lax.fori_loop(0, per // UNROLL, work, 0)


def local_and_offset(index, table, coupling, left, right, diag, seed, order):
    slots = left.shape[0]
    rows = coupling.shape[0]
    return pl.pallas_call(
        local_kernel,
        out_shape=[jax.ShapeDtypeStruct((rows, B, B), f32)] + [jax.ShapeDtypeStruct((rows // 2, B, B), bf16)] * 2,
        in_specs=[SMEM, HBM, VMEM, HBM, HBM, VMEM, VMEM] + [ANY] * len(order),
        out_specs=[VMEM] * 3,
        scratch_shapes=[
            pltpu.VMEM((rows, B, B), bf16),
            pltpu.VMEM((slots, B, B), bf16),
            pltpu.VMEM((slots, B, B), bf16),
            pltpu.VMEM(table.shape, bf16),
            pltpu.SemaphoreType.DMA((CHUNKS,)),
            pltpu.SemaphoreType.DMA((CHUNKS,)),
            pltpu.SemaphoreType.DMA,
        ],
        compiler_params=pltpu.CompilerParams(vmem_limit_bytes=16 * MIB),
        cost_estimate=pl.CostEstimate(
            flops=slots * 4 * B**3, bytes_accessed=slots * 4 * B * B + rows * 16 * B * B, transcendentals=0
        ),
        name="local_and_offset",
    )(index, stay(table), coupling, stay(left), stay(right), diag, seed, *order)


def first_totals_kernel(own, *refs):
    arrivals = (refs[2:4], refs[:2])
    outs = refs[-SIDE:]
    h = own.shape[0] // (2 * SIDE)
    for half in range(2):
        for b in range(SIDE):
            t = own[pl.ds((half * SIDE + b) * h, h)].astype(f32)
            for a in arrivals[half]:
                t = t + a[pl.ds(b * h, h)].astype(f32)
            outs[b][pl.ds(half * h, h)] = t.astype(bf16)


def first_totals(own, arrivals, order):
    rows = own.shape[0] // SIDE
    return pl.pallas_call(
        first_totals_kernel,
        out_shape=[jax.ShapeDtypeStruct((rows, B, B), bf16)] * SIDE,
        in_specs=[VMEM] * 5 + [ANY] * len(order),
        out_specs=[VMEM] * SIDE,
        compiler_params=pltpu.CompilerParams(vmem_limit_bytes=9 * MIB),
        cost_estimate=pl.CostEstimate(flops=0, bytes_accessed=256 * 2 * B * B, transcendentals=0),
        name="first_totals",
    )(own, *arrivals, *order)


def coupling_kernel(base_ref, diag_ref, *refs):
    parts = refs[:SIDE]
    new_ref, keep_ref, give_ref, new, held, sem = refs[4:]
    rows = base_ref.shape[0]
    half = rows // 2
    group = half // 2
    core = lax.axis_index("section") % 2
    copies = []
    for g in range(rows // group):

        def finish(i, _, g=g):
            r = g * group + i
            t = base_ref[r]
            for p in parts:
                t = t - p[r].astype(f32)
            new[r] = t
            th, tl = split(t)
            dh, dl = split(diag_ref[r])
            held[(r + core * half) % rows] = -(mm(dh, th) + (mm(dh, tl) + mm(dl, th))).astype(bf16)
            return 0

        lax.fori_loop(0, group, finish, 0, unroll=True)
        part = pl.ds(g * group, group)
        copies.append(pltpu.make_async_copy(new.at[part], new_ref.at[part], sem.at[g]))
        copies[-1].start()
    for i in range(half):
        keep_ref[i] = held[i]
        give_ref[i] = held[half + i]
    for c in copies:
        c.wait()


def coupling_and_step(base, diag, parts):
    rows = base.shape[0]
    half = rows // 2
    return pl.pallas_call(
        coupling_kernel,
        out_shape=[jax.ShapeDtypeStruct((rows, B, B), f32)] + cell_shapes([half, half]),
        in_specs=[VMEM] * (2 + SIDE),
        out_specs=[HBM, VMEM, VMEM],
        scratch_shapes=[
            pltpu.VMEM((rows, B, B), f32),
            pltpu.VMEM((rows, B, B), bf16),
            pltpu.SemaphoreType.DMA((4,)),
        ],
        compiler_params=pltpu.CompilerParams(vmem_limit_bytes=9 * MIB),
        cost_estimate=pl.CostEstimate(flops=rows * 6 * B**3, bytes_accessed=rows * 22 * B * B, transcendentals=0),
        name="coupling_and_step",
    )(base, diag, *parts)


def compose_kernel(chips, keep_ref, offset_ref, got_ref, got_offset_ref, *outs):
    section = lax.axis_index("section")
    chip = section // 2
    half = keep_ref.shape[0]
    per = half // chips

    def compose(first):
        for k in range(chips):
            for j in range(per):
                i = (chip + k) % chips * per + j
                mine = (keep_ref[i], offset_ref[i])
                other = (got_ref[i], got_offset_ref[i])
                (ma, oa), (mb, ob) = (mine, other) if first else (other, mine)
                outs[k][j] = mm(ma, mb).astype(bf16)
                outs[k][per + j] = (oa.astype(f32) + mm_nt(ob, ma)).astype(bf16)

    @pl.when(section % 2 == 0)
    def _():
        compose(True)

    @pl.when(section % 2 == 1)
    def _():
        compose(False)


def compose(chips, keep, offsets, got, got_offsets):
    half = keep.shape[0]
    return pl.pallas_call(
        functools.partial(compose_kernel, chips),
        out_shape=[jax.ShapeDtypeStruct((2 * half // chips, B, B), bf16)] * chips,
        in_specs=[VMEM] * 4,
        out_specs=[VMEM] * chips,
        compiler_params=pltpu.CompilerParams(vmem_limit_bytes=4 * MIB),
        cost_estimate=pl.CostEstimate(flops=half * 4 * B**3, bytes_accessed=half * 12 * B * B, transcendentals=0),
        name="compose",
    )(keep, offsets, got, got_offsets)


def chain_kernel(chips, *refs):
    parts = refs[:chips]
    outs = refs[chips : 2 * chips]
    maps, incoming = refs[2 * chips :]
    chip = lax.axis_index("section") // 2
    per = outs[0].shape[0]
    for part, k in zip(parts, ORDER):
        for i in range(2 * per):
            maps[(chip - k + chips) % chips, i] = part[i]
    current = [jnp.zeros((B, B), f32)] * per
    for c in range(chips - 1, -1, -1):
        for j in range(per):
            incoming[c, j] = current[j].astype(bf16)
            if c > 0:
                new = maps[c, per + j].astype(f32)
                if c < chips - 1:
                    high, low = split(current[j])
                    new = new + (mm_nt(high, maps[c, j]) + mm_nt(low, maps[c, j]))
                current[j] = new
    for k in range(chips):
        for j in range(per):
            outs[k][j] = incoming[(chip + k) % chips, j]


def run_chains(parts):
    chips = len(parts)
    per = parts[0].shape[0] // 2
    return pl.pallas_call(
        functools.partial(chain_kernel, chips),
        out_shape=[jax.ShapeDtypeStruct((per, B, B), bf16)] * chips,
        in_specs=[VMEM] * chips,
        out_specs=[VMEM] * chips,
        scratch_shapes=[pltpu.VMEM((chips, 2 * per, B, B), bf16), pltpu.VMEM((chips, per, B, B), bf16)],
        compiler_params=pltpu.CompilerParams(vmem_limit_bytes=4 * MIB),
        cost_estimate=pl.CostEstimate(
            flops=chips * per * 4 * B**3, bytes_accessed=chips * per * 6 * B * B, transcendentals=0
        ),
        name="run_chains",
    )(*parts)


def expand_kernel(chips, keep_ref, offset_ref, got_ref, got_offset_ref, *refs):
    parts = refs[:chips]
    mine_ref, other_ref = refs[chips:]
    section = lax.axis_index("section")
    chip = section // 2
    half = keep_ref.shape[0]
    per = half // chips

    def expand(first):
        for part, k in zip(parts, ORDER):
            for j in range(per):
                i = (chip - k + chips) % chips * per + j
                mine = (keep_ref[i], offset_ref[i])
                other = (got_ref[i], got_offset_ref[i])
                (ma, oa), (mb, ob) = (mine, other) if first else (other, mine)
                b = ob.astype(f32) + mm_nt(part[j], mb)
                a = oa.astype(f32) + mm_nt(b.astype(bf16), ma)
                mine_ref[i] = a if first else b
                other_ref[i] = (b if first else a).astype(bf16)

    @pl.when(section % 2 == 0)
    def _():
        expand(True)

    @pl.when(section % 2 == 1)
    def _():
        expand(False)


def expand(keep, offsets, got, got_offsets, parts):
    chips = len(parts)
    half = keep.shape[0]
    return pl.pallas_call(
        functools.partial(expand_kernel, chips),
        out_shape=[jax.ShapeDtypeStruct((half, B, B), f32), jax.ShapeDtypeStruct((half, B, B), bf16)],
        in_specs=[VMEM] * (4 + chips),
        out_specs=[VMEM] * 2,
        compiler_params=pltpu.CompilerParams(vmem_limit_bytes=4 * MIB),
        cost_estimate=pl.CostEstimate(flops=half * 6 * B**3, bytes_accessed=half * 16 * B * B, transcendentals=0),
        name="expand",
    )(keep, offsets, got, got_offsets, *parts)


def store_kernel(mine_ref, out_ref, sem):
    half = mine_ref.shape[0]
    core = lax.axis_index("section") % 2
    copy = pltpu.make_async_copy(mine_ref, out_ref.at[pl.ds(core * half, half)], sem)
    copy.start()
    copy.wait()


def store_rows(mine):
    half = mine.shape[0]
    return pl.pallas_call(
        store_kernel,
        out_shape=jax.ShapeDtypeStruct((2 * half, B, B), f32),
        in_specs=[VMEM],
        out_specs=HBM,
        scratch_shapes=[pltpu.SemaphoreType.DMA],
        compiler_params=pltpu.CompilerParams(vmem_limit_bytes=2 * MIB),
        cost_estimate=pl.CostEstimate(flops=0, bytes_accessed=half * 8 * B * B, transcendentals=0),
        name="store_rows",
    )(mine)


def add_kernel(got_ref, part_ref, out_ref, held, sem):
    half = got_ref.shape[0]
    group = half // 2
    core = lax.axis_index("section") % 2
    copies = []
    for g in range(2):
        for i in range(g * group, (g + 1) * group):
            held[i] = got_ref[i].astype(f32)
        to = out_ref.at[pl.ds((1 - core) * half + g * group, group)]
        copies.append(pltpu.make_async_copy(held.at[pl.ds(g * group, group)], to, sem.at[g]))
        copies[-1].start()
    for c in copies:
        c.wait()


def add_rows(got, part):
    half = got.shape[0]
    return pl.pallas_call(
        add_kernel,
        out_shape=jax.ShapeDtypeStruct(part.shape, f32),
        in_specs=[VMEM, HBM],
        out_specs=HBM,
        scratch_shapes=[pltpu.VMEM((half, B, B), f32), pltpu.SemaphoreType.DMA((2,))],
        input_output_aliases={1: 0},
        compiler_params=pltpu.CompilerParams(vmem_limit_bytes=4 * MIB),
        cost_estimate=pl.CostEstimate(flops=0, bytes_accessed=half * 6 * B * B, transcendentals=0),
        name="add_rows",
    )(got, part)


def moved(x, stage, by, sections):
    pairs = []
    for s in range(sections):
        for a in range(SIDE):
            for c in range(SIDE):
                if (s + stage) % 2 == 0:
                    to = (a + by) % SIDE * SIDE + c
                else:
                    to = a * SIDE + (c + by) % SIDE
                pairs.append((s * SIDE * SIDE + a * SIDE + c, s * SIDE * SIDE + to))
    return lax.ppermute(x, ("section", "row"), pairs)


def across(x, sections, by):
    return lax.ppermute(x, "section", [(i, (i + 2 * by) % sections) for i in range(sections)])


def partner(x, sections):
    return lax.ppermute(x, "section", [(i, i ^ 1) for i in range(sections)])


def add(a, b):
    return (a.astype(f32) + b.astype(f32)).astype(bf16)


def per_device(
    coupling,
    diag_inverse,
    pivot_inverse,
    cross_left,
    cross_right,
    cross_pivot,
    cross_owner,
    foreign_target_row,
    cross_count,
    local_left,
    local_right,
    local_pivot,
    local_target,
    adjoint_seed,
):
    sections = lax.axis_size("section")
    rows = coupling.shape[0]
    half = rows // 2
    n = SIDE * half
    group = 2 * n
    local_word = local_target | (local_pivot << PIVOT_BIT)

    far, on_chip, word = far_sums(
        [n] * 2,
        half,
        cross_owner[:, 0],
        foreign_target_row,
        cross_pivot,
        cross_count,
        pivot_inverse,
        cross_left,
        cross_right,
    )
    near = near_sums(group, [n] * 4 + [2 * n], word, on_chip)
    minus_in, plus_in = [], []
    for arrived, k, by in ((minus_in, 1, -1), (plus_in, 0, 1)):
        far_in = moved(far[k], 0, by, sections)
        arrived.append(moved(near[k], 0, by, sections))
        joined = add(near[2 + k], far_in)
        arrived += [moved(joined, 0, by, sections), joined]

    base, offsets, give_offsets = local_and_offset(
        local_word, pivot_inverse, coupling, local_left, local_right, diag_inverse, adjoint_seed, [minus_in[2], plus_in[2]]
    )
    got_offsets = partner(give_offsets, sections)

    arrivals = (minus_in[1], plus_in[0], minus_in[0], plus_in[1])
    totals = first_totals(near[4], arrivals, [base, got_offsets])
    parts = [totals[0]] + [moved(totals[k], 1, k, sections) for k in (1, 2, 3)]
    updated, keep, give = coupling_and_step(base, diag_inverse, parts)
    chips = sections // 2
    got = partner(give, sections)
    maps = compose(chips, keep, offsets, got, got_offsets)
    maps = [across(maps[k], sections, k) if k else maps[0] for k in ORDER]
    incoming = run_chains(maps)
    incoming = [across(incoming[k], sections, k) if k else incoming[0] for k in ORDER]
    mine, other = expand(keep, offsets, got, got_offsets, incoming)
    adjoint = add_rows(partner(other, sections), store_rows(mine))
    return (updated, adjoint)


def solution(mesh):
    spread = ("section", "row")
    block = P(spread, None, None)
    line = P(spread)
    return jax.shard_map(
        per_device,
        mesh=mesh,
        in_specs=(
            block,
            block,
            block,
            block,
            block,
            line,
            P(spread, None),
            line,
            line,
            block,
            block,
            line,
            line,
            block,
        ),
        out_specs=(block, block),
        check_vma=False,
    )
```
